32 devices in a mesh: members: 2 (over y), comp: 4 (over z), lat: 2 (over x), sub: 2 (over core).
Axes of the slice: x: 2, y: 2, z: 4, core: 2. Of those that a mesh axis runs over, the one named last changes fastest.
Arguments:
- spectrum: float32 [1920, 4096], P('comp', ('members', 'lat', 'sub')), parts along dimension 1, may hold values from 0.05 to 2
- sea_mask: int32 [4096], P(('members', 'lat', 'sub')), parts along dimension 0, may hold values 0 or 1
- neighbours: int32 [4, 4096], P(None, ('members', 'lat', 'sub')), parts along dimension 1, may hold values from 0 to 2047, as said below
- substeps: int32 [30], replicated, may hold values from 1 to 6, as said below
- courant: float32 [30], replicated, may hold values from 0.2 to 0.7
- source_operator: bfloat16 [1920, 1920], P('sub'), may hold values from -0.125 to 0.125
Outputs:
- new_spectrum: float32 [1920, 4096], P('comp', ('members', 'lat', 'sub')), parts along dimension 1
The draws below stay inside these ranges and needn't reach their ends.
There are 2 independent parts, one for each index of `members`. The reference program is written for one: setup_inputs(seed, part) draws one part's arguments, and reference() takes and returns one part's arrays. A program takes and returns all parts, laid end to end along the dimension named above; an argument that names none is the same for every part. Nothing has to cross between parts.
Inputs may be any that keep to these rules, and one draw needn't show every extreme that they name: Non-increasing with the band; the first band takes 6 substeps and the last band one. Points are numbered row by row, 256 to a row. The west and east neighbours lie in the same row, one or two columns away, wrapping around the row. The south neighbour lies in the row before and the north neighbour in the row after, within one column (wrapping); on the first and last row of the member's grid that neighbour is the point itself.
All inputs are finite; a program needn't handle non-finite values. No bound on the sum of `sea_mask` on one device may be relied on, other than what follows from the above.
Results may differ from the reference program's by a relative error of at most 0.0015.
Values may be sent and summed in bfloat16 or wider, within the bound.
No kernel may reach another device: no remote copies, remote signals or barrier semaphores. Data moves between devices by JAX's collectives and lax.ppermute only.
A program may use at most 64 MiB of HBM per device.

```python
import math
import jax
import jax.numpy as jnp

NF = 30
ND = 64
NBINS = 1920
NLON = 256
MAXSTEPS = 6
SRC_STEPS = 4
P_SIZE = 2048


def draw_neighbours(key, part):
    rows_all = P_SIZE // NLON
    position = jnp.arange(P_SIZE, dtype=jnp.int32)
    row_number = position // NLON
    column = position % NLON
    key_list = jax.random.split(key, 4)
    west_step = jax.random.randint(key_list[0], (P_SIZE,), 1, 3).astype(jnp.int32)
    east_step = jax.random.randint(key_list[1], (P_SIZE,), 1, 3).astype(jnp.int32)
    south_step = jax.random.randint(key_list[2], (P_SIZE,), -1, 2).astype(jnp.int32)
    north_step = jax.random.randint(key_list[3], (P_SIZE,), -1, 2).astype(jnp.int32)
    west_index = row_number * NLON + (column - west_step) % NLON
    east_index = row_number * NLON + (column + east_step) % NLON
    south_index = jnp.where(row_number > 0, (row_number - 1) * NLON + (column + south_step) % NLON, position)
    north_index = jnp.where(row_number < rows_all - 1, (row_number + 1) * NLON + (column + north_step) % NLON, position)
    return jnp.stack([west_index, east_index, south_index, north_index]).astype(jnp.int32)


def draw_substeps(key, part):
    raw_counts = jax.random.randint(key, (NF,), 1, MAXSTEPS + 1).astype(jnp.int32)
    raw_counts = raw_counts.at[0].set(MAXSTEPS).at[NF - 1].set(1)
    return (-jnp.sort(-raw_counts)).astype(jnp.int32)


def set_ends(entries, stream_key, low, largest):
    extent = entries.shape
    place = [jax.random.randint(jax.random.fold_in(stream_key, axis), (), 0, extent[axis]) for axis in range(len(extent))]
    entries = entries.at[tuple(place)].set(low)
    longest = extent.index(max(extent))
    place[longest] = (place[longest] + 1) % extent[longest]
    return entries.at[tuple(place)].set(largest)


def shard_levels(own_key, extent, shards, low, largest):
    gain, own = 1.0, jax.random.fold_in(own_key, 6)
    for dim, shards_of in shards:
        heights = jnp.exp(jax.random.uniform(jax.random.fold_in(own, dim), (shards_of,), jnp.float32, low / len(shards), largest / len(shards)))
        gain = gain * jnp.repeat(heights, extent[dim] // shards_of).reshape([-1 if axis == dim else 1 for axis in range(len(extent))])
    return gain


def normal_values(own_key, extent, spread, reach, pieces=(), kind=jnp.bfloat16):
    drawn = jax.random.normal(own_key, extent, jnp.float32) * spread
    if len(pieces) > 0:
        drawn = shard_levels(own_key, extent, pieces, -0.22, 0.18) * drawn
    return jnp.clip(drawn, min=-reach, max=reach).astype(kind)


def setup_inputs(seed: int = 0, part: int = 0) -> dict:
    arg_keys = jax.random.split(jax.random.key(seed), 7)
    own_keys = jax.random.split(jax.random.fold_in(arg_keys[6], part), 7)
    return {
        "spectrum": jnp.clip(jnp.exp(math.log(2.0) - 3.6888794 * jax.random.uniform(own_keys[0], (NBINS, P_SIZE), jnp.float32) ** shard_levels(own_keys[0], (NBINS, P_SIZE), ((0, 4), (1, 4)), -0.2, 0.2)), 0.05, 2.0),
        "sea_mask": set_ends((jax.random.randint(own_keys[1], (P_SIZE,), 0, 5) < 4).astype(jnp.int32), jax.random.fold_in(own_keys[1], 1), 0, 1),
        "neighbours": draw_neighbours(jax.random.fold_in(jax.random.fold_in(arg_keys[6], part), 71), part),
        "substeps": draw_substeps(jax.random.fold_in(arg_keys[6], 71), part),
        "courant": jnp.clip(jax.random.uniform(arg_keys[4], (NF,), jnp.float32, 0.2, 0.7), 0.2, 0.7),
        "source_operator": normal_values(arg_keys[5], (NBINS, NBINS), NBINS ** -0.5, 0.125, ((0, 2),)),
    }


STEP_SIZE = 0.1


def reference(spectrum, sea_mask, neighbours, substeps, courant, source_operator):
    bin_index = jnp.arange(NF * ND, dtype=jnp.int32)
    frequency = bin_index // ND
    direction = bin_index % ND
    angles = (direction.astype(jnp.float32) + 0.5) * (2.0 * math.pi / ND)
    cosine = jnp.cos(angles)
    sine_dir = jnp.sin(angles)
    bin_speed = courant[frequency]
    weight_x = bin_speed * jnp.abs(cosine)
    weight_y = bin_speed * jnp.abs(sine_dir)
    bin_steps = substeps[frequency]
    sea_float = sea_mask.astype(jnp.float32)
    field_now = sea_float[None, :] * spectrum
    for substep in range(MAXSTEPS):
        west_vals = field_now[:, neighbours[0]]
        east_vals = field_now[:, neighbours[1]]
        south_vals = field_now[:, neighbours[2]]
        north_vals = field_now[:, neighbours[3]]
        upwind_lon = jnp.where((cosine > 0)[:, None], west_vals, east_vals)
        upwind_lat = jnp.where((sine_dir > 0)[:, None], south_vals, north_vals)
        advanced = sea_float[None, :] * (field_now - weight_x[:, None] * (field_now - upwind_lon)
                                         - weight_y[:, None] * (field_now - upwind_lat))
        field_now = jnp.where((substep < bin_steps)[:, None], advanced, field_now)
    propagated = field_now
    start_spec = propagated.astype(jnp.bfloat16)
    state_now = start_spec.astype(jnp.float32)
    for source_step in range(SRC_STEPS):
        driving = jnp.dot(source_operator, state_now.astype(jnp.bfloat16), preferred_element_type=jnp.float32)
        state_now = state_now + STEP_SIZE * state_now * driving
    increment = (state_now - start_spec.astype(jnp.float32)).astype(jnp.bfloat16)
    return sea_float[None, :] * (propagated + increment.astype(jnp.float32))
```

```python
import functools
import math

import jax
import jax.numpy as jnp
from jax import lax
from jax.experimental import pallas as pl
from jax.experimental.pallas import tpu as pltpu
from jax.sharding import PartitionSpec as P

NF = 30
ND = 64
NLON = 256
MAXSTEPS = 6
SRC_STEPS = 4


STEP_SIZE = 0.1

HALO_TYPE = jnp.float16


def extended(cells, sides, width):
    for axis, dim in sides:
        count = lax.axis_size(axis)
        ends = count - 1
        head = lax.slice_in_dim(cells, 0, width, axis=dim)
        tail = lax.slice_in_dim(cells, cells.shape[dim] - width, cells.shape[dim], axis=dim)
        cells = jnp.concatenate(
            [
                lax.ppermute(tail, axis, [(i, (i + 1) % count) for i in range(ends)]),
                cells,
                lax.ppermute(head, axis, [((i + 1) % count, i) for i in range(ends)]),
            ],
            axis=dim,
        )
    return cells


def bin_tables(global_bins, substeps, courant):
    frequency = global_bins // ND
    direction = global_bins % ND
    chosen = frequency[:, None] == jnp.arange(NF, dtype=jnp.int32)[None, :]
    bin_steps = jnp.sum(jnp.where(chosen, substeps[None, :], 0), axis=1)
    bin_speed = jnp.sum(jnp.where(chosen, courant[None, :], 0.0), axis=1)
    angles = (direction.astype(jnp.float32) + 0.5) * (2.0 * math.pi / ND)
    cosine = jnp.cos(angles)
    sine_dir = jnp.sin(angles)
    return (
        bin_steps,
        bin_speed * jnp.abs(cosine),
        bin_speed * jnp.abs(sine_dir),
        cosine > 0,
        sine_dir > 0,
    )


def offset_codes(neighbours, sea_float, points_local):
    position = lax.axis_index(("lat", "sub")) * points_local + jnp.arange(
        points_local, dtype=jnp.int32
    )
    column = position % NLON
    west_gap = (column - neighbours[0] % NLON) % NLON
    east_gap = (neighbours[1] % NLON - column) % NLON

    def vertical_code(index_row):
        column_move = (index_row % NLON - column + 1) % NLON - 1
        return jnp.where(index_row == position, 2, column_move)

    stacked = jnp.stack(
        [west_gap, east_gap, vertical_code(neighbours[2]), vertical_code(neighbours[3])]
    ).astype(jnp.float32)
    return jnp.concatenate([stacked, sea_float[None, :]], axis=0).reshape(
        5, points_local // NLON, NLON
    )


def column_roll(values, amount):
    return jnp.roll(values, amount, axis=-1)


def vertical_pick(other_rows, code_row, center):
    moved = jnp.where(
        code_row == -1.0,
        column_roll(other_rows, 1),
        jnp.where(code_row == 1.0, column_roll(other_rows, -1), other_rows),
    )
    return jnp.where(code_row == 2.0, center, moved)


def advance(substep, center, below, above, point_codes, tables):
    bin_steps, weight_x, weight_y, from_west, from_south = tables
    west_vals = jnp.where(
        point_codes[0][None] == 1.0, column_roll(center, 1), column_roll(center, 2)
    )
    east_vals = jnp.where(
        point_codes[1][None] == 1.0, column_roll(center, -1), column_roll(center, -2)
    )
    upwind_lon = jnp.where(from_west[:, None, None], west_vals, east_vals)
    south_vals = vertical_pick(below, point_codes[2][None], center)
    north_vals = vertical_pick(above, point_codes[3][None], center)
    upwind_lat = jnp.where(from_south[:, None, None], south_vals, north_vals)
    advanced = point_codes[4][None] * (
        center
        - weight_x[:, None, None] * (center - upwind_lon)
        - weight_y[:, None, None] * (center - upwind_lat)
    )
    return jnp.where((substep < bin_steps)[:, None, None], advanced, center)


def propagate(spec_part, global_bins, substeps, courant, point_codes):
    tables = bin_tables(global_bins, substeps, courant)
    bin_count = spec_part.shape[0]
    points_local = spec_part.shape[1]
    row_count = points_local // NLON
    field_now = spec_part.reshape(bin_count, row_count, NLON)
    for substep in range(MAXSTEPS):
        padded = extended(field_now, ((("lat", "sub"), 1),), 1)
        field_now = advance(substep, field_now, padded[:, :-2], padded[:, 2:], point_codes, tables)
    return field_now.reshape(bin_count, points_local)


def per_device(spectrum, sea_mask, neighbours, substeps, courant, source_operator):
    comp_index = lax.axis_index("comp")
    bins_local = spectrum.shape[0]
    points_local = spectrum.shape[1]
    sea_float = sea_mask.astype(jnp.float32)
    point_codes = offset_codes(neighbours, sea_float, points_local)
    field_start = sea_float[None, :] * spectrum
    first_bin = comp_index * bins_local
    held_bins = first_bin + jnp.arange(bins_local, dtype=jnp.int32)
    propagated = propagate(field_start, held_bins, substeps, courant, point_codes)
    outgoing = propagated.astype(jnp.bfloat16)
    owned_cols = lax.all_to_all(outgoing, "comp", split_axis=1, concat_axis=0, tiled=True)
    whole_operator = lax.all_gather(source_operator, "sub", axis=0, tiled=True)
    point_rows = owned_cols.T
    start_state = point_rows.astype(jnp.float32)
    state_now = start_state
    full_rows = point_rows
    for source_step in range(SRC_STEPS):
        driving = lax.dot_general(
            full_rows, whole_operator, (((1,), (1,)), ((), ())), preferred_element_type=jnp.float32
        )
        state_now = state_now + STEP_SIZE * state_now * driving
        if source_step + 1 < SRC_STEPS:
            full_rows = state_now.astype(jnp.bfloat16)
    returned = (state_now - start_state).astype(jnp.bfloat16).T
    home_bins = lax.all_to_all(returned, "comp", split_axis=0, concat_axis=1, tiled=True)
    return sea_float[None, :] * (propagated + home_bins.astype(jnp.float32))


LANES = 128
QUAD = 16
SECTOR = 32


def lane_pick(values, index):
    return jnp.take_along_axis(values, index, axis=1, mode="promise_in_bounds")


def make_tables(tab_ref, u, codes_of, north):
    lane = lax.broadcasted_iota(jnp.int32, (QUAD, LANES), 1)
    for half in range(2):
        code = lambda i: jnp.broadcast_to(codes_of(i, half), (QUAD, LANES))
        column = lane + LANES * half
        west = (column + NLON - code(0).astype(jnp.int32)) % NLON
        east = (column + code(1).astype(jnp.int32)) % NLON
        move = jnp.where(north, code(3), code(2)).astype(jnp.int32)
        lat_from = (column + NLON + move) % NLON
        for slot, source in enumerate((west, east, lat_from)):
            tab_ref[u, half, 2 * slot] = source % LANES
            tab_ref[u, half, 2 * slot + 1] = (source // LANES == half).astype(jnp.int32)
        tab_ref[u, half, 6] = code(4).astype(jnp.int32)


def stencil_kernel(sizes, *refs):
    bins_local, half_bins, rows_local, dependent = sizes
    if dependent:
        place, steps_ref, courant_ref, trig, own, own_codes, pair, near, far, start_out, field_out, tab = refs
    else:
        place, steps_ref, courant_ref, trig, own, own_codes, pair, start_out, field_out, tab = refs
    lat, sub, parity, first_group = place[0], place[1], place[2], place[3]
    chip_rows = 2 * rows_local
    halo = chip_rows if dependent else 0
    north = lat == (0 if dependent else 1)
    flip = north.astype(jnp.int32)
    pair_codes = half_bins
    near_codes = half_bins // 2

    def where_is(v):
        core = (v // rows_local + flip) % 2
        local = v % rows_local
        local = local + flip * (rows_local - 1 - 2 * local)
        return core, local, core == sub

    for u in range(halo + chip_rows):
        core, local, mine = where_is(u % chip_rows)

        def codes_of(i, half):
            at = pl.ds(pl.multiple_of(local * NLON + half * LANES, LANES), LANES)
            if u < halo:
                return jnp.where(
                    mine,
                    near[pl.ds(near_codes + i, 1), at],
                    far[pl.ds(near_codes + i, 1), at],
                )
            return jnp.where(mine, own_codes[i : i + 1, at], pair[pl.ds(pair_codes + i, 1), at])

        make_tables(tab, u, codes_of, north)

    def block(index, carry):
        sector, side = index // 2, index % 2
        east = (side + flip) % 2
        group = 2 * sector + parity
        band = jnp.minimum((first_group + group) // 2, courant_ref.shape[0] - 1)
        speed, count = courant_ref[band], steps_ref[band]
        trig_row = pl.ds(pl.multiple_of(SECTOR * flip + QUAD * side, QUAD), QUAD)
        part_row = pl.multiple_of(group * SECTOR + side * QUAD, QUAD)
        own_row = jnp.minimum(sub * half_bins + part_row, bins_local - QUAD)
        own_row = pl.multiple_of(own_row, QUAD)
        sent_row = pl.multiple_of(sector * SECTOR + side * QUAD, QUAD)
        field = []
        for u in range(halo + chip_rows):
            core, local, mine = where_is(u % chip_rows)
            both = []
            for half in range(2):
                at = pl.ds(pl.multiple_of(local * NLON + half * LANES, LANES), LANES)
                if u < halo:
                    value = jnp.where(
                        mine,
                        near[pl.ds(sent_row, QUAD), at],
                        far[pl.ds(sent_row, QUAD), at],
                    )
                else:
                    value = jnp.where(
                        mine,
                        own[pl.ds(own_row, QUAD), at] * tab[u, half, 6].astype(jnp.float32),
                        pair[pl.ds(part_row, QUAD), at],
                    )
                both.append(value)
            field.append(both)
        for t in range(MAXSTEPS):
            now = jnp.where(t < count, speed, 0.0)
            weight_x = now * trig[0, trig_row, :]
            weight_y = now * trig[1, trig_row, :]
            lowest = max(0, halo - (MAXSTEPS - 1 - t))
            for u in reversed(range(lowest, halo + chip_rows)):
                centre, behind = field[u], field[max(u - 1, 0)]
                moved = []
                for half in range(2):
                    index_x = tab[u, half, 2 * east]
                    same_x = tab[u, half, 2 * east + 1] == 1
                    index_y = tab[u, half, 4]
                    same_y = tab[u, half, 5] == 1
                    sea = tab[u, half, 6].astype(jnp.float32)
                    upwind_x = jnp.where(same_x, lane_pick(centre[half], index_x), lane_pick(centre[1 - half], index_x))
                    upwind_y = jnp.where(same_y, lane_pick(behind[half], index_y), lane_pick(behind[1 - half], index_y))
                    here = centre[half]
                    moved.append(sea * (here - weight_x * (here - upwind_x) - weight_y * (here - upwind_y)))
                field[u] = moved
        for v in range(chip_rows):
            core, local, mine = where_is(v)
            for half in range(2):
                value = field[halo + v][half]
                quarter = local * 2 + half
                start_out[quarter * 2 + core, pl.ds(sent_row, QUAD), :] = value.astype(jnp.bfloat16)
                at = pl.ds(pl.multiple_of(local * NLON + half * LANES, LANES), LANES)
                field_out[1 - mine.astype(jnp.int32), pl.ds(sent_row, QUAD), at] = value
        return carry

    lax.fori_loop(0, half_bins // (2 * QUAD), block, 0)


def stencil(sizes, place, substeps, courant, trig, own, own_codes, pair, halos=()):
    bins_local, half_bins, rows_local, dependent = sizes
    blocks = 4 * rows_local
    rows = (4 if dependent else 2) * rows_local
    smem = pl.BlockSpec(memory_space=pltpu.SMEM)
    vmem = pl.BlockSpec(memory_space=pltpu.VMEM)
    cells = half_bins // 2 * rows_local * 2 * NLON
    return pl.pallas_call(
        functools.partial(stencil_kernel, sizes),
        name="stencil_dependent" if dependent else "stencil_free",
        in_specs=[smem] * 3 + [vmem] * (4 + len(halos)),
        out_specs=[vmem, vmem],
        out_shape=[
            jax.ShapeDtypeStruct((blocks, half_bins // 2, LANES), jnp.bfloat16),
            jax.ShapeDtypeStruct((2, half_bins // 2, rows_local * NLON), jnp.float32),
        ],
        scratch_shapes=[pltpu.VMEM((rows, 2, 7, QUAD, LANES), jnp.int32)],
        cost_estimate=pl.CostEstimate(flops=cells * MAXSTEPS * 100, bytes_accessed=cells * 16, transcendentals=0),
    )(place, substeps, courant, trig, own, own_codes, pair, *halos)


def integrate_kernel(sizes, place, free, dependent, own_w, other_w, out, w_ref, state, driver, sem):
    bins_local, half_bins, comps = sizes
    lat, sub = place[0], place[1]
    w_rows = own_w.shape[0]
    pieces = 3
    piece = w_rows // pieces
    copies = []
    for which, source in enumerate((own_w, other_w)):
        for p in range(pieces):
            at = pl.ds(p * piece, piece)
            copy = pltpu.make_async_copy(source.at[at], w_ref.at[which, at], sem.at[which, p])
            copy.start()
            copies.append(copy)
    sectors = half_bins // (2 * SECTOR)
    groups = bins_local // SECTOR
    for c in range(comps):
        first = (c * groups) % 2
        for s in range(2):
            for k in range(sectors):
                for dep, source in enumerate((free, dependent)):
                    parity = (first + lat + dep) % 2
                    row = c * bins_local + s * half_bins + (2 * k + parity) * SECTOR
                    row = pl.ds(pl.multiple_of(row, SECTOR), SECTOR)
                    block = source[2 * c + s, k * SECTOR : (k + 1) * SECTOR, :]
                    driver[0, row, :] = block
                    state[row, :] = block.astype(jnp.float32)
    total = comps * bins_local
    for step in range(SRC_STEPS):
        read, write = step % 2, (step + 1) % 2
        base = (0 if step == 0 else 2)
        for which in range(2):
            half_at = (sub + which) % 2 * w_rows
            for p in range(pieces):
                if step == 0:
                    copies[which * pieces + p].wait()
                drive = jnp.dot(
                    w_ref[which, p * piece : (p + 1) * piece, :],
                    driver[0 if step == 0 else 1 + step % 2, :total, :],
                    preferred_element_type=jnp.float32,
                )
                row = pl.ds(pl.multiple_of(half_at + p * piece, 64), piece)
                value = state[row, :]
                value = value + STEP_SIZE * value * drive
                if step + 1 < SRC_STEPS:
                    state[row, :] = value
                    driver[1 + (step + 1) % 2, row, :] = value.astype(jnp.bfloat16)
                else:
                    begun = driver[0, row, :].astype(jnp.float32)
                    out[row, :] = (value - begun).astype(jnp.bfloat16)


def integrate(sizes, place, free, dependent, own_w, other_w):
    bins_local, half_bins, comps = sizes
    total = comps * bins_local
    spare = total + SECTOR
    smem = pl.BlockSpec(memory_space=pltpu.SMEM)
    vmem = pl.BlockSpec(memory_space=pltpu.VMEM)
    hbm = pl.BlockSpec(memory_space=pl.ANY)
    return pl.pallas_call(
        functools.partial(integrate_kernel, sizes),
        name="integrate",
        in_specs=[smem, vmem, vmem, hbm, hbm],
        out_specs=vmem,
        out_shape=jax.ShapeDtypeStruct((total, LANES), jnp.bfloat16),
        scratch_shapes=[
            pltpu.VMEM((2,) + own_w.shape, jnp.bfloat16),
            pltpu.VMEM((spare, LANES), jnp.float32),
            pltpu.VMEM((3, spare, LANES), jnp.bfloat16),
            pltpu.SemaphoreType.DMA((2, 3)),
        ],
        compiler_params=pltpu.CompilerParams(vmem_limit_bytes=40 << 20),
        cost_estimate=pl.CostEstimate(
            flops=2 * SRC_STEPS * total * total * LANES, bytes_accessed=2 * total * total, transcendentals=0
        ),
    )(place, free, dependent, own_w, other_w)


def finish_kernel(sizes, place, mine_free, mine_dep, got_free, got_dep, raised, sea, out):
    bins_local, half_bins = sizes
    sub, parity = place[1], place[2]
    for other, pair in enumerate(((mine_free, mine_dep), (got_free, got_dep))):
        for k in range(half_bins // (2 * SECTOR)):
            for dep, source in enumerate(pair):
                row = (sub + other) % 2 * half_bins + (2 * k + (parity + dep) % 2) * SECTOR

                @pl.when(row < bins_local)
                def _():
                    rows = pl.ds(pl.multiple_of(row, SECTOR), SECTOR)
                    for j in range(out.shape[1] // LANES):
                        at = slice(j * LANES, (j + 1) * LANES)
                        value = source[0, k * SECTOR : (k + 1) * SECTOR, at]
                        value = value + raised[j, rows, :].astype(jnp.float32)
                        out[rows, at] = sea[0:1, at] * value


def finish(sizes, place, mine_free, mine_dep, got_free, got_dep, raised, sea):
    bins_local, half_bins = sizes
    points = sea.shape[1]
    smem = pl.BlockSpec(memory_space=pltpu.SMEM)
    vmem = pl.BlockSpec(memory_space=pltpu.VMEM)
    first = pl.BlockSpec((1, half_bins // 2, points), lambda i: (0, 0, 0))
    return pl.pallas_call(
        functools.partial(finish_kernel, sizes),
        name="finish",
        grid=(1,),
        in_specs=[smem, first, first, first, first, vmem, vmem],
        out_specs=vmem,
        out_shape=jax.ShapeDtypeStruct((bins_local, points), jnp.float32),
    )(place, mine_free, mine_dep, got_free, got_dep, raised, sea)


def swap(values, bits):
    count = lax.axis_size("lat") * lax.axis_size("sub")
    return lax.ppermute(values, ("lat", "sub"), [(i, i ^ bits) for i in range(count)])


def two_chip_device(spectrum, sea_mask, neighbours, substeps, courant, source_operator):
    comp, lat, sub = (lax.axis_index(name) for name in ("comp", "lat", "sub"))
    comps = lax.axis_size("comp")
    bins_local, points_local = spectrum.shape
    rows_local = points_local // NLON
    groups = bins_local // SECTOR
    half_bins = (groups + 3) // 4 * 2 * SECTOR
    sea = sea_mask.astype(jnp.float32)
    codes = offset_codes(neighbours, sea, points_local).reshape(5, points_local)
    codes = codes.at[2:4].set(jnp.where(codes[2:4] == 2.0, 0.0, codes[2:4]))
    codes = jnp.pad(codes, ((0, 3), (0, 0)))
    first_group = comp * groups
    parity = (first_group + lat) % 2
    place_free = jnp.stack([lat, sub, parity, first_group + sub * (half_bins // SECTOR)])
    place_dep = jnp.stack([lat, sub, 1 - parity, first_group + sub * (half_bins // SECTOR)])
    angles = (jnp.arange(ND, dtype=jnp.float32) + 0.5) * (2.0 * math.pi / ND)
    trig = jnp.abs(jnp.stack([jnp.cos(angles), jnp.sin(angles)]))
    trig = jnp.broadcast_to(trig[:, :, None], (2, ND, LANES))

    padded = jnp.pad(spectrum, ((0, 2 * half_bins - bins_local), (0, 0)))
    to_pair = lax.dynamic_slice_in_dim(padded, (1 - sub) * half_bins, half_bins, 0) * sea[None, :]
    to_pair = jnp.concatenate([to_pair, codes], axis=0)
    sectors = padded.reshape(2, half_bins // (2 * SECTOR), 2, SECTOR, points_local)

    def to_chip(core):
        part = lax.dynamic_slice(
            sectors,
            (core, 0, parity, 0, 0),
            (1, half_bins // (2 * SECTOR), 1, SECTOR, points_local),
        ).reshape(half_bins // 2, points_local)
        part = part * sea[None, :]
        return jnp.concatenate([part, codes, codes], axis=0).astype(HALO_TYPE)

    pair = swap(to_pair, 1)
    near = swap(to_chip(sub), 2).astype(jnp.float32)
    far = swap(to_chip(1 - sub), 3).astype(jnp.float32)
    other_w = swap(source_operator, 1)

    sizes = (bins_local, half_bins, rows_local)
    free_start, free_field = stencil(sizes + (False,), place_free, substeps, courant, trig, spectrum, codes, pair)
    free_state = lax.all_to_all(free_start, ("comp", "sub"), split_axis=0, concat_axis=0, tiled=True)
    dep_start, dep_field = stencil(
        sizes + (True,), place_dep, substeps, courant, trig, spectrum, codes, pair, (near, far)
    )
    dep_state = lax.all_to_all(dep_start, ("comp", "sub"), split_axis=0, concat_axis=0, tiled=True)
    got_free = swap(free_field[1:], 1)
    got_dep = swap(dep_field[1:], 1)
    raised = integrate((bins_local, half_bins, comps), place_free, free_state, dep_state, source_operator, other_w)
    raised = raised.reshape(comps, bins_local, LANES)
    home = lax.all_to_all(raised, "comp", split_axis=0, concat_axis=0, tiled=True)
    return finish((bins_local, half_bins), place_free, free_field, dep_field, got_free, got_dep, home, sea[None, :])


def device_step(*arrays):
    bins_local, points_local = arrays[0].shape
    two_chips = (
        lax.axis_size("lat") == 2
        and lax.axis_size("sub") == 2
        and bins_local % SECTOR == 0
        and points_local % NLON == 0
        and points_local == lax.axis_size("comp") * LANES
    )
    return (two_chip_device if two_chips else per_device)(*arrays)


def solution(mesh):
    placed = (
        P("comp", ("members", "lat", "sub")),
        P(("members", "lat", "sub")),
        P(None, ("members", "lat", "sub")),
        P(),
        P(),
        P("sub", None),
    )
    return jax.shard_map(
        device_step,
        mesh=mesh,
        in_specs=placed,
        out_specs=P("comp", ("members", "lat", "sub")),
        check_vma=False,
    )
```

```python
import functools
import math

import jax
import jax.numpy as jnp
from jax import lax
from jax.experimental import pallas as pl
from jax.experimental.pallas import tpu as pltpu
from jax.sharding import PartitionSpec as P

NF = 30
ND = 64
NLON = 256
MAXSTEPS = 6
SRC_STEPS = 4


STEP_SIZE = 0.1


def extended(cells, sides, width):
    for axis, dim in sides:
        count = lax.axis_size(axis)
        ends = count - 1
        head = lax.slice_in_dim(cells, 0, width, axis=dim)
        tail = lax.slice_in_dim(cells, cells.shape[dim] - width, cells.shape[dim], axis=dim)
        cells = jnp.concatenate(
            [
                lax.ppermute(tail, axis, [(i, (i + 1) % count) for i in range(ends)]),
                cells,
                lax.ppermute(head, axis, [((i + 1) % count, i) for i in range(ends)]),
            ],
            axis=dim,
        )
    return cells


def bin_tables(global_bins, substeps, courant):
    frequency = global_bins // ND
    direction = global_bins % ND
    chosen = frequency[:, None] == jnp.arange(NF, dtype=jnp.int32)[None, :]
    bin_steps = jnp.sum(jnp.where(chosen, substeps[None, :], 0), axis=1)
    bin_speed = jnp.sum(jnp.where(chosen, courant[None, :], 0.0), axis=1)
    angles = (direction.astype(jnp.float32) + 0.5) * (2.0 * math.pi / ND)
    cosine = jnp.cos(angles)
    sine_dir = jnp.sin(angles)
    return (
        bin_steps,
        bin_speed * jnp.abs(cosine),
        bin_speed * jnp.abs(sine_dir),
        cosine > 0,
        sine_dir > 0,
    )


def offset_codes(neighbours, sea_float, points_local):
    position = lax.axis_index(("lat", "sub")) * points_local + jnp.arange(
        points_local, dtype=jnp.int32
    )
    column = position % NLON
    west_gap = (column - neighbours[0] % NLON) % NLON
    east_gap = (neighbours[1] % NLON - column) % NLON

    def vertical_code(index_row):
        column_move = (index_row % NLON - column + 1) % NLON - 1
        return jnp.where(index_row == position, 2, column_move)

    stacked = jnp.stack(
        [west_gap, east_gap, vertical_code(neighbours[2]), vertical_code(neighbours[3])]
    ).astype(jnp.float32)
    return jnp.concatenate([stacked, sea_float[None, :]], axis=0).reshape(
        5, points_local // NLON, NLON
    )


def column_roll(values, amount):
    return jnp.roll(values, amount, axis=-1)


def vertical_pick(other_rows, code_row, center):
    moved = jnp.where(
        code_row == -1.0,
        column_roll(other_rows, 1),
        jnp.where(code_row == 1.0, column_roll(other_rows, -1), other_rows),
    )
    return jnp.where(code_row == 2.0, center, moved)


def advance(substep, center, below, above, point_codes, tables):
    bin_steps, weight_x, weight_y, from_west, from_south = tables
    west_vals = jnp.where(
        point_codes[0][None] == 1.0, column_roll(center, 1), column_roll(center, 2)
    )
    east_vals = jnp.where(
        point_codes[1][None] == 1.0, column_roll(center, -1), column_roll(center, -2)
    )
    upwind_lon = jnp.where(from_west[:, None, None], west_vals, east_vals)
    south_vals = vertical_pick(below, point_codes[2][None], center)
    north_vals = vertical_pick(above, point_codes[3][None], center)
    upwind_lat = jnp.where(from_south[:, None, None], south_vals, north_vals)
    advanced = point_codes[4][None] * (
        center
        - weight_x[:, None, None] * (center - upwind_lon)
        - weight_y[:, None, None] * (center - upwind_lat)
    )
    return jnp.where((substep < bin_steps)[:, None, None], advanced, center)


def propagate(spec_part, global_bins, substeps, courant, point_codes):
    tables = bin_tables(global_bins, substeps, courant)
    bin_count = spec_part.shape[0]
    points_local = spec_part.shape[1]
    row_count = points_local // NLON
    field_now = spec_part.reshape(bin_count, row_count, NLON)
    for substep in range(MAXSTEPS):
        padded = extended(field_now, ((("lat", "sub"), 1),), 1)
        field_now = advance(substep, field_now, padded[:, :-2], padded[:, 2:], point_codes, tables)
    return field_now.reshape(bin_count, points_local)


def per_device(spectrum, sea_mask, neighbours, substeps, courant, source_operator):
    comp_index = lax.axis_index("comp")
    bins_local = spectrum.shape[0]
    points_local = spectrum.shape[1]
    sea_float = sea_mask.astype(jnp.float32)
    point_codes = offset_codes(neighbours, sea_float, points_local)
    field_start = sea_float[None, :] * spectrum
    first_bin = comp_index * bins_local
    held_bins = first_bin + jnp.arange(bins_local, dtype=jnp.int32)
    propagated = propagate(field_start, held_bins, substeps, courant, point_codes)
    outgoing = propagated.astype(jnp.bfloat16)
    owned_cols = lax.all_to_all(outgoing, "comp", split_axis=1, concat_axis=0, tiled=True)
    whole_operator = lax.all_gather(source_operator, "sub", axis=0, tiled=True)
    point_rows = owned_cols.T
    start_state = point_rows.astype(jnp.float32)
    state_now = start_state
    full_rows = point_rows
    for source_step in range(SRC_STEPS):
        driving = lax.dot_general(
            full_rows, whole_operator, (((1,), (1,)), ((), ())), preferred_element_type=jnp.float32
        )
        state_now = state_now + STEP_SIZE * state_now * driving
        if source_step + 1 < SRC_STEPS:
            full_rows = state_now.astype(jnp.bfloat16)
    returned = (state_now - start_state).astype(jnp.bfloat16).T
    home_bins = lax.all_to_all(returned, "comp", split_axis=0, concat_axis=1, tiled=True)
    return sea_float[None, :] * (propagated + home_bins.astype(jnp.float32))


LANES = 128
TILE = 8
QUAD = 16
SECTOR = 32
CODE_SCALE = 32767.5


def lane_pick(values, index):
    return jnp.take_along_axis(values, index, axis=1, mode="promise_in_bounds")


def split_columns(first, second):
    lane = lax.broadcasted_iota(jnp.int32, first.shape, 1)
    even, low = 2 * lane % LANES, lane < LANES // 2
    return (
        jnp.where(low, lane_pick(first, even), lane_pick(second, even)),
        jnp.where(low, lane_pick(first, even + 1), lane_pick(second, even + 1)),
    )


def join_columns(even, odd):
    lane = lax.broadcasted_iota(jnp.int32, even.shape, 1)
    index, is_even = lane // 2, lane % 2 == 0
    upper = index + LANES // 2
    return (
        jnp.where(is_even, lane_pick(even, index), lane_pick(odd, index)),
        jnp.where(is_even, lane_pick(even, upper), lane_pick(odd, upper)),
    )


def encode(values):
    return ((values * CODE_SCALE + 0.5).astype(jnp.int32) - 32768).astype(jnp.int16)


def decode(values):
    return (values.astype(jnp.int32) + 32768).astype(jnp.float32) * (1.0 / CODE_SCALE)


def pack_kernel(sizes, place, spectrum, neighbours, sea_mask, mine, to_pair, to_near, to_far):
    bins_local, half_bins, rows_local = sizes
    sub, parity = place[1], place[2]
    sectors = half_bins // (2 * SECTOR)
    for row in range(rows_local):
        halves = [slice(row * NLON + h * LANES, row * NLON + (h + 1) * LANES) for h in range(2)]
        sea = [sea_mask[0:1, at].astype(jnp.float32) for at in halves]
        moves = []
        for h, at in enumerate(halves):
            lane = lax.broadcasted_iota(jnp.int32, (4, LANES), 1) + h * LANES
            move = (neighbours[:, at] - lane + NLON // 2) % NLON - NLON // 2
            moves.append(jnp.concatenate([move.astype(jnp.float32), sea[h], jnp.zeros((3, LANES))], axis=0))
        codes = split_columns(*moves)
        for h, at in enumerate(halves):
            mine[half_bins : half_bins + TILE, at] = codes[h]
            to_pair[half_bins : half_bins + TILE, at] = codes[h]
            coded = codes[h].astype(jnp.int32).astype(jnp.int16)
            to_near[half_bins // 2 : half_bins // 2 + TILE, at] = coded
            to_far[half_bins // 2 : half_bins // 2 + TILE, at] = coded
    sea_rows = [
        jnp.broadcast_to(sea_mask[0:1, j * LANES : (j + 1) * LANES].astype(jnp.float32), (SECTOR, LANES))
        for j in range(2 * rows_local)
    ]

    def sector_of(index, carry):
        core, group = index // (2 * sectors), index % (2 * sectors)
        source = jnp.minimum(core * half_bins + group * SECTOR, bins_local - SECTOR)
        source = pl.ds(pl.multiple_of(source, SECTOR), SECTOR)
        target = pl.ds(pl.multiple_of(group * SECTOR, SECTOR), SECTOR)
        sent = pl.ds(pl.multiple_of(group // 2 * SECTOR, SECTOR), SECTOR)
        blocks = []
        for row in range(rows_local):
            pair = [
                spectrum[source, (2 * row + h) * LANES : (2 * row + h + 1) * LANES] * sea_rows[2 * row + h]
                for h in range(2)
            ]
            blocks += split_columns(*pair)

        @pl.when(core == sub)
        def _():
            for j, block in enumerate(blocks):
                mine[target, j * LANES : (j + 1) * LANES] = block

        @pl.when(core != sub)
        def _():
            for j, block in enumerate(blocks):
                to_pair[target, j * LANES : (j + 1) * LANES] = block

        @pl.when((group % 2 == parity) & (core == sub))
        def _():
            for j, block in enumerate(blocks):
                to_near[sent, j * LANES : (j + 1) * LANES] = encode(block)

        @pl.when((group % 2 == parity) & (core != sub))
        def _():
            for j, block in enumerate(blocks):
                to_far[sent, j * LANES : (j + 1) * LANES] = encode(block)

        return carry

    lax.fori_loop(0, 4 * sectors, sector_of, 0)


def pack(sizes, place, spectrum, neighbours, sea_mask):
    bins_local, half_bins, rows_local = sizes
    points = rows_local * NLON
    smem = pl.BlockSpec(memory_space=pltpu.SMEM)
    vmem = pl.BlockSpec(memory_space=pltpu.VMEM)
    return pl.pallas_call(
        functools.partial(pack_kernel, sizes),
        name="pack",
        in_specs=[smem, vmem, vmem, vmem],
        out_specs=[vmem] * 4,
        out_shape=[jax.ShapeDtypeStruct((half_bins + TILE, points), jnp.float32)] * 2
        + [jax.ShapeDtypeStruct((half_bins // 2 + TILE, points), jnp.int16)] * 2,
    )(place, spectrum, neighbours, sea_mask)


def stencil_kernel(sizes, *refs):
    half_bins, rows_local, dependent = sizes
    if dependent:
        place, steps_ref, courant_ref, trig, mine, pair, near, far, start_out, field_out, tab = refs
    else:
        place, steps_ref, courant_ref, trig, mine, pair, start_out, field_out, tab = refs
    lat, sub, parity, first_group = place[0], place[1], place[2], place[3]
    chip_rows = 2 * rows_local
    halo = chip_rows if dependent else 0
    north = lat == (0 if dependent else 1)
    flip = north.astype(jnp.int32)

    def where_is(v):
        core = (v // rows_local + flip) % 2
        local = v % rows_local
        local = local + flip * (rows_local - 1 - 2 * local)
        return core, local, core == sub

    def lanes_of(local, half):
        return pl.ds(pl.multiple_of(local * NLON + half * LANES, LANES), LANES)

    for u in range(halo + chip_rows):
        core, local, here = where_is(u % chip_rows)
        for half in range(2):
            at = lanes_of(local, half)
            if u < halo:
                rows = slice(half_bins // 2, half_bins // 2 + TILE)
                codes = jnp.where(here, near[rows, at].astype(jnp.int32), far[rows, at].astype(jnp.int32))
                codes = codes.astype(jnp.float32)
            else:
                rows = slice(half_bins, half_bins + TILE)
                codes = jnp.where(here, mine[rows, at], pair[rows, at])
            wide = lambda i: jnp.broadcast_to(codes[i : i + 1], (TILE, LANES))
            tab[u, half, 0] = wide(0)
            tab[u, half, 1] = wide(1)
            tab[u, half, 2] = jnp.where(north, wide(3), wide(2))
            tab[u, half, 3] = wide(4)

    def tiles(value):
        return value.reshape(QUAD // TILE, TILE, LANES)

    def turn(value, amount):
        return pltpu.roll(value.reshape(QUAD, LANES), amount % LANES, 1).reshape(QUAD // TILE, TILE, LANES)

    def block(sector, east):
        group = 2 * sector + parity
        band = jnp.minimum((first_group + group) // 2, courant_ref.shape[0] - 1)
        speed, count = courant_ref[band], steps_ref[band]
        side = (flip + east) % 2
        trig_row = pl.ds(pl.multiple_of(SECTOR * flip + QUAD * side, QUAD), QUAD)
        part_row = pl.ds(pl.multiple_of(group * SECTOR + side * QUAD, QUAD), QUAD)
        sent_row = pl.ds(pl.multiple_of(sector * SECTOR + side * QUAD, QUAD), QUAD)
        trig_x, trig_y = tiles(trig[0, trig_row, :]), tiles(trig[1, trig_row, :])
        field = []
        for u in range(halo + chip_rows):
            core, local, here = where_is(u % chip_rows)
            both = []
            for half in range(2):
                at = lanes_of(local, half)
                if u < halo:
                    value = jnp.where(
                        here, near[sent_row, at].astype(jnp.int32), far[sent_row, at].astype(jnp.int32)
                    )
                    value = (value + 32768).astype(jnp.float32) * (1.0 / CODE_SCALE)
                else:
                    value = jnp.where(here, mine[part_row, at], pair[part_row, at])
                both.append(tiles(value))
            field.append(both)
        for t in range(MAXSTEPS):
            now = jnp.where(t < count, speed, 0.0)
            weight_x, weight_y = now * trig_x, now * trig_y
            keep = 1.0 - weight_x - weight_y
            lowest = max(0, halo - (MAXSTEPS - 1 - t))
            for u in reversed(range(lowest, halo + chip_rows)):
                (even, odd), (even_b, odd_b) = field[u], field[max(u - 1, 0)]
                moved = []
                for half in range(2):
                    move_x, move_y = tab[u, half, east], tab[u, half, 2]
                    near_x = (move_x == (1.0 if east else -1.0))[None]
                    back, ahead = (move_y == -1.0)[None], (move_y == 1.0)[None]
                    if half == 0:
                        one = odd if east else turn(odd, 1)
                        two = turn(even, -1 if east else 1)
                        centre, same = even, even_b
                        minus, plus = turn(odd_b, 1), odd_b
                    else:
                        one = turn(even, -1) if east else even
                        two = turn(odd, -1 if east else 1)
                        centre, same = odd, odd_b
                        minus, plus = even_b, turn(even_b, -1)
                    upwind_x = jnp.where(near_x, one, two)
                    upwind_y = jnp.where(back, minus, jnp.where(ahead, plus, same))
                    value = keep * centre + weight_x * upwind_x + weight_y * upwind_y
                    moved.append(tab[u, half, 3][None] * value)
                field[u] = moved
        for v in range(chip_rows):
            core, local, here = where_is(v)
            for half in range(2):
                value = field[halo + v][half].reshape(QUAD, LANES)
                start_out[(local * 2 + half) * 2 + core, sent_row, :] = value.astype(jnp.bfloat16)
                field_out[1 - here.astype(jnp.int32), sent_row, lanes_of(local, half)] = value

    def both_sides(sector, carry):
        block(sector, 0)
        block(sector, 1)
        return carry

    lax.fori_loop(0, half_bins // (2 * SECTOR), both_sides, 0)


def stencil(sizes, place, substeps, courant, trig, *fields):
    half_bins, rows_local, dependent = sizes
    blocks = 4 * rows_local
    rows = (4 if dependent else 2) * rows_local
    smem = pl.BlockSpec(memory_space=pltpu.SMEM)
    vmem = pl.BlockSpec(memory_space=pltpu.VMEM)
    cells = half_bins // 2 * rows_local * 2 * NLON
    return pl.pallas_call(
        functools.partial(stencil_kernel, sizes),
        name="stencil_dependent" if dependent else "stencil_free",
        in_specs=[smem] * 3 + [vmem] * (1 + len(fields)),
        out_specs=[vmem, vmem],
        out_shape=[
            jax.ShapeDtypeStruct((blocks, half_bins // 2, LANES), jnp.bfloat16),
            jax.ShapeDtypeStruct((2, half_bins // 2, rows_local * NLON), jnp.float32),
        ],
        scratch_shapes=[pltpu.VMEM((rows, 2, 4, TILE, LANES), jnp.float32)],
        cost_estimate=pl.CostEstimate(flops=cells * MAXSTEPS * 100, bytes_accessed=cells * 16, transcendentals=0),
    )(place, substeps, courant, trig, *fields)


def integrate_kernel(sizes, place, free, dependent, own_w, other_w, out, w_ref, state, driver, sem):
    bins_local, half_bins, comps = sizes
    lat, sub = place[0], place[1]
    w_rows = own_w.shape[0]
    pieces = 3
    piece = w_rows // pieces
    copies = []
    for which, source in enumerate((own_w, other_w)):
        for p in range(pieces):
            at = pl.ds(p * piece, piece)
            copy = pltpu.make_async_copy(source.at[at], w_ref.at[which, at], sem.at[which, p])
            copy.start()
            copies.append(copy)
    sectors = half_bins // (2 * SECTOR)
    groups = bins_local // SECTOR
    for c in range(comps):
        first = (c * groups) % 2
        for s in range(2):
            for k in range(sectors):
                for dep, source in enumerate((free, dependent)):
                    parity = (first + lat + dep) % 2
                    row = c * bins_local + s * half_bins + (2 * k + parity) * SECTOR
                    row = pl.ds(pl.multiple_of(row, SECTOR), SECTOR)
                    block = source[2 * c + s, k * SECTOR : (k + 1) * SECTOR, :]
                    driver[0, row, :] = block
                    state[row, :] = block.astype(jnp.float32)
    total = comps * bins_local
    for step in range(SRC_STEPS):
        for which in range(2):
            half_at = (sub + which) % 2 * w_rows
            stretch = piece if step == 0 else w_rows
            for p in range(w_rows // stretch):
                if step == 0:
                    copies[which * pieces + p].wait()
                drive = jnp.dot(
                    w_ref[which, p * stretch : (p + 1) * stretch, :],
                    driver[0 if step == 0 else 1 + step % 2, :total, :],
                    preferred_element_type=jnp.float32,
                )
                row = pl.ds(pl.multiple_of(half_at + p * stretch, 64), stretch)
                value = state[row, :]
                value = value + STEP_SIZE * value * drive
                if step + 1 < SRC_STEPS:
                    state[row, :] = value
                    driver[1 + (step + 1) % 2, row, :] = value.astype(jnp.bfloat16)
                else:
                    begun = driver[0, row, :].astype(jnp.float32)
                    out[row, :] = (value - begun).astype(jnp.bfloat16)


def integrate(sizes, place, free, dependent, own_w, other_w):
    bins_local, half_bins, comps = sizes
    total = comps * bins_local
    spare = total + SECTOR
    smem = pl.BlockSpec(memory_space=pltpu.SMEM)
    vmem = pl.BlockSpec(memory_space=pltpu.VMEM)
    hbm = pl.BlockSpec(memory_space=pl.ANY)
    return pl.pallas_call(
        functools.partial(integrate_kernel, sizes),
        name="integrate",
        in_specs=[smem, vmem, vmem, hbm, hbm],
        out_specs=vmem,
        out_shape=jax.ShapeDtypeStruct((total, LANES), jnp.bfloat16),
        scratch_shapes=[
            pltpu.VMEM((2,) + own_w.shape, jnp.bfloat16),
            pltpu.VMEM((spare, LANES), jnp.float32),
            pltpu.VMEM((3, spare, LANES), jnp.bfloat16),
            pltpu.SemaphoreType.DMA((2, 3)),
        ],
        compiler_params=pltpu.CompilerParams(vmem_limit_bytes=60 << 20),
        cost_estimate=pl.CostEstimate(
            flops=2 * SRC_STEPS * total * total * LANES, bytes_accessed=2 * total * total, transcendentals=0
        ),
    )(place, free, dependent, own_w, other_w)


def finish_kernel(sizes, place, mine_free, mine_dep, got_free, got_dep, raised, sea_mask, out):
    bins_local, half_bins = sizes
    sub, parity = place[1], place[2]
    tiles = out.shape[1] // LANES
    sea = [
        jnp.broadcast_to(sea_mask[0:1, j * LANES : (j + 1) * LANES].astype(jnp.float32), (SECTOR, LANES))
        for j in range(tiles)
    ]
    for other, pair in enumerate(((mine_free, mine_dep), (got_free, got_dep))):
        for k in range(half_bins // (2 * SECTOR)):
            for dep, source in enumerate(pair):
                row = (sub + other) % 2 * half_bins + (2 * k + (parity + dep) % 2) * SECTOR

                @pl.when(row < bins_local)
                def _():
                    rows = pl.ds(pl.multiple_of(row, SECTOR), SECTOR)
                    for j in range(0, tiles, 2):
                        halves = [
                            source[0, k * SECTOR : (k + 1) * SECTOR, i * LANES : (i + 1) * LANES]
                            + raised[i, rows, :].astype(jnp.float32)
                            for i in (j, j + 1)
                        ]
                        for i, value in enumerate(join_columns(*halves)):
                            out[rows, (j + i) * LANES : (j + i + 1) * LANES] = sea[j + i] * value


def finish(sizes, place, mine_free, mine_dep, got_free, got_dep, raised, sea_mask):
    bins_local, half_bins = sizes
    points = sea_mask.shape[1]
    smem = pl.BlockSpec(memory_space=pltpu.SMEM)
    vmem = pl.BlockSpec(memory_space=pltpu.VMEM)
    first = pl.BlockSpec((1, half_bins // 2, points), lambda i: (0, 0, 0))
    return pl.pallas_call(
        functools.partial(finish_kernel, sizes),
        name="finish",
        grid=(1,),
        in_specs=[smem, first, first, first, first, vmem, vmem],
        out_specs=vmem,
        out_shape=jax.ShapeDtypeStruct((bins_local, points), jnp.float32),
    )(place, mine_free, mine_dep, got_free, got_dep, raised, sea_mask)


def swap(values, bits):
    count = lax.axis_size("lat") * lax.axis_size("sub")
    return lax.ppermute(values, ("lat", "sub"), [(i, i ^ bits) for i in range(count)])


def two_chip_device(spectrum, sea_mask, neighbours, substeps, courant, source_operator):
    comp, lat, sub = (lax.axis_index(name) for name in ("comp", "lat", "sub"))
    comps = lax.axis_size("comp")
    bins_local, points_local = spectrum.shape
    rows_local = points_local // NLON
    groups = bins_local // SECTOR
    half_bins = (groups + 3) // 4 * 2 * SECTOR
    sea_mask = sea_mask[None, :]
    first_group = comp * groups
    parity = (first_group + lat) % 2
    half_first = first_group + sub * (half_bins // SECTOR)
    place = jnp.stack([lat, sub, parity, half_first])
    place_dep = jnp.stack([lat, sub, 1 - parity, half_first])
    angles = (jnp.arange(ND, dtype=jnp.float32) + 0.5) * (2.0 * math.pi / ND)
    trig = jnp.abs(jnp.stack([jnp.cos(angles), jnp.sin(angles)]))
    trig = jnp.broadcast_to(trig[:, :, None], (2, ND, LANES))

    mine, to_pair, to_near, to_far = pack((bins_local, half_bins, rows_local), place, spectrum, neighbours, sea_mask)
    pair = swap(to_pair, 1)
    near = swap(to_near, 2)
    far = swap(to_far, 3)
    other_w = swap(source_operator, 1)

    free_start, free_field = stencil(
        (half_bins, rows_local, False), place, substeps, courant, trig, mine, pair
    )
    free_state = lax.all_to_all(free_start, ("comp", "sub"), split_axis=0, concat_axis=0, tiled=True)
    near, far, _ = lax.optimization_barrier((near, far, free_start))
    dep_start, dep_field = stencil(
        (half_bins, rows_local, True), place_dep, substeps, courant, trig, mine, pair, near, far
    )
    dep_state = lax.all_to_all(dep_start, ("comp", "sub"), split_axis=0, concat_axis=0, tiled=True)
    got_free = swap(free_field[1:], 1)
    got_dep = swap(dep_field[1:], 1)
    raised = integrate((bins_local, half_bins, comps), place, free_state, dep_state, source_operator, other_w)
    raised = raised.reshape(comps, bins_local, LANES)
    home = lax.all_to_all(raised, "comp", split_axis=0, concat_axis=0, tiled=True)
    return finish((bins_local, half_bins), place, free_field, dep_field, got_free, got_dep, home, sea_mask)


def device_step(*arrays):
    bins_local, points_local = arrays[0].shape
    two_chips = (
        lax.axis_size("lat") == 2
        and lax.axis_size("sub") == 2
        and bins_local % SECTOR == 0
        and points_local % NLON == 0
        and points_local == lax.axis_size("comp") * LANES
    )
    return (two_chip_device if two_chips else per_device)(*arrays)


def solution(mesh):
    placed = (
        P("comp", ("members", "lat", "sub")),
        P(("members", "lat", "sub")),
        P(None, ("members", "lat", "sub")),
        P(),
        P(),
        P("sub", None),
    )
    return jax.shard_map(
        device_step,
        mesh=mesh,
        in_specs=placed,
        out_specs=P("comp", ("members", "lat", "sub")),
        check_vma=False,
    )
```

```python
import functools
import math

import jax
import jax.numpy as jnp
import numpy as np
from jax import lax
from jax.experimental import pallas as pl
from jax.experimental.pallas import tpu as pltpu
from jax.sharding import PartitionSpec as P

NF = 30
ND = 64
NLON = 256
MAXSTEPS = 6
SRC_STEPS = 4


STEP_SIZE = 0.1


def extended(cells, sides, width):
    for axis, dim in sides:
        count = lax.axis_size(axis)
        ends = count - 1
        head = lax.slice_in_dim(cells, 0, width, axis=dim)
        tail = lax.slice_in_dim(cells, cells.shape[dim] - width, cells.shape[dim], axis=dim)
        cells = jnp.concatenate(
            [
                lax.ppermute(tail, axis, [(i, (i + 1) % count) for i in range(ends)]),
                cells,
                lax.ppermute(head, axis, [((i + 1) % count, i) for i in range(ends)]),
            ],
            axis=dim,
        )
    return cells


def bin_tables(global_bins, substeps, courant):
    frequency = global_bins // ND
    direction = global_bins % ND
    chosen = frequency[:, None] == jnp.arange(NF, dtype=jnp.int32)[None, :]
    bin_steps = jnp.sum(jnp.where(chosen, substeps[None, :], 0), axis=1)
    bin_speed = jnp.sum(jnp.where(chosen, courant[None, :], 0.0), axis=1)
    angles = (direction.astype(jnp.float32) + 0.5) * (2.0 * math.pi / ND)
    cosine = jnp.cos(angles)
    sine_dir = jnp.sin(angles)
    return (
        bin_steps,
        bin_speed * jnp.abs(cosine),
        bin_speed * jnp.abs(sine_dir),
        cosine > 0,
        sine_dir > 0,
    )


def offset_codes(neighbours, sea_float, points_local):
    position = lax.axis_index(("lat", "sub")) * points_local + jnp.arange(
        points_local, dtype=jnp.int32
    )
    column = position % NLON
    west_gap = (column - neighbours[0] % NLON) % NLON
    east_gap = (neighbours[1] % NLON - column) % NLON

    def vertical_code(index_row):
        column_move = (index_row % NLON - column + 1) % NLON - 1
        return jnp.where(index_row == position, 2, column_move)

    stacked = jnp.stack(
        [west_gap, east_gap, vertical_code(neighbours[2]), vertical_code(neighbours[3])]
    ).astype(jnp.float32)
    return jnp.concatenate([stacked, sea_float[None, :]], axis=0).reshape(
        5, points_local // NLON, NLON
    )


def column_roll(values, amount):
    return jnp.roll(values, amount, axis=-1)


def vertical_pick(other_rows, code_row, center):
    moved = jnp.where(
        code_row == -1.0,
        column_roll(other_rows, 1),
        jnp.where(code_row == 1.0, column_roll(other_rows, -1), other_rows),
    )
    return jnp.where(code_row == 2.0, center, moved)


def advance(substep, center, below, above, point_codes, tables):
    bin_steps, weight_x, weight_y, from_west, from_south = tables
    west_vals = jnp.where(
        point_codes[0][None] == 1.0, column_roll(center, 1), column_roll(center, 2)
    )
    east_vals = jnp.where(
        point_codes[1][None] == 1.0, column_roll(center, -1), column_roll(center, -2)
    )
    upwind_lon = jnp.where(from_west[:, None, None], west_vals, east_vals)
    south_vals = vertical_pick(below, point_codes[2][None], center)
    north_vals = vertical_pick(above, point_codes[3][None], center)
    upwind_lat = jnp.where(from_south[:, None, None], south_vals, north_vals)
    advanced = point_codes[4][None] * (
        center
        - weight_x[:, None, None] * (center - upwind_lon)
        - weight_y[:, None, None] * (center - upwind_lat)
    )
    return jnp.where((substep < bin_steps)[:, None, None], advanced, center)


def propagate(spec_part, global_bins, substeps, courant, point_codes):
    tables = bin_tables(global_bins, substeps, courant)
    bin_count = spec_part.shape[0]
    points_local = spec_part.shape[1]
    row_count = points_local // NLON
    field_now = spec_part.reshape(bin_count, row_count, NLON)
    for substep in range(MAXSTEPS):
        padded = extended(field_now, ((("lat", "sub"), 1),), 1)
        field_now = advance(substep, field_now, padded[:, :-2], padded[:, 2:], point_codes, tables)
    return field_now.reshape(bin_count, points_local)


def per_device(spectrum, sea_mask, neighbours, substeps, courant, source_operator):
    comp_index = lax.axis_index("comp")
    bins_local = spectrum.shape[0]
    points_local = spectrum.shape[1]
    sea_float = sea_mask.astype(jnp.float32)
    point_codes = offset_codes(neighbours, sea_float, points_local)
    field_start = sea_float[None, :] * spectrum
    first_bin = comp_index * bins_local
    held_bins = first_bin + jnp.arange(bins_local, dtype=jnp.int32)
    propagated = propagate(field_start, held_bins, substeps, courant, point_codes)
    outgoing = propagated.astype(jnp.bfloat16)
    owned_cols = lax.all_to_all(outgoing, "comp", split_axis=1, concat_axis=0, tiled=True)
    whole_operator = lax.all_gather(source_operator, "sub", axis=0, tiled=True)
    point_rows = owned_cols.T
    start_state = point_rows.astype(jnp.float32)
    state_now = start_state
    full_rows = point_rows
    for source_step in range(SRC_STEPS):
        driving = lax.dot_general(
            full_rows, whole_operator, (((1,), (1,)), ((), ())), preferred_element_type=jnp.float32
        )
        state_now = state_now + STEP_SIZE * state_now * driving
        if source_step + 1 < SRC_STEPS:
            full_rows = state_now.astype(jnp.bfloat16)
    returned = (state_now - start_state).astype(jnp.bfloat16).T
    home_bins = lax.all_to_all(returned, "comp", split_axis=0, concat_axis=1, tiled=True)
    return sea_float[None, :] * (propagated + home_bins.astype(jnp.float32))


LANES = 128
TILE = 8
QUAD = 16
SECTOR = 32
CODE_SCALE = 32767.5


def lane_pick(values, index):
    return jnp.take_along_axis(values, index, axis=1, mode="promise_in_bounds")


def split_columns(first, second):
    lane = lax.broadcasted_iota(jnp.int32, first.shape, 1)
    even, low = 2 * lane % LANES, lane < LANES // 2
    return (
        jnp.where(low, lane_pick(first, even), lane_pick(second, even)),
        jnp.where(low, lane_pick(first, even + 1), lane_pick(second, even + 1)),
    )


def join_columns(even, odd):
    lane = lax.broadcasted_iota(jnp.int32, even.shape, 1)
    index, is_even = lane // 2, lane % 2 == 0
    upper = index + LANES // 2
    return (
        jnp.where(is_even, lane_pick(even, index), lane_pick(odd, index)),
        jnp.where(is_even, lane_pick(even, upper), lane_pick(odd, upper)),
    )


def encode(values):
    return ((values * CODE_SCALE + 0.5).astype(jnp.int32) - 32768).astype(jnp.int16)


def decode(values):
    return (values.astype(jnp.int32) + 32768).astype(jnp.float32) * (1.0 / CODE_SCALE)


def device_place(bins_local):
    lat, sub = lax.axis_index("lat"), lax.axis_index("sub")
    first_group = lax.axis_index("comp") * (bins_local // SECTOR)
    return lat, sub, (first_group + lat) % 2, first_group


def pack_kernel(sizes, spectrum, neighbours, sea_mask, mine, to_pair, to_near, to_far):
    bins_local, half_bins, rows_local = sizes
    _, sub, parity, _ = device_place(bins_local)
    sectors = half_bins // (2 * SECTOR)
    for row in range(rows_local):
        halves = [slice(row * NLON + h * LANES, row * NLON + (h + 1) * LANES) for h in range(2)]
        sea = [sea_mask[0:1, at].astype(jnp.float32) for at in halves]
        moves = []
        for h, at in enumerate(halves):
            lane = lax.broadcasted_iota(jnp.int32, (4, LANES), 1) + h * LANES
            move = (neighbours[:, at] - lane + NLON // 2) % NLON - NLON // 2
            moves.append(jnp.concatenate([move.astype(jnp.float32), sea[h], jnp.zeros((3, LANES))], axis=0))
        codes = split_columns(*moves)
        for h, at in enumerate(halves):
            mine[half_bins : half_bins + TILE, at] = codes[h]
            to_pair[half_bins : half_bins + TILE, at] = codes[h]
            coded = codes[h].astype(jnp.int32).astype(jnp.int16)
            to_near[half_bins // 2 : half_bins // 2 + TILE, at] = coded
            to_far[half_bins // 2 : half_bins // 2 + TILE, at] = coded
    sea_rows = [
        jnp.broadcast_to(sea_mask[0:1, j * LANES : (j + 1) * LANES].astype(jnp.float32), (SECTOR, LANES))
        for j in range(2 * rows_local)
    ]

    for other in range(2):
        base = (sub + other) % 2 * half_bins
        whole, sent = (to_pair, to_far) if other else (mine, to_near)
        for k in range(sectors):
            for rest in range(2):
                group = (2 * k + (parity + rest) % 2) * SECTOR
                source = pl.ds(pl.multiple_of(jnp.minimum(base + group, bins_local - SECTOR), SECTOR), SECTOR)
                target = pl.ds(pl.multiple_of(group, SECTOR), SECTOR)
                for row in range(rows_local):
                    pair = [
                        spectrum[source, (2 * row + h) * LANES : (2 * row + h + 1) * LANES] * sea_rows[2 * row + h]
                        for h in range(2)
                    ]
                    for h, block in enumerate(split_columns(*pair)):
                        at = slice((2 * row + h) * LANES, (2 * row + h + 1) * LANES)
                        whole[target, at] = block
                        if not rest:
                            sent[k * SECTOR : (k + 1) * SECTOR, at] = encode(block)


def pack(sizes, spectrum, neighbours, sea_mask):
    bins_local, half_bins, rows_local = sizes
    points = rows_local * NLON
    vmem = pl.BlockSpec(memory_space=pltpu.VMEM)
    return pl.pallas_call(
        functools.partial(pack_kernel, sizes),
        name="pack",
        in_specs=[vmem, vmem, vmem],
        out_specs=[vmem] * 4,
        out_shape=[jax.ShapeDtypeStruct((half_bins + TILE, points), jnp.float32)] * 2
        + [jax.ShapeDtypeStruct((half_bins // 2 + TILE, points), jnp.int16)] * 2,
    )(spectrum, neighbours, sea_mask)


def stencil_kernel(sizes, *refs):
    bins_local, half_bins, rows_local, dependent = sizes
    if dependent:
        steps_ref, courant_ref, trig, mine, pair, near, far, start_out, field_out, tab = refs
    else:
        steps_ref, courant_ref, trig, mine, pair, start_out, field_out, tab = refs
    lat, sub, parity, first_group = device_place(bins_local)
    parity = (parity + int(dependent)) % 2
    first_group = first_group + sub * (half_bins // SECTOR)
    chip_rows = 2 * rows_local
    halo = chip_rows if dependent else 0
    north = lat == (0 if dependent else 1)
    flip = north.astype(jnp.int32)

    def where_is(v):
        core = (v // rows_local + flip) % 2
        local = v % rows_local
        local = local + flip * (rows_local - 1 - 2 * local)
        return core, local, core == sub

    def lanes_of(local, half):
        return pl.ds(pl.multiple_of(local * NLON + half * LANES, LANES), LANES)

    for u in range(halo + chip_rows):
        core, local, here = where_is(u % chip_rows)
        for half in range(2):
            at = lanes_of(local, half)
            if u < halo:
                rows = slice(half_bins // 2, half_bins // 2 + TILE)
                codes = jnp.where(here, near[rows, at].astype(jnp.int32), far[rows, at].astype(jnp.int32))
                codes = codes.astype(jnp.float32)
            else:
                rows = slice(half_bins, half_bins + TILE)
                codes = jnp.where(here, mine[rows, at], pair[rows, at])
            wide = lambda i: jnp.broadcast_to(codes[i : i + 1], (TILE, LANES))
            tab[u, half, 0] = wide(0)
            tab[u, half, 1] = wide(1)
            tab[u, half, 2] = jnp.where(north, wide(3), wide(2))
            tab[u, half, 3] = wide(4)

    def tiles(value):
        return value.reshape(QUAD // TILE, TILE, LANES)

    def turn(value, amount):
        return pltpu.roll(value.reshape(QUAD, LANES), amount % LANES, 1).reshape(QUAD // TILE, TILE, LANES)

    def block(sector, east):
        group = 2 * sector + parity
        band = jnp.minimum((first_group + group) // 2, courant_ref.shape[0] - 1)
        speed, count = courant_ref[band], steps_ref[band]
        side = (flip + east) % 2
        trig_row = pl.ds(pl.multiple_of(SECTOR * flip + QUAD * side, QUAD), QUAD)
        part_row = pl.ds(pl.multiple_of(group * SECTOR + side * QUAD, QUAD), QUAD)
        sent_row = pl.ds(pl.multiple_of(sector * SECTOR + side * QUAD, QUAD), QUAD)
        trig_x, trig_y = tiles(trig[0, trig_row, :]), tiles(trig[1, trig_row, :])
        field = []
        for u in range(halo + chip_rows):
            core, local, here = where_is(u % chip_rows)
            both = []
            for half in range(2):
                at = lanes_of(local, half)
                if u < halo:
                    value = jnp.where(
                        here, near[sent_row, at].astype(jnp.int32), far[sent_row, at].astype(jnp.int32)
                    )
                    value = (value + 32768).astype(jnp.float32) * (1.0 / CODE_SCALE)
                else:
                    value = jnp.where(here, mine[part_row, at], pair[part_row, at])
                both.append(tiles(value))
            field.append(both)
        for t in range(MAXSTEPS):
            now = jnp.where(t < count, speed, 0.0)
            weight_x, weight_y = now * trig_x, now * trig_y
            keep = 1.0 - weight_x - weight_y
            lowest = max(0, halo - (MAXSTEPS - 1 - t))
            for u in reversed(range(lowest, halo + chip_rows)):
                (even, odd), (even_b, odd_b) = field[u], field[max(u - 1, 0)]
                moved = []
                for half in range(2):
                    move_x, move_y = tab[u, half, east], tab[u, half, 2]
                    near_x = (move_x == (1.0 if east else -1.0))[None]
                    back, ahead = (move_y == -1.0)[None], (move_y == 1.0)[None]
                    if half == 0:
                        one = odd if east else turn(odd, 1)
                        two = turn(even, -1 if east else 1)
                        centre, same = even, even_b
                        minus, plus = turn(odd_b, 1), odd_b
                    else:
                        one = turn(even, -1) if east else even
                        two = turn(odd, -1 if east else 1)
                        centre, same = odd, odd_b
                        minus, plus = even_b, turn(even_b, -1)
                    upwind_x = jnp.where(near_x, one, two)
                    upwind_y = jnp.where(back, minus, jnp.where(ahead, plus, same))
                    value = keep * centre + weight_x * upwind_x + weight_y * upwind_y
                    moved.append(tab[u, half, 3][None] * value)
                field[u] = moved
        for v in range(chip_rows):
            core, local, here = where_is(v)
            for half in range(2):
                value = field[halo + v][half].reshape(QUAD, LANES)
                start_out[(local * 2 + half) * 2 + core, sent_row, :] = value.astype(jnp.bfloat16)
                field_out[1 - here.astype(jnp.int32), sent_row, lanes_of(local, half)] = value

    def both_sides(sector, carry):
        block(sector, 0)
        block(sector, 1)
        return carry

    lax.fori_loop(0, half_bins // (2 * SECTOR), both_sides, 0)


def stencil(sizes, substeps, courant, trig, *fields):
    bins_local, half_bins, rows_local, dependent = sizes
    blocks = 4 * rows_local
    rows = (4 if dependent else 2) * rows_local
    smem = pl.BlockSpec(memory_space=pltpu.SMEM)
    vmem = pl.BlockSpec(memory_space=pltpu.VMEM)
    cells = half_bins // 2 * rows_local * 2 * NLON
    return pl.pallas_call(
        functools.partial(stencil_kernel, sizes),
        name="stencil_dependent" if dependent else "stencil_free",
        in_specs=[smem] * 2 + [vmem] * (1 + len(fields)),
        out_specs=[vmem, vmem],
        out_shape=[
            jax.ShapeDtypeStruct((blocks, half_bins // 2, LANES), jnp.bfloat16),
            jax.ShapeDtypeStruct((2, half_bins // 2, rows_local * NLON), jnp.float32),
        ],
        scratch_shapes=[pltpu.VMEM((rows, 2, 4, TILE, LANES), jnp.float32)],
        cost_estimate=pl.CostEstimate(flops=cells * MAXSTEPS * 100, bytes_accessed=cells * 16, transcendentals=0),
    )(substeps, courant, trig, *fields)


def integrate_kernel(sizes, arrived, own_w, other_w, out, w_ref, joined, state, driver, sem):
    bins_local, half_bins, comps = sizes
    lat, sub, _, _ = device_place(bins_local)
    w_rows = own_w.shape[0]
    total = comps * bins_local
    copies = []
    for other, source in enumerate((own_w, other_w)):
        at = pl.ds(pl.multiple_of((sub + other) % 2 * w_rows, 64), w_rows)
        copy = pltpu.make_async_copy(source, w_ref.at[at], sem.at[other])
        copy.start()
        copies.append(copy)
    sectors = half_bins // (2 * SECTOR)
    groups = bins_local // SECTOR
    for c in range(comps):
        first = (c * groups) % 2
        for s in range(2):
            for k in range(sectors):
                for dep in range(2):
                    parity = (first + lat + dep) % 2
                    row = c * bins_local + s * half_bins + (2 * k + parity) * SECTOR
                    row = pl.ds(pl.multiple_of(row, SECTOR), SECTOR)
                    joined[row, :] = arrived[2 * c + s, (sectors * dep + k) * SECTOR : (sectors * dep + k + 1) * SECTOR, :]
    for b in range(total // LANES):
        at = slice(b * LANES, (b + 1) * LANES)
        block = joined[at, :].astype(jnp.float32).T
        state[:, at] = block
        driver[0, :, at] = block.astype(jnp.bfloat16)
    for copy in copies:
        copy.wait()
    width = 2 * LANES
    for step in range(SRC_STEPS):
        read = 0 if step == 0 else 1 + step % 2
        for first in range(0, total, width):
            at = slice(first, min(first + width, total))
            drive = lax.dot_general(
                driver[read], w_ref[at, :], (((1,), (1,)), ((), ())), preferred_element_type=jnp.float32
            )
            value = state[:, at]
            value = value + STEP_SIZE * value * drive
            if step + 1 < SRC_STEPS:
                state[:, at] = value
                driver[1 + (step + 1) % 2, :, at] = value.astype(jnp.bfloat16)
            else:
                raised = value - driver[0, :, at].astype(jnp.float32)
                out[at, :] = raised.T.astype(jnp.bfloat16)


def integrate(sizes, arrived, own_w, other_w):
    bins_local, half_bins, comps = sizes
    total = comps * bins_local
    vmem = pl.BlockSpec(memory_space=pltpu.VMEM)
    hbm = pl.BlockSpec(memory_space=pl.ANY)
    return pl.pallas_call(
        functools.partial(integrate_kernel, sizes),
        name="integrate",
        in_specs=[vmem, hbm, hbm],
        out_specs=vmem,
        out_shape=jax.ShapeDtypeStruct((total, LANES), jnp.bfloat16),
        scratch_shapes=[
            pltpu.VMEM((total, total), jnp.bfloat16),
            pltpu.VMEM((total + SECTOR, LANES), jnp.bfloat16),
            pltpu.VMEM((LANES, total), jnp.float32),
            pltpu.VMEM((3, LANES, total), jnp.bfloat16),
            pltpu.SemaphoreType.DMA((2,)),
        ],
        compiler_params=pltpu.CompilerParams(vmem_limit_bytes=60 << 20),
        cost_estimate=pl.CostEstimate(
            flops=2 * SRC_STEPS * total * total * LANES, bytes_accessed=2 * total * total, transcendentals=0
        ),
    )(arrived, own_w, other_w)


def finish_kernel(sizes, mine_free, mine_dep, got_free, got_dep, raised, sea_mask, out, whole, sem):
    bins_local, half_bins = sizes
    _, sub, parity, _ = device_place(bins_local)
    tiles = whole.shape[1] // LANES
    sea = [
        jnp.broadcast_to(sea_mask[0:1, j * LANES : (j + 1) * LANES].astype(jnp.float32), (SECTOR, LANES))
        for j in range(tiles)
    ]
    for other, pair in enumerate(((mine_free, mine_dep), (got_free, got_dep))):
        for k in range(half_bins // (2 * SECTOR)):
            for dep, source in enumerate(pair):
                row = (sub + other) % 2 * half_bins + (2 * k + (parity + dep) % 2) * SECTOR
                rows = pl.ds(pl.multiple_of(row, SECTOR), SECTOR)
                added = pl.ds(pl.multiple_of(jnp.minimum(row, bins_local - SECTOR), SECTOR), SECTOR)
                for j in range(0, tiles, 2):
                    halves = [
                        source[0, k * SECTOR : (k + 1) * SECTOR, i * LANES : (i + 1) * LANES]
                        + raised[i, added, :].astype(jnp.float32)
                        for i in (j, j + 1)
                    ]
                    for i, value in enumerate(join_columns(*halves)):
                        whole[rows, (j + i) * LANES : (j + i + 1) * LANES] = sea[j + i] * value
    copy = pltpu.make_async_copy(whole.at[pl.ds(0, bins_local)], out, sem)
    copy.start()
    copy.wait()


def finish(sizes, mine_free, mine_dep, got_free, got_dep, raised, sea_mask):
    bins_local, half_bins = sizes
    points = sea_mask.shape[1]
    vmem = pl.BlockSpec(memory_space=pltpu.VMEM)
    first = pl.BlockSpec((1, half_bins // 2, points), lambda i: (0, 0, 0))
    return pl.pallas_call(
        functools.partial(finish_kernel, sizes),
        name="finish",
        grid=(1,),
        in_specs=[first, first, first, first, vmem, vmem],
        out_specs=pl.BlockSpec(memory_space=pl.ANY),
        out_shape=jax.ShapeDtypeStruct((bins_local, points), jnp.float32),
        scratch_shapes=[pltpu.VMEM((2 * half_bins, points), jnp.float32), pltpu.SemaphoreType.DMA],
    )(mine_free, mine_dep, got_free, got_dep, raised, sea_mask)


def swap(values, bits):
    count = lax.axis_size("lat") * lax.axis_size("sub")
    return lax.ppermute(values, ("lat", "sub"), [(i, i ^ bits) for i in range(count)])


def two_chip_device(spectrum, sea_mask, neighbours, substeps, courant, source_operator):
    comps = lax.axis_size("comp")
    bins_local, points_local = spectrum.shape
    rows_local = points_local // NLON
    half_bins = (bins_local // SECTOR + 3) // 4 * 2 * SECTOR
    sea_mask = sea_mask[None, :]
    angles = (np.arange(ND, dtype=np.float32) + np.float32(0.5)) * np.float32(2.0 * math.pi / ND)
    trig = np.abs(np.stack([np.cos(angles), np.sin(angles)])).astype(np.float32)
    trig = jnp.asarray(np.repeat(trig[:, :, None], LANES, axis=2))

    mine, to_pair, to_near, to_far = pack((bins_local, half_bins, rows_local), spectrum, neighbours, sea_mask)
    pair = swap(to_pair, 1)
    near = swap(to_near, 2)
    far = swap(to_far, 3)
    other_w = swap(source_operator, 1)

    free_start, free_field = stencil((bins_local, half_bins, rows_local, False), substeps, courant, trig, mine, pair)
    near, far, _ = lax.optimization_barrier((near, far, free_start))
    dep_start, dep_field = stencil(
        (bins_local, half_bins, rows_local, True), substeps, courant, trig, mine, pair, near, far
    )
    start = jnp.concatenate([free_start, dep_start], axis=1)
    arrived = lax.all_to_all(start, ("comp", "sub"), split_axis=0, concat_axis=0, tiled=True)
    got_free = swap(free_field[1:], 1)
    got_dep = swap(dep_field[1:], 1)
    raised = integrate((bins_local, half_bins, comps), arrived, source_operator, other_w)
    raised = raised.reshape(comps, bins_local, LANES)
    home = lax.all_to_all(raised, "comp", split_axis=0, concat_axis=0, tiled=True)
    return finish((bins_local, half_bins), free_field, dep_field, got_free, got_dep, home, sea_mask)


def device_step(*arrays):
    bins_local, points_local = arrays[0].shape
    two_chips = (
        lax.axis_size("lat") == 2
        and lax.axis_size("sub") == 2
        and bins_local % SECTOR == 0
        and points_local % NLON == 0
        and points_local == lax.axis_size("comp") * LANES
        and lax.axis_size("comp") * bins_local % LANES == 0
    )
    return (two_chip_device if two_chips else per_device)(*arrays)


def solution(mesh):
    placed = (
        P("comp", ("members", "lat", "sub")),
        P(("members", "lat", "sub")),
        P(None, ("members", "lat", "sub")),
        P(),
        P(),
        P("sub", None),
    )
    return jax.shard_map(
        device_step,
        mesh=mesh,
        in_specs=placed,
        out_specs=P("comp", ("members", "lat", "sub")),
        check_vma=False,
    )
```

```python
import functools
import math

import jax
import jax.numpy as jnp
import numpy as np
from jax import lax
from jax.experimental import pallas as pl
from jax.experimental.pallas import tpu as pltpu
from jax.sharding import PartitionSpec as P

NF = 30
ND = 64
NLON = 256
MAXSTEPS = 6
SRC_STEPS = 4


STEP_SIZE = 0.1


def extended(cells, sides, width):
    for axis, dim in sides:
        count = lax.axis_size(axis)
        ends = count - 1
        head = lax.slice_in_dim(cells, 0, width, axis=dim)
        tail = lax.slice_in_dim(cells, cells.shape[dim] - width, cells.shape[dim], axis=dim)
        cells = jnp.concatenate(
            [
                lax.ppermute(tail, axis, [(i, (i + 1) % count) for i in range(ends)]),
                cells,
                lax.ppermute(head, axis, [((i + 1) % count, i) for i in range(ends)]),
            ],
            axis=dim,
        )
    return cells


def bin_tables(global_bins, substeps, courant):
    frequency = global_bins // ND
    direction = global_bins % ND
    chosen = frequency[:, None] == jnp.arange(NF, dtype=jnp.int32)[None, :]
    bin_steps = jnp.sum(jnp.where(chosen, substeps[None, :], 0), axis=1)
    bin_speed = jnp.sum(jnp.where(chosen, courant[None, :], 0.0), axis=1)
    angles = (direction.astype(jnp.float32) + 0.5) * (2.0 * math.pi / ND)
    cosine = jnp.cos(angles)
    sine_dir = jnp.sin(angles)
    return (
        bin_steps,
        bin_speed * jnp.abs(cosine),
        bin_speed * jnp.abs(sine_dir),
        cosine > 0,
        sine_dir > 0,
    )


def offset_codes(neighbours, sea_float, points_local):
    position = lax.axis_index(("lat", "sub")) * points_local + jnp.arange(
        points_local, dtype=jnp.int32
    )
    column = position % NLON
    west_gap = (column - neighbours[0] % NLON) % NLON
    east_gap = (neighbours[1] % NLON - column) % NLON

    def vertical_code(index_row):
        column_move = (index_row % NLON - column + 1) % NLON - 1
        return jnp.where(index_row == position, 2, column_move)

    stacked = jnp.stack(
        [west_gap, east_gap, vertical_code(neighbours[2]), vertical_code(neighbours[3])]
    ).astype(jnp.float32)
    return jnp.concatenate([stacked, sea_float[None, :]], axis=0).reshape(
        5, points_local // NLON, NLON
    )


def column_roll(values, amount):
    return jnp.roll(values, amount, axis=-1)


def vertical_pick(other_rows, code_row, center):
    moved = jnp.where(
        code_row == -1.0,
        column_roll(other_rows, 1),
        jnp.where(code_row == 1.0, column_roll(other_rows, -1), other_rows),
    )
    return jnp.where(code_row == 2.0, center, moved)


def advance(substep, center, below, above, point_codes, tables):
    bin_steps, weight_x, weight_y, from_west, from_south = tables
    west_vals = jnp.where(
        point_codes[0][None] == 1.0, column_roll(center, 1), column_roll(center, 2)
    )
    east_vals = jnp.where(
        point_codes[1][None] == 1.0, column_roll(center, -1), column_roll(center, -2)
    )
    upwind_lon = jnp.where(from_west[:, None, None], west_vals, east_vals)
    south_vals = vertical_pick(below, point_codes[2][None], center)
    north_vals = vertical_pick(above, point_codes[3][None], center)
    upwind_lat = jnp.where(from_south[:, None, None], south_vals, north_vals)
    advanced = point_codes[4][None] * (
        center
        - weight_x[:, None, None] * (center - upwind_lon)
        - weight_y[:, None, None] * (center - upwind_lat)
    )
    return jnp.where((substep < bin_steps)[:, None, None], advanced, center)


def propagate(spec_part, global_bins, substeps, courant, point_codes):
    tables = bin_tables(global_bins, substeps, courant)
    bin_count = spec_part.shape[0]
    points_local = spec_part.shape[1]
    row_count = points_local // NLON
    field_now = spec_part.reshape(bin_count, row_count, NLON)
    for substep in range(MAXSTEPS):
        padded = extended(field_now, ((("lat", "sub"), 1),), 1)
        field_now = advance(substep, field_now, padded[:, :-2], padded[:, 2:], point_codes, tables)
    return field_now.reshape(bin_count, points_local)


def per_device(spectrum, sea_mask, neighbours, substeps, courant, source_operator):
    comp_index = lax.axis_index("comp")
    bins_local = spectrum.shape[0]
    points_local = spectrum.shape[1]
    sea_float = sea_mask.astype(jnp.float32)
    point_codes = offset_codes(neighbours, sea_float, points_local)
    field_start = sea_float[None, :] * spectrum
    first_bin = comp_index * bins_local
    held_bins = first_bin + jnp.arange(bins_local, dtype=jnp.int32)
    propagated = propagate(field_start, held_bins, substeps, courant, point_codes)
    outgoing = propagated.astype(jnp.bfloat16)
    owned_cols = lax.all_to_all(outgoing, "comp", split_axis=1, concat_axis=0, tiled=True)
    whole_operator = lax.all_gather(source_operator, "sub", axis=0, tiled=True)
    point_rows = owned_cols.T
    start_state = point_rows.astype(jnp.float32)
    state_now = start_state
    full_rows = point_rows
    for source_step in range(SRC_STEPS):
        driving = lax.dot_general(
            full_rows, whole_operator, (((1,), (1,)), ((), ())), preferred_element_type=jnp.float32
        )
        state_now = state_now + STEP_SIZE * state_now * driving
        if source_step + 1 < SRC_STEPS:
            full_rows = state_now.astype(jnp.bfloat16)
    returned = (state_now - start_state).astype(jnp.bfloat16).T
    home_bins = lax.all_to_all(returned, "comp", split_axis=0, concat_axis=1, tiled=True)
    return sea_float[None, :] * (propagated + home_bins.astype(jnp.float32))


LANES = 128
TILE = 8
QUAD = 16
SECTOR = 32
CODE_SCALE = 32767.5
GRANT = pltpu.CompilerParams(vmem_limit_bytes=12 << 20)


def lane_pick(values, index):
    return jnp.take_along_axis(values, index, axis=1, mode="promise_in_bounds")


def split_columns(first, second):
    lane = lax.broadcasted_iota(jnp.int32, first.shape, 1)
    even, low = 2 * lane % LANES, lane < LANES // 2
    return (
        jnp.where(low, lane_pick(first, even), lane_pick(second, even)),
        jnp.where(low, lane_pick(first, even + 1), lane_pick(second, even + 1)),
    )


def join_columns(even, odd):
    lane = lax.broadcasted_iota(jnp.int32, even.shape, 1)
    index, is_even = lane // 2, lane % 2 == 0
    upper = index + LANES // 2
    return (
        jnp.where(is_even, lane_pick(even, index), lane_pick(odd, index)),
        jnp.where(is_even, lane_pick(even, upper), lane_pick(odd, upper)),
    )


def encode(values):
    return ((values * CODE_SCALE + 0.5).astype(jnp.int32) - 32768).astype(jnp.int16)


def decode(values):
    return (values.astype(jnp.int32) + 32768).astype(jnp.float32) * (1.0 / CODE_SCALE)


def device_place(bins_local):
    lat, sub = lax.axis_index("lat"), lax.axis_index("sub")
    first_group = lax.axis_index("comp") * (bins_local // SECTOR)
    return lat, sub, (first_group + lat) % 2, first_group


def pack_kernel(sizes, spectrum, neighbours, sea_mask, mine, to_pair, to_near, to_far):
    bins_local, half_bins, rows_local = sizes
    _, sub, parity, _ = device_place(bins_local)
    sectors = half_bins // (2 * SECTOR)
    for row in range(rows_local):
        halves = [slice(row * NLON + h * LANES, row * NLON + (h + 1) * LANES) for h in range(2)]
        sea = [sea_mask[0:1, at].astype(jnp.float32) for at in halves]
        moves = []
        for h, at in enumerate(halves):
            lane = lax.broadcasted_iota(jnp.int32, (4, LANES), 1) + h * LANES
            move = (neighbours[:, at] - lane + NLON // 2) % NLON - NLON // 2
            moves.append(jnp.concatenate([move.astype(jnp.float32), sea[h], jnp.zeros((3, LANES))], axis=0))
        codes = split_columns(*moves)
        for h, at in enumerate(halves):
            mine[half_bins : half_bins + TILE, at] = codes[h]
            to_pair[half_bins : half_bins + TILE, at] = codes[h]
            coded = codes[h].astype(jnp.int32).astype(jnp.int16)
            to_near[half_bins // 2 : half_bins // 2 + TILE, at] = coded
            to_far[half_bins // 2 : half_bins // 2 + TILE, at] = coded
    sea_rows = [
        jnp.broadcast_to(sea_mask[0:1, j * LANES : (j + 1) * LANES].astype(jnp.float32), (SECTOR, LANES))
        for j in range(2 * rows_local)
    ]

    for other in range(2):
        base = (sub + other) % 2 * half_bins
        whole, sent = (to_pair, to_far) if other else (mine, to_near)
        for k in range(sectors):
            for rest in range(2):
                group = (2 * k + (parity + rest) % 2) * SECTOR
                source = pl.ds(pl.multiple_of(jnp.minimum(base + group, bins_local - SECTOR), SECTOR), SECTOR)
                target = pl.ds(pl.multiple_of(group, SECTOR), SECTOR)
                for row in range(rows_local):
                    pair = [
                        spectrum[source, (2 * row + h) * LANES : (2 * row + h + 1) * LANES] * sea_rows[2 * row + h]
                        for h in range(2)
                    ]
                    for h, block in enumerate(split_columns(*pair)):
                        at = slice((2 * row + h) * LANES, (2 * row + h + 1) * LANES)
                        whole[target, at] = block
                        if not rest:
                            sent[k * SECTOR : (k + 1) * SECTOR, at] = encode(block)


def pack(sizes, spectrum, neighbours, sea_mask):
    bins_local, half_bins, rows_local = sizes
    points = rows_local * NLON
    vmem = pl.BlockSpec(memory_space=pltpu.VMEM)
    return pl.pallas_call(
        functools.partial(pack_kernel, sizes),
        name="pack",
        compiler_params=GRANT,
        in_specs=[vmem, vmem, vmem],
        out_specs=[vmem] * 4,
        out_shape=[pltpu.VMEM((half_bins + TILE, points), jnp.float32)] * 2
        + [pltpu.VMEM((half_bins // 2 + TILE, points), jnp.int16)] * 2,
    )(spectrum, neighbours, sea_mask)


def stencil_kernel(sizes, *refs):
    bins_local, half_bins, rows_local, dependent = sizes
    if dependent:
        (steps_ref, courant_ref, trig, mine, pair, near, far, free_start, own_w, other_w) = refs[:10]
        start_out, field_out, whole_w, tab, sem = refs[10:]
    else:
        steps_ref, courant_ref, trig, mine, pair, start_out, field_out, tab = refs
    lat, sub, parity, first_group = device_place(bins_local)
    parity = (parity + int(dependent)) % 2
    first_group = first_group + sub * (half_bins // SECTOR)
    chip_rows = 2 * rows_local
    halo = chip_rows if dependent else 0
    sent_first = 0
    copies = []
    if dependent:
        w_rows = own_w.shape[0]
        for other, source in enumerate((own_w, other_w)):
            at = pl.ds(pl.multiple_of((sub + other) % 2 * w_rows, 64), w_rows)
            copy = pltpu.make_async_copy(source, whole_w.at[at], sem.at[other])
            copy.start()
            copies.append(copy)
        sent_first = half_bins // 2
        for block in range(start_out.shape[0]):
            start_out[block, :sent_first, :] = free_start[block]
    north = lat == (0 if dependent else 1)
    flip = north.astype(jnp.int32)

    def where_is(v):
        core = (v // rows_local + flip) % 2
        local = v % rows_local
        local = local + flip * (rows_local - 1 - 2 * local)
        return core, local, core == sub

    def lanes_of(local, half):
        return pl.ds(pl.multiple_of(local * NLON + half * LANES, LANES), LANES)

    for u in range(halo + chip_rows):
        core, local, here = where_is(u % chip_rows)
        for half in range(2):
            at = lanes_of(local, half)
            if u < halo:
                rows = slice(half_bins // 2, half_bins // 2 + TILE)
                codes = jnp.where(here, near[rows, at].astype(jnp.int32), far[rows, at].astype(jnp.int32))
                codes = codes.astype(jnp.float32)
            else:
                rows = slice(half_bins, half_bins + TILE)
                codes = jnp.where(here, mine[rows, at], pair[rows, at])
            wide = lambda i: jnp.broadcast_to(codes[i : i + 1], (TILE, LANES))
            tab[u, half, 0] = wide(0)
            tab[u, half, 1] = wide(1)
            tab[u, half, 2] = jnp.where(north, wide(3), wide(2))
            tab[u, half, 3] = wide(4)

    def tiles(value):
        return value.reshape(QUAD // TILE, TILE, LANES)

    def turn(value, amount):
        return pltpu.roll(value.reshape(QUAD, LANES), amount % LANES, 1).reshape(QUAD // TILE, TILE, LANES)

    def block(sector, east):
        group = 2 * sector + parity
        band = jnp.minimum((first_group + group) // 2, courant_ref.shape[0] - 1)
        speed, count = courant_ref[band], steps_ref[band]
        side = (flip + east) % 2
        trig_row = pl.ds(pl.multiple_of(SECTOR * flip + QUAD * side, QUAD), QUAD)
        part_row = pl.ds(pl.multiple_of(group * SECTOR + side * QUAD, QUAD), QUAD)
        sent_row = pl.ds(pl.multiple_of(sector * SECTOR + side * QUAD, QUAD), QUAD)
        start_row = pl.ds(pl.multiple_of(sent_first + sector * SECTOR + side * QUAD, QUAD), QUAD)
        trig_x, trig_y = tiles(trig[0, trig_row, :]), tiles(trig[1, trig_row, :])
        field = []
        for u in range(halo + chip_rows):
            core, local, here = where_is(u % chip_rows)
            both = []
            for half in range(2):
                at = lanes_of(local, half)
                if u < halo:
                    value = jnp.where(
                        here, near[sent_row, at].astype(jnp.int32), far[sent_row, at].astype(jnp.int32)
                    )
                    value = (value + 32768).astype(jnp.float32) * (1.0 / CODE_SCALE)
                else:
                    value = jnp.where(here, mine[part_row, at], pair[part_row, at])
                both.append(tiles(value))
            field.append(both)
        for t in range(MAXSTEPS):
            now = jnp.where(t < count, speed, 0.0)
            weight_x, weight_y = now * trig_x, now * trig_y
            keep = 1.0 - weight_x - weight_y
            lowest = max(0, halo - (MAXSTEPS - 1 - t))
            for u in reversed(range(lowest, halo + chip_rows)):
                (even, odd), (even_b, odd_b) = field[u], field[max(u - 1, 0)]
                moved = []
                for half in range(2):
                    move_x, move_y = tab[u, half, east], tab[u, half, 2]
                    near_x = (move_x == (1.0 if east else -1.0))[None]
                    back, ahead = (move_y == -1.0)[None], (move_y == 1.0)[None]
                    if half == 0:
                        one = odd if east else turn(odd, 1)
                        two = turn(even, -1 if east else 1)
                        centre, same = even, even_b
                        minus, plus = turn(odd_b, 1), odd_b
                    else:
                        one = turn(even, -1) if east else even
                        two = turn(odd, -1 if east else 1)
                        centre, same = odd, odd_b
                        minus, plus = even_b, turn(even_b, -1)
                    upwind_x = jnp.where(near_x, one, two)
                    upwind_y = jnp.where(back, minus, jnp.where(ahead, plus, same))
                    value = keep * centre + weight_x * upwind_x + weight_y * upwind_y
                    moved.append(tab[u, half, 3][None] * value)
                field[u] = moved
        for v in range(chip_rows):
            core, local, here = where_is(v)
            for half in range(2):
                value = field[halo + v][half].reshape(QUAD, LANES)
                start_out[(local * 2 + half) * 2 + core, start_row, :] = value.astype(jnp.bfloat16)
                field_out[1 - here.astype(jnp.int32), sent_row, lanes_of(local, half)] = value

    def both_sides(sector, carry):
        block(sector, 0)
        block(sector, 1)
        return carry

    lax.fori_loop(0, half_bins // (2 * SECTOR), both_sides, 0)
    for copy in copies:
        copy.wait()


def stencil(sizes, substeps, courant, trig, *fields, operator=()):
    bins_local, half_bins, rows_local, dependent = sizes
    blocks = 4 * rows_local
    rows = (4 if dependent else 2) * rows_local
    smem = pl.BlockSpec(memory_space=pltpu.SMEM)
    vmem = pl.BlockSpec(memory_space=pltpu.VMEM)
    hbm = pl.BlockSpec(memory_space=pl.ANY)
    cells = half_bins // 2 * rows_local * 2 * NLON
    start_bins = half_bins if dependent else half_bins // 2
    out_shape = [
        pltpu.VMEM((blocks, start_bins, LANES), jnp.bfloat16),
        pltpu.VMEM((2, half_bins // 2, rows_local * NLON), jnp.float32),
    ]
    scratch = [pltpu.VMEM((rows, 2, 4, TILE, LANES), jnp.float32)]
    if dependent:
        total = operator[0].shape[1]
        out_shape.append(pltpu.VMEM((total, total), jnp.bfloat16))
        scratch.append(pltpu.SemaphoreType.DMA((2,)))
    return pl.pallas_call(
        functools.partial(stencil_kernel, sizes),
        name="stencil_dependent" if dependent else "stencil_free",
        compiler_params=GRANT,
        in_specs=[smem] * 2 + [vmem] * (1 + len(fields)) + [hbm] * len(operator),
        out_specs=[vmem] * len(out_shape),
        out_shape=out_shape,
        scratch_shapes=scratch,
        cost_estimate=pl.CostEstimate(flops=cells * MAXSTEPS * 100, bytes_accessed=cells * 16, transcendentals=0),
    )(*map(off_chip, (substeps, courant, trig)), *map(on_chip, fields), *map(off_chip, operator))


def integrate_kernel(sizes, arrived, whole_w, out, state, driver):
    bins_local, half_bins, comps = sizes
    lat = lax.axis_index("lat")
    total = comps * bins_local
    sectors = half_bins // (2 * SECTOR)
    groups = bins_local // SECTOR
    for c in range(comps):
        first = (c * groups) % 2
        for s in range(2):
            for k in range(sectors):
                for dep in range(2):
                    parity = (first + lat + dep) % 2
                    row = c * bins_local + s * half_bins + (2 * k + parity) * SECTOR
                    row = pl.ds(pl.multiple_of(row, SECTOR), SECTOR)
                    block = arrived[2 * c + s, (sectors * dep + k) * SECTOR : (sectors * dep + k + 1) * SECTOR, :]
                    driver[0, row, :] = block
                    state[row, :] = block.astype(jnp.float32)
    stretch = total // 2
    for step in range(SRC_STEPS):
        read = 0 if step == 0 else 1 + step % 2
        for first in range(0, total, stretch):
            at = slice(first, first + stretch)
            drive = jnp.dot(whole_w[at, :], driver[read, :total, :], preferred_element_type=jnp.float32)
            value = state[at, :]
            value = value + STEP_SIZE * value * drive
            if step + 1 < SRC_STEPS:
                state[at, :] = value
                driver[1 + (step + 1) % 2, at, :] = value.astype(jnp.bfloat16)
            else:
                out[at, :] = (value - driver[0, at, :].astype(jnp.float32)).astype(jnp.bfloat16)


def integrate(sizes, arrived, whole_w):
    bins_local, half_bins, comps = sizes
    total = comps * bins_local
    vmem = pl.BlockSpec(memory_space=pltpu.VMEM)
    return pl.pallas_call(
        functools.partial(integrate_kernel, sizes),
        name="integrate",
        compiler_params=GRANT,
        in_specs=[vmem, vmem],
        out_specs=vmem,
        out_shape=pltpu.VMEM((total, LANES), jnp.bfloat16),
        scratch_shapes=[
            pltpu.VMEM((total + SECTOR, LANES), jnp.float32),
            pltpu.VMEM((3, total + SECTOR, LANES), jnp.bfloat16),
        ],
        cost_estimate=pl.CostEstimate(
            flops=2 * SRC_STEPS * total * total * LANES, bytes_accessed=2 * total * total, transcendentals=0
        ),
    )(on_chip(arrived), on_chip(whole_w))


def finish_kernel(sizes, mine_free, mine_dep, got_free, got_dep, raised, sea_mask, out, whole, sem):
    bins_local, half_bins = sizes
    _, sub, parity, _ = device_place(bins_local)
    tiles = whole.shape[1] // LANES
    sea = [
        jnp.broadcast_to(sea_mask[0:1, j * LANES : (j + 1) * LANES].astype(jnp.float32), (SECTOR, LANES))
        for j in range(tiles)
    ]
    sectors = half_bins // (2 * SECTOR)

    def rows_out(group, semaphore):
        at = pl.ds(pl.multiple_of(group, SECTOR), SECTOR)
        return pltpu.make_async_copy(whole.at[at], out.at[at], semaphore)

    for other, pair in enumerate(((mine_free, mine_dep), (got_free, got_dep))):
        base = (sub + other) % 2 * half_bins
        for k in range(sectors):
            for dep, source in enumerate(pair):
                row = base + (2 * k + (parity + dep) % 2) * SECTOR
                rows = pl.ds(pl.multiple_of(row, SECTOR), SECTOR)
                added = pl.ds(pl.multiple_of(jnp.minimum(row, bins_local - SECTOR), SECTOR), SECTOR)
                for j in range(0, tiles, 2):
                    halves = [
                        source[0, k * SECTOR : (k + 1) * SECTOR, i * LANES : (i + 1) * LANES]
                        + raised[i, added, :].astype(jnp.float32)
                        for i in (j, j + 1)
                    ]
                    for i, value in enumerate(join_columns(*halves)):
                        whole[rows, (j + i) * LANES : (j + i + 1) * LANES] = sea[j + i] * value
            for rest in range(2):
                group = base + (2 * k + rest) * SECTOR

                @pl.when(group < bins_local)
                def _():
                    rows_out(group, sem.at[other, k, rest]).start()

    for other in range(2):
        for k in range(sectors):
            for rest in range(2):
                group = (sub + other) % 2 * half_bins + (2 * k + rest) * SECTOR

                @pl.when(group < bins_local)
                def _():
                    rows_out(group, sem.at[other, k, rest]).wait()


def finish(sizes, mine_free, mine_dep, got_free, got_dep, raised, sea_mask):
    bins_local, half_bins = sizes
    points = sea_mask.shape[1]
    vmem = pl.BlockSpec(memory_space=pltpu.VMEM)
    fields = [on_chip(field) for field in (mine_free, mine_dep, got_free, got_dep, raised)]
    return pl.pallas_call(
        functools.partial(finish_kernel, sizes),
        name="finish",
        compiler_params=GRANT,
        in_specs=[vmem] * 6,
        out_specs=pl.BlockSpec(memory_space=pl.ANY),
        out_shape=jax.ShapeDtypeStruct((bins_local, points), jnp.float32),
        scratch_shapes=[
            pltpu.VMEM((2 * half_bins, points), jnp.float32),
            pltpu.SemaphoreType.DMA((2, half_bins // (2 * SECTOR), 2)),
        ],
    )(*fields, sea_mask)


def on_chip(values):
    return pltpu.with_memory_space_constraint(values, pltpu.VMEM)


def off_chip(values):
    return pltpu.with_memory_space_constraint(values, pltpu.HBM)


def swap(values, bits):
    count = lax.axis_size("lat") * lax.axis_size("sub")
    return lax.ppermute(values, ("lat", "sub"), [(i, i ^ bits) for i in range(count)])


def two_chip_device(spectrum, sea_mask, neighbours, substeps, courant, source_operator):
    comps = lax.axis_size("comp")
    bins_local, points_local = spectrum.shape
    rows_local = points_local // NLON
    half_bins = (bins_local // SECTOR + 3) // 4 * 2 * SECTOR
    sea_mask = sea_mask[None, :]
    angles = (np.arange(ND, dtype=np.float32) + np.float32(0.5)) * np.float32(2.0 * math.pi / ND)
    trig = np.abs(np.stack([np.cos(angles), np.sin(angles)])).astype(np.float32)
    trig = jnp.asarray(np.repeat(trig[:, :, None], LANES, axis=2))

    mine, to_pair, to_near, to_far = pack((bins_local, half_bins, rows_local), spectrum, neighbours, sea_mask)
    pair = swap(to_pair, 1)
    near = swap(to_near, 2)
    far = swap(to_far, 3)
    other_w = swap(source_operator, 1)

    free_start, free_field = stencil((bins_local, half_bins, rows_local, False), substeps, courant, trig, mine, pair)
    near, far, _ = lax.optimization_barrier((near, far, free_start))
    start, dep_field, whole_w = stencil(
        (bins_local, half_bins, rows_local, True),
        substeps,
        courant,
        trig,
        mine,
        pair,
        near,
        far,
        free_start,
        operator=(source_operator, other_w),
    )
    arrived = lax.all_to_all(start, ("comp", "sub"), split_axis=0, concat_axis=0, tiled=True)
    got_free = swap(free_field[1:], 1)
    got_dep = swap(dep_field[1:], 1)
    raised = integrate((bins_local, half_bins, comps), arrived, whole_w)
    raised = raised.reshape(comps, bins_local, LANES)
    home = lax.all_to_all(raised, "comp", split_axis=0, concat_axis=0, tiled=True)
    return finish((bins_local, half_bins), free_field, dep_field, got_free, got_dep, home, sea_mask)


def device_step(*arrays):
    bins_local, points_local = arrays[0].shape
    two_chips = (
        lax.axis_size("lat") == 2
        and lax.axis_size("sub") == 2
        and bins_local % SECTOR == 0
        and points_local % NLON == 0
        and points_local == lax.axis_size("comp") * LANES
        and lax.axis_size("comp") * bins_local % LANES == 0
    )
    return (two_chip_device if two_chips else per_device)(*arrays)


def solution(mesh):
    placed = (
        P("comp", ("members", "lat", "sub")),
        P(("members", "lat", "sub")),
        P(None, ("members", "lat", "sub")),
        P(),
        P(),
        P("sub", None),
    )
    return jax.shard_map(
        device_step,
        mesh=mesh,
        in_specs=placed,
        out_specs=P("comp", ("members", "lat", "sub")),
        check_vma=False,
    )
```

```python
import functools
import math

import jax
import jax.numpy as jnp
import numpy as np
from jax import lax
from jax.experimental import pallas as pl
from jax.experimental.pallas import tpu as pltpu
from jax.sharding import PartitionSpec as P

NF = 30
ND = 64
NLON = 256
MAXSTEPS = 6
SRC_STEPS = 4


STEP_SIZE = 0.1


def extended(cells, sides, width):
    for axis, dim in sides:
        count = lax.axis_size(axis)
        ends = count - 1
        head = lax.slice_in_dim(cells, 0, width, axis=dim)
        tail = lax.slice_in_dim(cells, cells.shape[dim] - width, cells.shape[dim], axis=dim)
        cells = jnp.concatenate(
            [
                lax.ppermute(tail, axis, [(i, (i + 1) % count) for i in range(ends)]),
                cells,
                lax.ppermute(head, axis, [((i + 1) % count, i) for i in range(ends)]),
            ],
            axis=dim,
        )
    return cells


def bin_tables(global_bins, substeps, courant):
    frequency = global_bins // ND
    direction = global_bins % ND
    chosen = frequency[:, None] == jnp.arange(NF, dtype=jnp.int32)[None, :]
    bin_steps = jnp.sum(jnp.where(chosen, substeps[None, :], 0), axis=1)
    bin_speed = jnp.sum(jnp.where(chosen, courant[None, :], 0.0), axis=1)
    angles = (direction.astype(jnp.float32) + 0.5) * (2.0 * math.pi / ND)
    cosine = jnp.cos(angles)
    sine_dir = jnp.sin(angles)
    return (
        bin_steps,
        bin_speed * jnp.abs(cosine),
        bin_speed * jnp.abs(sine_dir),
        cosine > 0,
        sine_dir > 0,
    )


def offset_codes(neighbours, sea_float, points_local):
    position = lax.axis_index(("lat", "sub")) * points_local + jnp.arange(
        points_local, dtype=jnp.int32
    )
    column = position % NLON
    west_gap = (column - neighbours[0] % NLON) % NLON
    east_gap = (neighbours[1] % NLON - column) % NLON

    def vertical_code(index_row):
        column_move = (index_row % NLON - column + 1) % NLON - 1
        return jnp.where(index_row == position, 2, column_move)

    stacked = jnp.stack(
        [west_gap, east_gap, vertical_code(neighbours[2]), vertical_code(neighbours[3])]
    ).astype(jnp.float32)
    return jnp.concatenate([stacked, sea_float[None, :]], axis=0).reshape(
        5, points_local // NLON, NLON
    )


def column_roll(values, amount):
    return jnp.roll(values, amount, axis=-1)


def vertical_pick(other_rows, code_row, center):
    moved = jnp.where(
        code_row == -1.0,
        column_roll(other_rows, 1),
        jnp.where(code_row == 1.0, column_roll(other_rows, -1), other_rows),
    )
    return jnp.where(code_row == 2.0, center, moved)


def advance(substep, center, below, above, point_codes, tables):
    bin_steps, weight_x, weight_y, from_west, from_south = tables
    west_vals = jnp.where(
        point_codes[0][None] == 1.0, column_roll(center, 1), column_roll(center, 2)
    )
    east_vals = jnp.where(
        point_codes[1][None] == 1.0, column_roll(center, -1), column_roll(center, -2)
    )
    upwind_lon = jnp.where(from_west[:, None, None], west_vals, east_vals)
    south_vals = vertical_pick(below, point_codes[2][None], center)
    north_vals = vertical_pick(above, point_codes[3][None], center)
    upwind_lat = jnp.where(from_south[:, None, None], south_vals, north_vals)
    advanced = point_codes[4][None] * (
        center
        - weight_x[:, None, None] * (center - upwind_lon)
        - weight_y[:, None, None] * (center - upwind_lat)
    )
    return jnp.where((substep < bin_steps)[:, None, None], advanced, center)


def propagate(spec_part, global_bins, substeps, courant, point_codes):
    tables = bin_tables(global_bins, substeps, courant)
    bin_count = spec_part.shape[0]
    points_local = spec_part.shape[1]
    row_count = points_local // NLON
    field_now = spec_part.reshape(bin_count, row_count, NLON)
    for substep in range(MAXSTEPS):
        padded = extended(field_now, ((("lat", "sub"), 1),), 1)
        field_now = advance(substep, field_now, padded[:, :-2], padded[:, 2:], point_codes, tables)
    return field_now.reshape(bin_count, points_local)


def per_device(spectrum, sea_mask, neighbours, substeps, courant, source_operator):
    comp_index = lax.axis_index("comp")
    bins_local = spectrum.shape[0]
    points_local = spectrum.shape[1]
    sea_float = sea_mask.astype(jnp.float32)
    point_codes = offset_codes(neighbours, sea_float, points_local)
    field_start = sea_float[None, :] * spectrum
    first_bin = comp_index * bins_local
    held_bins = first_bin + jnp.arange(bins_local, dtype=jnp.int32)
    propagated = propagate(field_start, held_bins, substeps, courant, point_codes)
    outgoing = propagated.astype(jnp.bfloat16)
    owned_cols = lax.all_to_all(outgoing, "comp", split_axis=1, concat_axis=0, tiled=True)
    whole_operator = lax.all_gather(source_operator, "sub", axis=0, tiled=True)
    point_rows = owned_cols.T
    start_state = point_rows.astype(jnp.float32)
    state_now = start_state
    full_rows = point_rows
    for source_step in range(SRC_STEPS):
        driving = lax.dot_general(
            full_rows, whole_operator, (((1,), (1,)), ((), ())), preferred_element_type=jnp.float32
        )
        state_now = state_now + STEP_SIZE * state_now * driving
        if source_step + 1 < SRC_STEPS:
            full_rows = state_now.astype(jnp.bfloat16)
    returned = (state_now - start_state).astype(jnp.bfloat16).T
    home_bins = lax.all_to_all(returned, "comp", split_axis=0, concat_axis=1, tiled=True)
    return sea_float[None, :] * (propagated + home_bins.astype(jnp.float32))


LANES = 128
TILE = 8
QUAD = 16
SECTOR = 32
CODE_SCALE = 32767.5
GRANT = pltpu.CompilerParams(vmem_limit_bytes=16 << 20)


def lane_pick(values, index):
    return jnp.take_along_axis(values, index, axis=1, mode="promise_in_bounds")


def split_columns(first, second):
    lane = lax.broadcasted_iota(jnp.int32, first.shape, 1)
    even, low = 2 * lane % LANES, lane < LANES // 2
    return (
        jnp.where(low, lane_pick(first, even), lane_pick(second, even)),
        jnp.where(low, lane_pick(first, even + 1), lane_pick(second, even + 1)),
    )


def join_columns(even, odd):
    lane = lax.broadcasted_iota(jnp.int32, even.shape, 1)
    index, is_even = lane // 2, lane % 2 == 0
    upper = index + LANES // 2
    return (
        jnp.where(is_even, lane_pick(even, index), lane_pick(odd, index)),
        jnp.where(is_even, lane_pick(even, upper), lane_pick(odd, upper)),
    )


def encode(values):
    return ((values * CODE_SCALE + 0.5).astype(jnp.int32) - 32768).astype(jnp.int16)


def decode(values):
    return (values.astype(jnp.int32) + 32768).astype(jnp.float32) * (1.0 / CODE_SCALE)


def device_place(bins_local):
    lat, sub = lax.axis_index("lat"), lax.axis_index("sub")
    first_group = lax.axis_index("comp") * (bins_local // SECTOR)
    return lat, sub, (first_group + lat) % 2, first_group


def pack_kernel(sizes, spectrum, neighbours, sea_mask, mine, to_pair, to_near, to_far):
    bins_local, half_bins, rows_local = sizes
    _, sub, parity, _ = device_place(bins_local)
    sectors = half_bins // (2 * SECTOR)
    for row in range(rows_local):
        halves = [slice(row * NLON + h * LANES, row * NLON + (h + 1) * LANES) for h in range(2)]
        sea = [sea_mask[0:1, at].astype(jnp.float32) for at in halves]
        moves = []
        for h, at in enumerate(halves):
            lane = lax.broadcasted_iota(jnp.int32, (4, LANES), 1) + h * LANES
            move = (neighbours[:, at] - lane + NLON // 2) % NLON - NLON // 2
            moves.append(jnp.concatenate([move.astype(jnp.float32), sea[h], jnp.zeros((3, LANES))], axis=0))
        codes = split_columns(*moves)
        for h, at in enumerate(halves):
            mine[half_bins : half_bins + TILE, at] = codes[h]
            to_pair[half_bins : half_bins + TILE, at] = codes[h]
            coded = codes[h].astype(jnp.int32).astype(jnp.int16)
            to_near[half_bins // 2 : half_bins // 2 + TILE, at] = coded
            to_far[half_bins // 2 : half_bins // 2 + TILE, at] = coded
    sea_rows = [
        jnp.broadcast_to(sea_mask[0:1, j * LANES : (j + 1) * LANES].astype(jnp.float32), (SECTOR, LANES))
        for j in range(2 * rows_local)
    ]

    for other in range(2):
        base = (sub + other) % 2 * half_bins
        whole, sent = (to_pair, to_far) if other else (mine, to_near)
        for k in range(sectors):
            for rest in range(2):
                group = (2 * k + (parity + rest) % 2) * SECTOR
                source = pl.ds(pl.multiple_of(jnp.minimum(base + group, bins_local - SECTOR), SECTOR), SECTOR)
                target = pl.ds(pl.multiple_of(group, SECTOR), SECTOR)
                for row in range(rows_local):
                    pair = [
                        spectrum[source, (2 * row + h) * LANES : (2 * row + h + 1) * LANES] * sea_rows[2 * row + h]
                        for h in range(2)
                    ]
                    for h, block in enumerate(split_columns(*pair)):
                        at = slice((2 * row + h) * LANES, (2 * row + h + 1) * LANES)
                        whole[target, at] = block
                        if not rest:
                            sent[k * SECTOR : (k + 1) * SECTOR, at] = encode(block)


def pack(sizes, spectrum, neighbours, sea_mask):
    bins_local, half_bins, rows_local = sizes
    points = rows_local * NLON
    vmem = pl.BlockSpec(memory_space=pltpu.VMEM)
    return pl.pallas_call(
        functools.partial(pack_kernel, sizes),
        name="pack",
        compiler_params=GRANT,
        in_specs=[vmem, vmem, vmem],
        out_specs=[vmem] * 4,
        out_shape=[pltpu.VMEM((half_bins + TILE, points), jnp.float32)] * 2
        + [pltpu.VMEM((half_bins // 2 + TILE, points), jnp.int16)] * 2,
    )(*map(off_chip, (spectrum, neighbours, sea_mask)))


def stencil_kernel(sizes, *refs):
    bins_local, half_bins, rows_local, dependent = sizes
    if dependent:
        steps_ref, courant_ref, trig, mine, pair, near, far, free_start, start_out, field_out, tab = refs
    else:
        steps_ref, courant_ref, trig, mine, pair, start_out, field_out, tab = refs
    lat, sub, parity, first_group = device_place(bins_local)
    parity = (parity + int(dependent)) % 2
    first_group = first_group + sub * (half_bins // SECTOR)
    chip_rows = 2 * rows_local
    halo = chip_rows if dependent else 0
    sent_first = 0
    if dependent:
        sent_first = half_bins // 2
        for block in range(start_out.shape[0]):
            start_out[block, :sent_first, :] = free_start[block]
    north = lat == (0 if dependent else 1)
    flip = north.astype(jnp.int32)

    def where_is(v):
        core = (v // rows_local + flip) % 2
        local = v % rows_local
        local = local + flip * (rows_local - 1 - 2 * local)
        return core, local, core == sub

    def lanes_of(local, half):
        return pl.ds(pl.multiple_of(local * NLON + half * LANES, LANES), LANES)

    for u in range(halo + chip_rows):
        core, local, here = where_is(u % chip_rows)
        for half in range(2):
            at = lanes_of(local, half)
            if u < halo:
                rows = slice(half_bins // 2, half_bins // 2 + TILE)
                codes = jnp.where(here, near[rows, at].astype(jnp.int32), far[rows, at].astype(jnp.int32))
                codes = codes.astype(jnp.float32)
            else:
                rows = slice(half_bins, half_bins + TILE)
                codes = jnp.where(here, mine[rows, at], pair[rows, at])
            wide = lambda i: jnp.broadcast_to(codes[i : i + 1], (TILE, LANES))
            tab[u, half, 0] = wide(0)
            tab[u, half, 1] = wide(1)
            tab[u, half, 2] = jnp.where(north, wide(3), wide(2))
            tab[u, half, 3] = wide(4)

    def tiles(value):
        return value.reshape(QUAD // TILE, TILE, LANES)

    def turn(value, amount):
        return pltpu.roll(value.reshape(QUAD, LANES), amount % LANES, 1).reshape(QUAD // TILE, TILE, LANES)

    def block(sector, east):
        group = 2 * sector + parity
        band = jnp.minimum((first_group + group) // 2, courant_ref.shape[0] - 1)
        speed, count = courant_ref[band], steps_ref[band]
        side = (flip + east) % 2
        trig_row = pl.ds(pl.multiple_of(SECTOR * flip + QUAD * side, QUAD), QUAD)
        part_row = pl.ds(pl.multiple_of(group * SECTOR + side * QUAD, QUAD), QUAD)
        sent_row = pl.ds(pl.multiple_of(sector * SECTOR + side * QUAD, QUAD), QUAD)
        start_row = pl.ds(pl.multiple_of(sent_first + sector * SECTOR + side * QUAD, QUAD), QUAD)
        trig_x, trig_y = tiles(trig[0, trig_row, :]), tiles(trig[1, trig_row, :])
        field = []
        for u in range(halo + chip_rows):
            core, local, here = where_is(u % chip_rows)
            both = []
            for half in range(2):
                at = lanes_of(local, half)
                if u < halo:
                    value = jnp.where(
                        here, near[sent_row, at].astype(jnp.int32), far[sent_row, at].astype(jnp.int32)
                    )
                    value = (value + 32768).astype(jnp.float32) * (1.0 / CODE_SCALE)
                else:
                    value = jnp.where(here, mine[part_row, at], pair[part_row, at])
                both.append(tiles(value))
            field.append(both)
        for t in range(MAXSTEPS):
            now = jnp.where(t < count, speed, 0.0)
            weight_x, weight_y = now * trig_x, now * trig_y
            keep = 1.0 - weight_x - weight_y
            lowest = max(0, halo - (MAXSTEPS - 1 - t))
            for u in reversed(range(lowest, halo + chip_rows)):
                (even, odd), (even_b, odd_b) = field[u], field[max(u - 1, 0)]
                moved = []
                for half in range(2):
                    move_x, move_y = tab[u, half, east], tab[u, half, 2]
                    near_x = (move_x == (1.0 if east else -1.0))[None]
                    back, ahead = (move_y == -1.0)[None], (move_y == 1.0)[None]
                    if half == 0:
                        one = odd if east else turn(odd, 1)
                        two = turn(even, -1 if east else 1)
                        centre, same = even, even_b
                        minus, plus = turn(odd_b, 1), odd_b
                    else:
                        one = turn(even, -1) if east else even
                        two = turn(odd, -1 if east else 1)
                        centre, same = odd, odd_b
                        minus, plus = even_b, turn(even_b, -1)
                    upwind_x = jnp.where(near_x, one, two)
                    upwind_y = jnp.where(back, minus, jnp.where(ahead, plus, same))
                    value = keep * centre + weight_x * upwind_x + weight_y * upwind_y
                    moved.append(tab[u, half, 3][None] * value)
                field[u] = moved
        for v in range(chip_rows):
            core, local, here = where_is(v)
            for half in range(2):
                value = field[halo + v][half].reshape(QUAD, LANES)
                start_out[(local * 2 + half) * 2 + core, start_row, :] = value.astype(jnp.bfloat16)
                field_out[1 - here.astype(jnp.int32), sent_row, lanes_of(local, half)] = value

    def both_sides(sector, carry):
        block(sector, 0)
        block(sector, 1)
        return carry

    lax.fori_loop(0, half_bins // (2 * SECTOR), both_sides, 0)


def stencil(sizes, substeps, courant, trig, *fields):
    bins_local, half_bins, rows_local, dependent = sizes
    blocks = 4 * rows_local
    rows = (4 if dependent else 2) * rows_local
    smem = pl.BlockSpec(memory_space=pltpu.SMEM)
    vmem = pl.BlockSpec(memory_space=pltpu.VMEM)
    cells = half_bins // 2 * rows_local * 2 * NLON
    start_bins = half_bins if dependent else half_bins // 2
    out_shape = [
        pltpu.VMEM((blocks, start_bins, LANES), jnp.bfloat16),
        pltpu.VMEM((2, half_bins // 2, rows_local * NLON), jnp.float32),
    ]
    scratch = [pltpu.VMEM((rows, 2, 4, TILE, LANES), jnp.float32)]
    return pl.pallas_call(
        functools.partial(stencil_kernel, sizes),
        name="stencil_dependent" if dependent else "stencil_free",
        compiler_params=GRANT,
        in_specs=[smem] * 2 + [vmem] * (1 + len(fields)),
        out_specs=[vmem] * len(out_shape),
        out_shape=out_shape,
        scratch_shapes=scratch,
        cost_estimate=pl.CostEstimate(flops=cells * MAXSTEPS * 100, bytes_accessed=cells * 16, transcendentals=0),
    )(*map(off_chip, (substeps, courant, trig)), *map(on_chip, fields))


def integrate_kernel(sizes, arrived, own_w, other_w, *refs):
    bins_local, half_bins, comps = sizes
    outs, (held_w, state, driver, sem) = refs[:comps], refs[comps:]
    comp, lat, sub = (lax.axis_index(name) for name in ("comp", "lat", "sub"))
    total = comps * bins_local
    stretch = total // 2
    pieces = 2
    piece = stretch // pieces
    copies = []
    for other, source in enumerate((own_w, other_w)):
        for p in range(pieces):
            copy = pltpu.make_async_copy(
                source.at[pl.ds(p * piece, piece)], held_w.at[other, pl.ds(p * piece, piece)], sem.at[other, p]
            )
            copy.start()
            copies.append(copy)
    sectors = half_bins // (2 * SECTOR)
    groups = bins_local // SECTOR
    for c in range(comps):
        first = (c * groups) % 2
        for s in range(2):
            for k in range(sectors):
                for dep in range(2):
                    parity = (first + lat + dep) % 2
                    row = c * bins_local + s * half_bins + (2 * k + parity) * SECTOR
                    row = pl.ds(pl.multiple_of(row, SECTOR), SECTOR)
                    block = arrived[2 * c + s, (sectors * dep + k) * SECTOR : (sectors * dep + k + 1) * SECTOR, :]
                    driver[0, row, :] = block
                    state[row, :] = block.astype(jnp.float32)
    for step in range(SRC_STEPS):
        read = 0 if step == 0 else 1 + step % 2
        write = 1 + (step + 1) % 2
        parts = pieces if step == 0 else 1
        rows = stretch // parts
        for other in range(2):
            for p in range(parts):
                if step == 0:
                    copies[other * pieces + p].wait()
                at = pl.ds(pl.multiple_of((sub + other) % 2 * stretch + p * rows, SECTOR), rows)
                drive = jnp.dot(
                    held_w[other, p * rows : (p + 1) * rows, :],
                    driver[read, :total, :],
                    preferred_element_type=jnp.float32,
                )
                value = state[at, :]
                value = value + STEP_SIZE * value * drive
                if step + 1 < SRC_STEPS:
                    state[at, :] = value
                    driver[write, at, :] = value.astype(jnp.bfloat16)
                else:
                    driver[write, at, :] = (value - driver[0, at, :].astype(jnp.float32)).astype(jnp.bfloat16)
    for k in range(comps):
        at = pl.ds(pl.multiple_of((comp + k) % comps * bins_local, SECTOR), bins_local)
        outs[k][...] = driver[write, at, :]


def integrate(sizes, arrived, own_w, other_w):
    bins_local, half_bins, comps = sizes
    total = comps * bins_local
    vmem = pl.BlockSpec(memory_space=pltpu.VMEM)
    return pl.pallas_call(
        functools.partial(integrate_kernel, sizes),
        name="integrate",
        compiler_params=GRANT,
        in_specs=[vmem] + [pl.BlockSpec(memory_space=pl.ANY)] * 2,
        out_specs=[vmem] * comps,
        out_shape=[pltpu.VMEM((bins_local, LANES), jnp.bfloat16)] * comps,
        scratch_shapes=[
            pltpu.VMEM((2,) + own_w.shape, jnp.bfloat16),
            pltpu.VMEM((total + SECTOR, LANES), jnp.float32),
            pltpu.VMEM((3, total + SECTOR, LANES), jnp.bfloat16),
            pltpu.SemaphoreType.DMA((2, 2)),
        ],
        cost_estimate=pl.CostEstimate(
            flops=2 * SRC_STEPS * total * total * LANES, bytes_accessed=2 * total * total, transcendentals=0
        ),
    )(on_chip(arrived), off_chip(own_w), off_chip(other_w))


def finish_kernel(sizes, *refs):
    bins_local, half_bins = sizes
    mine_free, mine_dep, got_free, got_dep, sea_mask = refs[:5]
    out, whole, raised, sem = refs[-4:]
    steps_up = refs[5:-4]
    comp = lax.axis_index("comp")
    for k, increments in enumerate(steps_up):
        raised[(comp + len(steps_up) - k) % len(steps_up)] = increments[...]
    _, sub, parity, _ = device_place(bins_local)
    tiles = whole.shape[1] // LANES
    sea = [
        jnp.broadcast_to(sea_mask[0:1, j * LANES : (j + 1) * LANES].astype(jnp.float32), (SECTOR, LANES))
        for j in range(tiles)
    ]
    sectors = half_bins // (2 * SECTOR)

    def rows_out(group, semaphore):
        at = pl.ds(pl.multiple_of(group, SECTOR), SECTOR)
        return pltpu.make_async_copy(whole.at[at], out.at[at], semaphore)

    for other, pair in enumerate(((mine_free, mine_dep), (got_free, got_dep))):
        base = (sub + other) % 2 * half_bins
        for k in range(sectors):
            for dep, source in enumerate(pair):
                row = base + (2 * k + (parity + dep) % 2) * SECTOR
                rows = pl.ds(pl.multiple_of(row, SECTOR), SECTOR)
                added = pl.ds(pl.multiple_of(jnp.minimum(row, bins_local - SECTOR), SECTOR), SECTOR)
                for j in range(0, tiles, 2):
                    halves = [
                        source[0, k * SECTOR : (k + 1) * SECTOR, i * LANES : (i + 1) * LANES]
                        + raised[i, added, :].astype(jnp.float32)
                        for i in (j, j + 1)
                    ]
                    for i, value in enumerate(join_columns(*halves)):
                        whole[rows, (j + i) * LANES : (j + i + 1) * LANES] = sea[j + i] * value
            for rest in range(2):
                group = base + (2 * k + rest) * SECTOR

                @pl.when(group < bins_local)
                def _():
                    rows_out(group, sem.at[other, k, rest]).start()

    for other in range(2):
        for k in range(sectors):
            for rest in range(2):
                group = (sub + other) % 2 * half_bins + (2 * k + rest) * SECTOR

                @pl.when(group < bins_local)
                def _():
                    rows_out(group, sem.at[other, k, rest]).wait()


def finish(sizes, fields, sea_mask, steps_up):
    bins_local, half_bins = sizes
    points = sea_mask.shape[1]
    vmem = pl.BlockSpec(memory_space=pltpu.VMEM)
    comps = len(steps_up)
    return pl.pallas_call(
        functools.partial(finish_kernel, sizes),
        name="finish",
        compiler_params=GRANT,
        in_specs=[vmem] * (5 + comps),
        out_specs=pl.BlockSpec(memory_space=pl.ANY),
        out_shape=jax.ShapeDtypeStruct((bins_local, points), jnp.float32),
        scratch_shapes=[
            pltpu.VMEM((2 * half_bins, points), jnp.float32),
            pltpu.VMEM((comps, bins_local, LANES), jnp.bfloat16),
            pltpu.SemaphoreType.DMA((2, half_bins // (2 * SECTOR), 2)),
        ],
    )(*map(on_chip, fields), sea_mask, *map(on_chip, steps_up))


def on_chip(values):
    return pltpu.with_memory_space_constraint(values, pltpu.VMEM)


def off_chip(values):
    return pltpu.with_memory_space_constraint(values, pltpu.HBM)


def swap(values, bits):
    count = lax.axis_size("lat") * lax.axis_size("sub")
    return lax.ppermute(values, ("lat", "sub"), [(i, i ^ bits) for i in range(count)])


def two_chip_device(spectrum, sea_mask, neighbours, substeps, courant, source_operator):
    comps = lax.axis_size("comp")
    bins_local, points_local = spectrum.shape
    rows_local = points_local // NLON
    half_bins = (bins_local // SECTOR + 3) // 4 * 2 * SECTOR
    sea_mask = sea_mask[None, :]
    angles = (np.arange(ND, dtype=np.float32) + np.float32(0.5)) * np.float32(2.0 * math.pi / ND)
    trig = np.abs(np.stack([np.cos(angles), np.sin(angles)])).astype(np.float32)
    trig = jnp.asarray(np.repeat(trig[:, :, None], LANES, axis=2))

    mine, to_pair, to_near, to_far = pack((bins_local, half_bins, rows_local), spectrum, neighbours, sea_mask)
    pair = swap(to_pair, 1)
    near = swap(to_near, 2)
    far = swap(to_far, 3)
    free_start, free_field = stencil((bins_local, half_bins, rows_local, False), substeps, courant, trig, mine, pair)
    near, far, source_operator, _ = lax.optimization_barrier((near, far, source_operator, free_start))
    other_w = swap(source_operator, 1)
    start, dep_field = stencil(
        (bins_local, half_bins, rows_local, True),
        substeps,
        courant,
        trig,
        mine,
        pair,
        near,
        far,
        free_start,
    )
    arrived = lax.all_to_all(start, ("comp", "sub"), split_axis=0, concat_axis=0, tiled=True)
    got_free = swap(free_field[1:], 1)
    got_dep = swap(dep_field[1:], 1)
    raised = integrate((bins_local, half_bins, comps), arrived, source_operator, other_w)
    home = [raised[0]] + [
        lax.ppermute(raised[k], "comp", [(i, (i + k) % comps) for i in range(comps)]) for k in range(1, comps)
    ]
    return finish((bins_local, half_bins), (free_field, dep_field, got_free, got_dep), sea_mask, home)


def device_step(*arrays):
    bins_local, points_local = arrays[0].shape
    two_chips = (
        lax.axis_size("lat") == 2
        and lax.axis_size("sub") == 2
        and bins_local % SECTOR == 0
        and points_local % NLON == 0
        and points_local == lax.axis_size("comp") * LANES
        and lax.axis_size("comp") * bins_local % LANES == 0
    )
    return (two_chip_device if two_chips else per_device)(*arrays)


def solution(mesh):
    placed = (
        P("comp", ("members", "lat", "sub")),
        P(("members", "lat", "sub")),
        P(None, ("members", "lat", "sub")),
        P(),
        P(),
        P("sub", None),
    )
    return jax.shard_map(
        device_step,
        mesh=mesh,
        in_specs=placed,
        out_specs=P("comp", ("members", "lat", "sub")),
        check_vma=False,
    )
```

```python
import functools
import math

import jax
import jax.numpy as jnp
import numpy as np
from jax import lax
from jax.experimental import pallas as pl
from jax.experimental.pallas import tpu as pltpu
from jax.sharding import PartitionSpec as P


NF = 30
ND = 64
NLON = 256
MAXSTEPS = 6
SRC_STEPS = 4


STEP_SIZE = 0.1


def extended(cells, sides, width):
    for axis, dim in sides:
        count = lax.axis_size(axis)
        ends = count - 1
        head = lax.slice_in_dim(cells, 0, width, axis=dim)
        tail = lax.slice_in_dim(cells, cells.shape[dim] - width, cells.shape[dim], axis=dim)
        cells = jnp.concatenate(
            [
                lax.ppermute(tail, axis, [(i, (i + 1) % count) for i in range(ends)]),
                cells,
                lax.ppermute(head, axis, [((i + 1) % count, i) for i in range(ends)]),
            ],
            axis=dim,
        )
    return cells


def bin_tables(global_bins, substeps, courant):
    frequency = global_bins // ND
    direction = global_bins % ND
    chosen = frequency[:, None] == jnp.arange(NF, dtype=jnp.int32)[None, :]
    bin_steps = jnp.sum(jnp.where(chosen, substeps[None, :], 0), axis=1)
    bin_speed = jnp.sum(jnp.where(chosen, courant[None, :], 0.0), axis=1)
    angles = (direction.astype(jnp.float32) + 0.5) * (2.0 * math.pi / ND)
    cosine = jnp.cos(angles)
    sine_dir = jnp.sin(angles)
    return (
        bin_steps,
        bin_speed * jnp.abs(cosine),
        bin_speed * jnp.abs(sine_dir),
        cosine > 0,
        sine_dir > 0,
    )


def offset_codes(neighbours, sea_float, points_local):
    position = lax.axis_index(("lat", "sub")) * points_local + jnp.arange(
        points_local, dtype=jnp.int32
    )
    column = position % NLON
    west_gap = (column - neighbours[0] % NLON) % NLON
    east_gap = (neighbours[1] % NLON - column) % NLON

    def vertical_code(index_row):
        column_move = (index_row % NLON - column + 1) % NLON - 1
        return jnp.where(index_row == position, 2, column_move)

    stacked = jnp.stack(
        [west_gap, east_gap, vertical_code(neighbours[2]), vertical_code(neighbours[3])]
    ).astype(jnp.float32)
    return jnp.concatenate([stacked, sea_float[None, :]], axis=0).reshape(
        5, points_local // NLON, NLON
    )


def column_roll(values, amount):
    return jnp.roll(values, amount, axis=-1)


def vertical_pick(other_rows, code_row, center):
    moved = jnp.where(
        code_row == -1.0,
        column_roll(other_rows, 1),
        jnp.where(code_row == 1.0, column_roll(other_rows, -1), other_rows),
    )
    return jnp.where(code_row == 2.0, center, moved)


def advance(substep, center, below, above, point_codes, tables):
    bin_steps, weight_x, weight_y, from_west, from_south = tables
    west_vals = jnp.where(
        point_codes[0][None] == 1.0, column_roll(center, 1), column_roll(center, 2)
    )
    east_vals = jnp.where(
        point_codes[1][None] == 1.0, column_roll(center, -1), column_roll(center, -2)
    )
    upwind_lon = jnp.where(from_west[:, None, None], west_vals, east_vals)
    south_vals = vertical_pick(below, point_codes[2][None], center)
    north_vals = vertical_pick(above, point_codes[3][None], center)
    upwind_lat = jnp.where(from_south[:, None, None], south_vals, north_vals)
    advanced = point_codes[4][None] * (
        center
        - weight_x[:, None, None] * (center - upwind_lon)
        - weight_y[:, None, None] * (center - upwind_lat)
    )
    return jnp.where((substep < bin_steps)[:, None, None], advanced, center)


def propagate(spec_part, global_bins, substeps, courant, point_codes):
    tables = bin_tables(global_bins, substeps, courant)
    bin_count = spec_part.shape[0]
    points_local = spec_part.shape[1]
    row_count = points_local // NLON
    field_now = spec_part.reshape(bin_count, row_count, NLON)
    for substep in range(MAXSTEPS):
        padded = extended(field_now, ((("lat", "sub"), 1),), 1)
        field_now = advance(substep, field_now, padded[:, :-2], padded[:, 2:], point_codes, tables)
    return field_now.reshape(bin_count, points_local)


def per_device(spectrum, sea_mask, neighbours, substeps, courant, source_operator):
    comp_index = lax.axis_index("comp")
    bins_local = spectrum.shape[0]
    points_local = spectrum.shape[1]
    sea_float = sea_mask.astype(jnp.float32)
    point_codes = offset_codes(neighbours, sea_float, points_local)
    field_start = sea_float[None, :] * spectrum
    first_bin = comp_index * bins_local
    held_bins = first_bin + jnp.arange(bins_local, dtype=jnp.int32)
    propagated = propagate(field_start, held_bins, substeps, courant, point_codes)
    outgoing = propagated.astype(jnp.bfloat16)
    owned_cols = lax.all_to_all(outgoing, "comp", split_axis=1, concat_axis=0, tiled=True)
    whole_operator = lax.all_gather(source_operator, "sub", axis=0, tiled=True)
    point_rows = owned_cols.T
    start_state = point_rows.astype(jnp.float32)
    state_now = start_state
    full_rows = point_rows
    for source_step in range(SRC_STEPS):
        driving = lax.dot_general(
            full_rows, whole_operator, (((1,), (1,)), ((), ())), preferred_element_type=jnp.float32
        )
        state_now = state_now + STEP_SIZE * state_now * driving
        if source_step + 1 < SRC_STEPS:
            full_rows = state_now.astype(jnp.bfloat16)
    returned = (state_now - start_state).astype(jnp.bfloat16).T
    home_bins = lax.all_to_all(returned, "comp", split_axis=0, concat_axis=1, tiled=True)
    return sea_float[None, :] * (propagated + home_bins.astype(jnp.float32))


LANES = 128
TILE = 8
QUAD = 16
SECTOR = 32
CODE_SCALE = 32767.5
GRANT = pltpu.CompilerParams(vmem_limit_bytes=16 << 20)


def lane_pick(values, index):
    return jnp.take_along_axis(values, index, axis=1, mode="promise_in_bounds")


def split_columns(first, second):
    lane = lax.broadcasted_iota(jnp.int32, first.shape, 1)
    even, low = 2 * lane % LANES, lane < LANES // 2
    return (
        jnp.where(low, lane_pick(first, even), lane_pick(second, even)),
        jnp.where(low, lane_pick(first, even + 1), lane_pick(second, even + 1)),
    )


def join_columns(even, odd):
    lane = lax.broadcasted_iota(jnp.int32, even.shape, 1)
    index, is_even = lane // 2, lane % 2 == 0
    upper = index + LANES // 2
    return (
        jnp.where(is_even, lane_pick(even, index), lane_pick(odd, index)),
        jnp.where(is_even, lane_pick(even, upper), lane_pick(odd, upper)),
    )


def encode(values):
    return ((values * CODE_SCALE + 0.5).astype(jnp.int32) - 32768).astype(jnp.int16)


def device_place(bins_local):
    lat, sub = lax.axis_index("lat"), lax.axis_index("sub")
    first_group = lax.axis_index("comp") * (bins_local // SECTOR)
    return lat, sub, (first_group + lat) % 2, first_group


def pack_kernel(sizes, spectrum, neighbours, sea_mask, mine, to_pair, to_near, to_far):
    bins_local, half_bins, rows_local = sizes
    _, sub, parity, _ = device_place(bins_local)
    sectors = half_bins // (2 * SECTOR)
    for row in range(rows_local):
        halves = [slice(row * NLON + h * LANES, row * NLON + (h + 1) * LANES) for h in range(2)]
        sea = [sea_mask[0:1, at].astype(jnp.float32) for at in halves]
        moves = []
        for h, at in enumerate(halves):
            lane = lax.broadcasted_iota(jnp.int32, (4, LANES), 1) + h * LANES
            move = (neighbours[:, at] - lane + NLON // 2) % NLON - NLON // 2
            moves.append(jnp.concatenate([move.astype(jnp.float32), sea[h], jnp.zeros((3, LANES))], axis=0))
        codes = split_columns(*moves)
        for h, at in enumerate(halves):
            mine[half_bins : half_bins + TILE, at] = codes[h]
            to_pair[half_bins : half_bins + TILE, at] = codes[h]
            coded = codes[h].astype(jnp.int32).astype(jnp.int16)
            to_near[half_bins // 2 : half_bins // 2 + TILE, at] = coded
            to_far[half_bins // 2 : half_bins // 2 + TILE, at] = coded
    sea_rows = [
        jnp.broadcast_to(sea_mask[0:1, j * LANES : (j + 1) * LANES].astype(jnp.float32), (SECTOR, LANES))
        for j in range(2 * rows_local)
    ]

    for other in range(2):
        base = (sub + other) % 2 * half_bins
        whole, sent = (to_pair, to_far) if other else (mine, to_near)
        for k in range(sectors):
            for rest in range(2):
                group = (2 * k + (parity + rest) % 2) * SECTOR
                source = pl.ds(pl.multiple_of(jnp.minimum(base + group, bins_local - SECTOR), SECTOR), SECTOR)
                target = pl.ds(pl.multiple_of(group, SECTOR), SECTOR)
                for row in range(rows_local):
                    pair = [
                        spectrum[source, (2 * row + h) * LANES : (2 * row + h + 1) * LANES] * sea_rows[2 * row + h]
                        for h in range(2)
                    ]
                    for h, block in enumerate(split_columns(*pair)):
                        at = slice((2 * row + h) * LANES, (2 * row + h + 1) * LANES)
                        whole[target, at] = block
                        if not rest:
                            sent[k * SECTOR : (k + 1) * SECTOR, at] = encode(block)


def pack(sizes, spectrum, neighbours, sea_mask):
    _, half_bins, rows_local = sizes
    points = rows_local * NLON
    vmem = pl.BlockSpec(memory_space=pltpu.VMEM)
    return pl.pallas_call(
        functools.partial(pack_kernel, sizes),
        name="pack",
        compiler_params=GRANT,
        in_specs=[vmem, vmem, vmem],
        out_specs=[vmem] * 4,
        out_shape=[pltpu.VMEM((half_bins + TILE, points), jnp.float32)] * 2
        + [pltpu.VMEM((half_bins // 2 + TILE, points), jnp.int16)] * 2,
    )(*map(off_chip, (spectrum, neighbours, sea_mask)))


def stencil_kernel(sizes, *refs):
    bins_local, half_bins, rows_local, dependent = sizes
    if dependent:
        steps_ref, courant_ref, trig, mine, pair, near, far, free_start, other_w, own_w = refs[:10]
        start_out, field_out, whole_w, tab, sem = refs[10:]
    else:
        steps_ref, courant_ref, trig, mine, pair, start_out, field_out, tab = refs
    lat, sub, parity, first_group = device_place(bins_local)
    parity = (parity + int(dependent)) % 2
    first_group = first_group + sub * (half_bins // SECTOR)
    chip_rows = 2 * rows_local
    halo = chip_rows if dependent else 0
    copies = []
    sent_first = half_bins // 2 if dependent else 0
    if dependent:
        for b in range(start_out.shape[0]):
            start_out[b, :sent_first, :] = free_start[b]
        for other, source in enumerate((own_w, other_w)):
            at = pl.ds(pl.multiple_of((sub + other) % 2 * source.shape[0], 64), source.shape[0])
            copies.append(pltpu.make_async_copy(source, whole_w.at[at], sem.at[other]))
            copies[other].start()
    north = lat == (0 if dependent else 1)
    flip = north.astype(jnp.int32)

    def where_is(v):
        core = (v // rows_local + flip) % 2
        local = v % rows_local
        local = local + flip * (rows_local - 1 - 2 * local)
        return core, local, core == sub

    def lanes_of(local, half):
        return pl.ds(pl.multiple_of(local * NLON + half * LANES, LANES), LANES)

    for u in range(halo + chip_rows):
        _, local, here = where_is(u % chip_rows)
        for half in range(2):
            at = lanes_of(local, half)
            if u < halo:
                rows = slice(half_bins // 2, half_bins // 2 + TILE)
                codes = jnp.where(here, near[rows, at].astype(jnp.int32), far[rows, at].astype(jnp.int32))
                codes = codes.astype(jnp.float32)
            else:
                rows = slice(half_bins, half_bins + TILE)
                codes = jnp.where(here, mine[rows, at], pair[rows, at])
            wide = lambda i: jnp.broadcast_to(codes[i : i + 1], (TILE, LANES))
            tab[u, half, 0] = wide(0)
            tab[u, half, 1] = wide(1)
            tab[u, half, 2] = jnp.where(north, wide(3), wide(2))
            tab[u, half, 3] = wide(4)

    def tiles(value):
        return value.reshape(QUAD // TILE, TILE, LANES)

    def turn(value, amount):
        return pltpu.roll(value.reshape(QUAD, LANES), amount % LANES, 1).reshape(QUAD // TILE, TILE, LANES)

    def block(sector, east):
        group = 2 * sector + parity
        band = jnp.minimum((first_group + group) // 2, courant_ref.shape[0] - 1)
        speed, count = courant_ref[band], steps_ref[band]
        side = (flip + east) % 2
        trig_row = pl.ds(pl.multiple_of(SECTOR * flip + QUAD * side, QUAD), QUAD)
        part_row = pl.ds(pl.multiple_of(group * SECTOR + side * QUAD, QUAD), QUAD)
        sent_row = pl.ds(pl.multiple_of(sector * SECTOR + side * QUAD, QUAD), QUAD)
        start_row = pl.ds(pl.multiple_of(sent_first + sector * SECTOR + side * QUAD, QUAD), QUAD)
        trig_x, trig_y = tiles(trig[0, trig_row, :]), tiles(trig[1, trig_row, :])
        field = []
        for u in range(halo + chip_rows):
            core, local, here = where_is(u % chip_rows)
            both = []
            for half in range(2):
                at = lanes_of(local, half)
                if u < halo:
                    value = jnp.where(
                        here, near[sent_row, at].astype(jnp.int32), far[sent_row, at].astype(jnp.int32)
                    )
                    value = (value + 32768).astype(jnp.float32) * (1.0 / CODE_SCALE)
                else:
                    value = jnp.where(here, mine[part_row, at], pair[part_row, at])
                both.append(tiles(value))
            field.append(both)
        for t in range(MAXSTEPS):
            now = jnp.where(t < count, speed, 0.0)
            weight_x, weight_y = now * trig_x, now * trig_y
            keep = 1.0 - weight_x - weight_y
            lowest = max(0, halo - (MAXSTEPS - 1 - t))
            for u in reversed(range(lowest, halo + chip_rows)):
                (even, odd), (even_b, odd_b) = field[u], field[max(u - 1, 0)]
                moved = []
                for half in range(2):
                    move_x, move_y = tab[u, half, east], tab[u, half, 2]
                    near_x = (move_x == (1.0 if east else -1.0))[None]
                    back, ahead = (move_y == -1.0)[None], (move_y == 1.0)[None]
                    if half == 0:
                        one = odd if east else turn(odd, 1)
                        two = turn(even, -1 if east else 1)
                        centre, same = even, even_b
                        minus, plus = turn(odd_b, 1), odd_b
                    else:
                        one = turn(even, -1) if east else even
                        two = turn(odd, -1 if east else 1)
                        centre, same = odd, odd_b
                        minus, plus = even_b, turn(even_b, -1)
                    upwind_x = jnp.where(near_x, one, two)
                    upwind_y = jnp.where(back, minus, jnp.where(ahead, plus, same))
                    value = keep * centre + weight_x * upwind_x + weight_y * upwind_y
                    moved.append(tab[u, half, 3][None] * value)
                field[u] = moved
        for v in range(chip_rows):
            core, local, here = where_is(v)
            for half in range(2):
                value = field[halo + v][half].reshape(QUAD, LANES)
                start_out[(local * 2 + half) * 2 + core, start_row, :] = value.astype(jnp.bfloat16)
                field_out[1 - here.astype(jnp.int32), sent_row, lanes_of(local, half)] = value

    def both_sides(sector, carry):
        block(sector, 0)
        block(sector, 1)
        return carry

    lax.fori_loop(0, half_bins // (2 * SECTOR), both_sides, 0)
    for copy in copies:
        copy.wait()


def stencil(sizes, substeps, courant, trig, *fields, operator=None):
    _, half_bins, rows_local, dependent = sizes
    blocks = 4 * rows_local
    rows = (4 if dependent else 2) * rows_local
    smem = pl.BlockSpec(memory_space=pltpu.SMEM)
    vmem = pl.BlockSpec(memory_space=pltpu.VMEM)
    cells = half_bins // 2 * rows_local * 2 * NLON
    in_specs = [smem] * 2 + [vmem] * (1 + len(fields))
    out_shape = [
        pltpu.VMEM((blocks, half_bins // (1 if dependent else 2), LANES), jnp.bfloat16),
        pltpu.VMEM((2, half_bins // 2, rows_local * NLON), jnp.float32),
    ]
    scratch = [pltpu.VMEM((rows, 2, 4, TILE, LANES), jnp.float32)]
    args = list(map(off_chip, (substeps, courant, trig))) + list(map(on_chip, fields))
    if dependent:
        in_specs.append(pl.BlockSpec(memory_space=pl.ANY))
        args.append(off_chip(operator))
        out_shape.append(pltpu.VMEM((2 * operator.shape[0], operator.shape[1]), jnp.bfloat16))
        scratch.append(pltpu.SemaphoreType.DMA((2,)))
    return pl.pallas_call(
        functools.partial(stencil_kernel, sizes),
        name="stencil_dependent" if dependent else "stencil_free",
        compiler_params=GRANT,
        in_specs=in_specs,
        out_specs=[vmem] * len(out_shape),
        out_shape=out_shape,
        scratch_shapes=scratch,
        cost_estimate=pl.CostEstimate(flops=cells * MAXSTEPS * 100, bytes_accessed=cells * 16, transcendentals=0),
    )(*args)


def integrate_kernel(sizes, arrived, whole_w, *refs):
    bins_local, half_bins, comps = sizes
    outs, (state, driver) = refs[:comps], refs[comps:]
    comp, lat = lax.axis_index("comp"), lax.axis_index("lat")
    total = comps * bins_local
    sectors = half_bins // (2 * SECTOR)
    groups = bins_local // SECTOR
    for c in range(comps):
        first = (c * groups) % 2
        for s in range(2):
            for k in range(sectors):
                for dep in range(2):
                    parity = (first + lat + dep) % 2
                    row = c * bins_local + s * half_bins + (2 * k + parity) * SECTOR
                    row = pl.ds(pl.multiple_of(row, SECTOR), SECTOR)
                    block = arrived[2 * c + s, (sectors * dep + k) * SECTOR : (sectors * dep + k + 1) * SECTOR, :]
                    driver[0, row, :] = block
                    state[row, :] = block.astype(jnp.float32)
    stretch = total // 2
    for step in range(SRC_STEPS):
        read = 0 if step == 0 else 1 + step % 2
        write = 1 + (step + 1) % 2
        for first in range(0, total, stretch):
            at = slice(first, first + stretch)
            drive = jnp.dot(whole_w[at, :], driver[read, :total, :], preferred_element_type=jnp.float32)
            value = state[at, :]
            value = value + STEP_SIZE * value * drive
            if step + 1 < SRC_STEPS:
                state[at, :] = value
                driver[write, at, :] = value.astype(jnp.bfloat16)
            else:
                driver[write, at, :] = (value - driver[0, at, :].astype(jnp.float32)).astype(jnp.bfloat16)
    for k in range(comps):
        at = pl.ds(pl.multiple_of((comp + k) % comps * bins_local, SECTOR), bins_local)
        outs[k][...] = driver[write, at, :]


def integrate(sizes, arrived, whole_w):
    bins_local, _, comps = sizes
    total = comps * bins_local
    vmem = pl.BlockSpec(memory_space=pltpu.VMEM)
    return pl.pallas_call(
        functools.partial(integrate_kernel, sizes),
        name="integrate",
        compiler_params=GRANT,
        in_specs=[vmem] * 2,
        out_specs=[vmem] * comps,
        out_shape=[pltpu.VMEM((bins_local, LANES), jnp.bfloat16)] * comps,
        scratch_shapes=[
            pltpu.VMEM((total + SECTOR, LANES), jnp.float32),
            pltpu.VMEM((3, total + SECTOR, LANES), jnp.bfloat16),
        ],
        cost_estimate=pl.CostEstimate(
            flops=2 * SRC_STEPS * total * total * LANES, bytes_accessed=2 * total * total, transcendentals=0
        ),
    )(on_chip(arrived), on_chip(whole_w))


def finish_kernel(sizes, *refs):
    bins_local, half_bins = sizes
    mine_free, mine_dep, got_free, got_dep, sea_mask = refs[:5]
    out, whole, raised, sem = refs[-4:]
    steps_up = refs[5:-4]
    comp = lax.axis_index("comp")
    for k, increments in enumerate(steps_up):
        raised[(comp + len(steps_up) - k) % len(steps_up)] = increments[...]
    _, sub, parity, _ = device_place(bins_local)
    tiles = whole.shape[1] // LANES
    sea = [
        jnp.broadcast_to(sea_mask[0:1, j * LANES : (j + 1) * LANES].astype(jnp.float32), (SECTOR, LANES))
        for j in range(tiles)
    ]
    sectors = half_bins // (2 * SECTOR)

    def rows_out(group, semaphore):
        at = pl.ds(pl.multiple_of(group, SECTOR), SECTOR)
        return pltpu.make_async_copy(whole.at[at], out.at[at], semaphore)

    for other, pair in enumerate(((mine_free, mine_dep), (got_free, got_dep))):
        base = (sub + other) % 2 * half_bins
        for k in range(sectors):
            for dep, source in enumerate(pair):
                row = base + (2 * k + (parity + dep) % 2) * SECTOR
                rows = pl.ds(pl.multiple_of(row, SECTOR), SECTOR)
                added = pl.ds(pl.multiple_of(jnp.minimum(row, bins_local - SECTOR), SECTOR), SECTOR)
                for j in range(0, tiles, 2):
                    halves = [
                        source[0, k * SECTOR : (k + 1) * SECTOR, i * LANES : (i + 1) * LANES]
                        + raised[i, added, :].astype(jnp.float32)
                        for i in (j, j + 1)
                    ]
                    for i, value in enumerate(join_columns(*halves)):
                        whole[rows, (j + i) * LANES : (j + i + 1) * LANES] = sea[j + i] * value
            for rest in range(2):
                group = base + (2 * k + rest) * SECTOR

                @pl.when(group < bins_local)
                def _():
                    rows_out(group, sem.at[other, k, rest]).start()

    for other in range(2):
        for k in range(sectors):
            for rest in range(2):
                group = (sub + other) % 2 * half_bins + (2 * k + rest) * SECTOR

                @pl.when(group < bins_local)
                def _():
                    rows_out(group, sem.at[other, k, rest]).wait()


def finish(sizes, fields, sea_mask, steps_up):
    bins_local, half_bins = sizes
    points = sea_mask.shape[1]
    vmem = pl.BlockSpec(memory_space=pltpu.VMEM)
    comps = len(steps_up)
    return pl.pallas_call(
        functools.partial(finish_kernel, sizes),
        name="finish",
        compiler_params=GRANT,
        in_specs=[vmem] * (5 + comps),
        out_specs=pl.BlockSpec(memory_space=pl.ANY),
        out_shape=jax.ShapeDtypeStruct((bins_local, points), jnp.float32),
        scratch_shapes=[
            pltpu.VMEM((2 * half_bins, points), jnp.float32),
            pltpu.VMEM((comps, bins_local, LANES), jnp.bfloat16),
            pltpu.SemaphoreType.DMA((2, half_bins // (2 * SECTOR), 2)),
        ],
    )(*map(on_chip, fields), sea_mask, *map(on_chip, steps_up))


def on_chip(values):
    return pltpu.with_memory_space_constraint(values, pltpu.VMEM)


def off_chip(values):
    return pltpu.with_memory_space_constraint(values, pltpu.HBM)


def swap(values, bits):
    count = lax.axis_size("lat") * lax.axis_size("sub")
    return lax.ppermute(values, ("lat", "sub"), [(i, i ^ bits) for i in range(count)])


def two_chip_device(spectrum, sea_mask, neighbours, substeps, courant, source_operator):
    comps = lax.axis_size("comp")
    bins_local, points_local = spectrum.shape
    rows_local = points_local // NLON
    half_bins = (bins_local // SECTOR + 3) // 4 * 2 * SECTOR
    sea_mask = sea_mask[None, :]
    angles = (np.arange(ND, dtype=np.float32) + np.float32(0.5)) * np.float32(2.0 * math.pi / ND)
    trig = np.abs(np.stack([np.cos(angles), np.sin(angles)])).astype(np.float32)
    trig = jnp.asarray(np.repeat(trig[:, :, None], LANES, axis=2))

    mine, to_pair, to_near, to_far = pack((bins_local, half_bins, rows_local), spectrum, neighbours, sea_mask)
    pair = swap(to_pair, 1)
    near = swap(to_near, 2)
    far = swap(to_far, 3)
    source_operator, mine = lax.optimization_barrier((source_operator, mine))
    other_w = swap(source_operator, 1)

    free_start, free_field = stencil((bins_local, half_bins, rows_local, False), substeps, courant, trig, mine, pair)
    near, far, other_w, free_start = lax.optimization_barrier((near, far, other_w, free_start))
    start, dep_field, whole_w = stencil(
        (bins_local, half_bins, rows_local, True),
        substeps,
        courant,
        trig,
        mine,
        pair,
        near,
        far,
        free_start,
        other_w,
        operator=source_operator,
    )
    arrived = lax.all_to_all(start, ("comp", "sub"), split_axis=0, concat_axis=0, tiled=True)
    raised = integrate((bins_local, half_bins, comps), arrived, whole_w)
    free_field, dep_field, raised = lax.optimization_barrier((free_field, dep_field, raised))
    home = [raised[0]] + [
        lax.ppermute(raised[k], "comp", [(i, (i + k) % comps) for i in range(comps)]) for k in range(1, comps)
    ]
    got_free = swap(free_field[1:], 1)
    got_dep = swap(dep_field[1:], 1)
    return finish((bins_local, half_bins), (free_field, dep_field, got_free, got_dep), sea_mask, home)


def device_step(*arrays):
    bins_local, points_local = arrays[0].shape
    two_chips = (
        lax.axis_size("lat") == 2
        and lax.axis_size("sub") == 2
        and bins_local % SECTOR == 0
        and points_local % NLON == 0
        and points_local == lax.axis_size("comp") * LANES
        and lax.axis_size("comp") * bins_local % LANES == 0
    )
    return (two_chip_device if two_chips else per_device)(*arrays)


def solution(mesh):
    placed = (
        P("comp", ("members", "lat", "sub")),
        P(("members", "lat", "sub")),
        P(None, ("members", "lat", "sub")),
        P(),
        P(),
        P("sub", None),
    )
    return jax.shard_map(
        device_step,
        mesh=mesh,
        in_specs=placed,
        out_specs=P("comp", ("members", "lat", "sub")),
        check_vma=False,
    )
```

```python
import functools
import math

import jax
import jax.numpy as jnp
import numpy as np
from jax import lax
from jax.experimental import pallas as pl
from jax.experimental.pallas import tpu as pltpu
from jax.sharding import PartitionSpec as P


NF = 30
ND = 64
NLON = 256
MAXSTEPS = 6
SRC_STEPS = 4


STEP_SIZE = 0.1


def extended(cells, sides, width):
    for axis, dim in sides:
        count = lax.axis_size(axis)
        ends = count - 1
        head = lax.slice_in_dim(cells, 0, width, axis=dim)
        tail = lax.slice_in_dim(cells, cells.shape[dim] - width, cells.shape[dim], axis=dim)
        cells = jnp.concatenate(
            [
                lax.ppermute(tail, axis, [(i, (i + 1) % count) for i in range(ends)]),
                cells,
                lax.ppermute(head, axis, [((i + 1) % count, i) for i in range(ends)]),
            ],
            axis=dim,
        )
    return cells


def bin_tables(global_bins, substeps, courant):
    frequency = global_bins // ND
    direction = global_bins % ND
    chosen = frequency[:, None] == jnp.arange(NF, dtype=jnp.int32)[None, :]
    bin_steps = jnp.sum(jnp.where(chosen, substeps[None, :], 0), axis=1)
    bin_speed = jnp.sum(jnp.where(chosen, courant[None, :], 0.0), axis=1)
    angles = (direction.astype(jnp.float32) + 0.5) * (2.0 * math.pi / ND)
    cosine = jnp.cos(angles)
    sine_dir = jnp.sin(angles)
    return (
        bin_steps,
        bin_speed * jnp.abs(cosine),
        bin_speed * jnp.abs(sine_dir),
        cosine > 0,
        sine_dir > 0,
    )


def offset_codes(neighbours, sea_float, points_local):
    position = lax.axis_index(("lat", "sub")) * points_local + jnp.arange(
        points_local, dtype=jnp.int32
    )
    column = position % NLON
    west_gap = (column - neighbours[0] % NLON) % NLON
    east_gap = (neighbours[1] % NLON - column) % NLON

    def vertical_code(index_row):
        column_move = (index_row % NLON - column + 1) % NLON - 1
        return jnp.where(index_row == position, 2, column_move)

    stacked = jnp.stack(
        [west_gap, east_gap, vertical_code(neighbours[2]), vertical_code(neighbours[3])]
    ).astype(jnp.float32)
    return jnp.concatenate([stacked, sea_float[None, :]], axis=0).reshape(
        5, points_local // NLON, NLON
    )


def column_roll(values, amount):
    return jnp.roll(values, amount, axis=-1)


def vertical_pick(other_rows, code_row, center):
    moved = jnp.where(
        code_row == -1.0,
        column_roll(other_rows, 1),
        jnp.where(code_row == 1.0, column_roll(other_rows, -1), other_rows),
    )
    return jnp.where(code_row == 2.0, center, moved)


def advance(substep, center, below, above, point_codes, tables):
    bin_steps, weight_x, weight_y, from_west, from_south = tables
    west_vals = jnp.where(
        point_codes[0][None] == 1.0, column_roll(center, 1), column_roll(center, 2)
    )
    east_vals = jnp.where(
        point_codes[1][None] == 1.0, column_roll(center, -1), column_roll(center, -2)
    )
    upwind_lon = jnp.where(from_west[:, None, None], west_vals, east_vals)
    south_vals = vertical_pick(below, point_codes[2][None], center)
    north_vals = vertical_pick(above, point_codes[3][None], center)
    upwind_lat = jnp.where(from_south[:, None, None], south_vals, north_vals)
    advanced = point_codes[4][None] * (
        center
        - weight_x[:, None, None] * (center - upwind_lon)
        - weight_y[:, None, None] * (center - upwind_lat)
    )
    return jnp.where((substep < bin_steps)[:, None, None], advanced, center)


def propagate(spec_part, global_bins, substeps, courant, point_codes):
    tables = bin_tables(global_bins, substeps, courant)
    bin_count = spec_part.shape[0]
    points_local = spec_part.shape[1]
    row_count = points_local // NLON
    field_now = spec_part.reshape(bin_count, row_count, NLON)
    for substep in range(MAXSTEPS):
        padded = extended(field_now, ((("lat", "sub"), 1),), 1)
        field_now = advance(substep, field_now, padded[:, :-2], padded[:, 2:], point_codes, tables)
    return field_now.reshape(bin_count, points_local)


def per_device(spectrum, sea_mask, neighbours, substeps, courant, source_operator):
    comp_index = lax.axis_index("comp")
    bins_local = spectrum.shape[0]
    points_local = spectrum.shape[1]
    sea_float = sea_mask.astype(jnp.float32)
    point_codes = offset_codes(neighbours, sea_float, points_local)
    field_start = sea_float[None, :] * spectrum
    first_bin = comp_index * bins_local
    held_bins = first_bin + jnp.arange(bins_local, dtype=jnp.int32)
    propagated = propagate(field_start, held_bins, substeps, courant, point_codes)
    outgoing = propagated.astype(jnp.bfloat16)
    owned_cols = lax.all_to_all(outgoing, "comp", split_axis=1, concat_axis=0, tiled=True)
    whole_operator = lax.all_gather(source_operator, "sub", axis=0, tiled=True)
    point_rows = owned_cols.T
    start_state = point_rows.astype(jnp.float32)
    state_now = start_state
    full_rows = point_rows
    for source_step in range(SRC_STEPS):
        driving = lax.dot_general(
            full_rows, whole_operator, (((1,), (1,)), ((), ())), preferred_element_type=jnp.float32
        )
        state_now = state_now + STEP_SIZE * state_now * driving
        if source_step + 1 < SRC_STEPS:
            full_rows = state_now.astype(jnp.bfloat16)
    returned = (state_now - start_state).astype(jnp.bfloat16).T
    home_bins = lax.all_to_all(returned, "comp", split_axis=0, concat_axis=1, tiled=True)
    return sea_float[None, :] * (propagated + home_bins.astype(jnp.float32))


LANES = 128
TILE = 8
QUAD = 16
SECTOR = 32
CODE_SCALE = 32767.5
GRANT = pltpu.CompilerParams(vmem_limit_bytes=16 << 20)


def lane_pick(values, index):
    return jnp.take_along_axis(values, index, axis=1, mode="promise_in_bounds")


def split_columns(first, second):
    lane = lax.broadcasted_iota(jnp.int32, first.shape, 1)
    even, low = 2 * lane % LANES, lane < LANES // 2
    return (
        jnp.where(low, lane_pick(first, even), lane_pick(second, even)),
        jnp.where(low, lane_pick(first, even + 1), lane_pick(second, even + 1)),
    )


def join_columns(even, odd):
    lane = lax.broadcasted_iota(jnp.int32, even.shape, 1)
    index, is_even = lane // 2, lane % 2 == 0
    upper = index + LANES // 2
    return (
        jnp.where(is_even, lane_pick(even, index), lane_pick(odd, index)),
        jnp.where(is_even, lane_pick(even, upper), lane_pick(odd, upper)),
    )


def encode(values):
    return ((values * CODE_SCALE + 0.5).astype(jnp.int32) - 32768).astype(jnp.int16)


def device_place(bins_local):
    lat, sub = lax.axis_index("lat"), lax.axis_index("sub")
    first_group = lax.axis_index("comp") * (bins_local // SECTOR)
    return lat, sub, (first_group + lat) % 2, first_group


def pack_kernel(sizes, spectrum, neighbours, sea_mask, mine, to_pair, to_near, to_far):
    bins_local, half_bins, rows_local = sizes
    _, sub, parity, _ = device_place(bins_local)
    sectors = half_bins // (2 * SECTOR)
    for row in range(rows_local):
        halves = [slice(row * NLON + h * LANES, row * NLON + (h + 1) * LANES) for h in range(2)]
        sea = [sea_mask[0:1, at].astype(jnp.float32) for at in halves]
        moves = []
        for h, at in enumerate(halves):
            lane = lax.broadcasted_iota(jnp.int32, (4, LANES), 1) + h * LANES
            move = (neighbours[:, at] - lane + NLON // 2) % NLON - NLON // 2
            moves.append(jnp.concatenate([move.astype(jnp.float32), sea[h], jnp.zeros((3, LANES))], axis=0))
        codes = split_columns(*moves)
        for h, at in enumerate(halves):
            mine[half_bins : half_bins + TILE, at] = codes[h]
            to_pair[half_bins : half_bins + TILE, at] = codes[h]
            coded = codes[h].astype(jnp.int32).astype(jnp.int16)
            to_near[half_bins // 2 : half_bins // 2 + TILE, at] = coded
            to_far[half_bins // 2 : half_bins // 2 + TILE, at] = coded
    sea_rows = [
        jnp.broadcast_to(sea_mask[0:1, j * LANES : (j + 1) * LANES].astype(jnp.float32), (SECTOR, LANES))
        for j in range(2 * rows_local)
    ]

    for other in range(2):
        base = (sub + other) % 2 * half_bins
        whole, sent = (to_pair, to_far) if other else (mine, to_near)
        for k in range(sectors):
            for rest in range(2):
                group = (2 * k + (parity + rest) % 2) * SECTOR
                source = pl.ds(pl.multiple_of(jnp.minimum(base + group, bins_local - SECTOR), SECTOR), SECTOR)
                target = pl.ds(pl.multiple_of(group, SECTOR), SECTOR)
                for row in range(rows_local):
                    pair = [
                        spectrum[source, (2 * row + h) * LANES : (2 * row + h + 1) * LANES] * sea_rows[2 * row + h]
                        for h in range(2)
                    ]
                    for h, block in enumerate(split_columns(*pair)):
                        at = slice((2 * row + h) * LANES, (2 * row + h + 1) * LANES)
                        whole[target, at] = block
                        if not rest:
                            sent[k * SECTOR : (k + 1) * SECTOR, at] = encode(block)


def pack(sizes, spectrum, neighbours, sea_mask):
    _, half_bins, rows_local = sizes
    points = rows_local * NLON
    vmem = pl.BlockSpec(memory_space=pltpu.VMEM)
    return pl.pallas_call(
        functools.partial(pack_kernel, sizes),
        name="pack",
        compiler_params=GRANT,
        in_specs=[vmem, vmem, vmem],
        out_specs=[vmem] * 4,
        out_shape=[pltpu.VMEM((half_bins + TILE, points), jnp.float32)] * 2
        + [pltpu.VMEM((half_bins // 2 + TILE, points), jnp.int16)] * 2,
    )(*map(off_chip, (spectrum, neighbours, sea_mask)))


def stencil_kernel(sizes, *refs):
    bins_local, half_bins, rows_local, dependent = sizes
    if dependent:
        steps_ref, courant_ref, trig, mine, pair, near, far, kept, crossed, other_w, own_w = refs[:11]
        passed, field_out, whole_w = refs[11:14]
        sent, (tab, begun, sem) = refs[14:-3], refs[-3:]
    else:
        steps_ref, courant_ref, trig, mine, pair, kept, passed, field_out, tab, begun = refs
    lat, sub, parity, first_group = device_place(bins_local)
    parity = (parity + int(dependent)) % 2
    first_group = first_group + sub * (half_bins // SECTOR)
    chip_rows = 2 * rows_local
    halo = chip_rows if dependent else 0
    copies = []
    if dependent:
        for other, source in enumerate((own_w, other_w)):
            at = pl.ds(pl.multiple_of((sub + other) % 2 * source.shape[0], 64), source.shape[0])
            copies.append(pltpu.make_async_copy(source, whole_w.at[at], sem.at[other]))
            copies[other].start()
    north = lat == (0 if dependent else 1)
    flip = north.astype(jnp.int32)

    def where_is(v):
        core = (v // rows_local + flip) % 2
        local = v % rows_local
        local = local + flip * (rows_local - 1 - 2 * local)
        return core, local, core == sub

    def lanes_of(local, half):
        return pl.ds(pl.multiple_of(local * NLON + half * LANES, LANES), LANES)

    for u in range(halo + chip_rows):
        _, local, here = where_is(u % chip_rows)
        for half in range(2):
            at = lanes_of(local, half)
            if u < halo:
                rows = slice(half_bins // 2, half_bins // 2 + TILE)
                codes = jnp.where(here, near[rows, at].astype(jnp.int32), far[rows, at].astype(jnp.int32))
                codes = codes.astype(jnp.float32)
            else:
                rows = slice(half_bins, half_bins + TILE)
                codes = jnp.where(here, mine[rows, at], pair[rows, at])
            wide = lambda i: jnp.broadcast_to(codes[i : i + 1], (TILE, LANES))
            tab[u, half, 0] = wide(0)
            tab[u, half, 1] = wide(1)
            tab[u, half, 2] = jnp.where(north, wide(3), wide(2))
            tab[u, half, 3] = wide(4)

    def tiles(value):
        return value.reshape(QUAD // TILE, TILE, LANES)

    def turn(value, amount):
        return pltpu.roll(value.reshape(QUAD, LANES), amount % LANES, 1).reshape(QUAD // TILE, TILE, LANES)

    def block(sector, east):
        group = 2 * sector + parity
        band = jnp.minimum((first_group + group) // 2, courant_ref.shape[0] - 1)
        speed, count = courant_ref[band], steps_ref[band]
        side = (flip + east) % 2
        trig_row = pl.ds(pl.multiple_of(SECTOR * flip + QUAD * side, QUAD), QUAD)
        part_row = pl.ds(pl.multiple_of(group * SECTOR + side * QUAD, QUAD), QUAD)
        sent_row = pl.ds(pl.multiple_of(sector * SECTOR + side * QUAD, QUAD), QUAD)
        trig_x, trig_y = tiles(trig[0, trig_row, :]), tiles(trig[1, trig_row, :])
        field = []
        for u in range(halo + chip_rows):
            core, local, here = where_is(u % chip_rows)
            both = []
            for half in range(2):
                at = lanes_of(local, half)
                if u < halo:
                    value = jnp.where(
                        here, near[sent_row, at].astype(jnp.int32), far[sent_row, at].astype(jnp.int32)
                    )
                    value = (value + 32768).astype(jnp.float32) * (1.0 / CODE_SCALE)
                else:
                    value = jnp.where(here, mine[part_row, at], pair[part_row, at])
                both.append(tiles(value))
            field.append(both)
        for t in range(MAXSTEPS):
            now = jnp.where(t < count, speed, 0.0)
            weight_x, weight_y = now * trig_x, now * trig_y
            keep = 1.0 - weight_x - weight_y
            lowest = max(0, halo - (MAXSTEPS - 1 - t))
            for u in reversed(range(lowest, halo + chip_rows)):
                (even, odd), (even_b, odd_b) = field[u], field[max(u - 1, 0)]
                moved = []
                for half in range(2):
                    move_x, move_y = tab[u, half, east], tab[u, half, 2]
                    near_x = (move_x == (1.0 if east else -1.0))[None]
                    back, ahead = (move_y == -1.0)[None], (move_y == 1.0)[None]
                    if half == 0:
                        one = odd if east else turn(odd, 1)
                        two = turn(even, -1 if east else 1)
                        centre, same = even, even_b
                        minus, plus = turn(odd_b, 1), odd_b
                    else:
                        one = turn(even, -1) if east else even
                        two = turn(odd, -1 if east else 1)
                        centre, same = odd, odd_b
                        minus, plus = even_b, turn(even_b, -1)
                    upwind_x = jnp.where(near_x, one, two)
                    upwind_y = jnp.where(back, minus, jnp.where(ahead, plus, same))
                    value = keep * centre + weight_x * upwind_x + weight_y * upwind_y
                    moved.append(tab[u, half, 3][None] * value)
                field[u] = moved
        for v in range(chip_rows):
            core, local, here = where_is(v)
            for half in range(2):
                value = field[halo + v][half].reshape(QUAD, LANES)
                other = 1 - here.astype(jnp.int32)
                begun[other, local * 2 + half, sent_row, :] = value.astype(jnp.bfloat16)
                field_out[other, sent_row, lanes_of(local, half)] = value

    def both_sides(sector, carry):
        block(sector, 0)
        block(sector, 1)
        return carry

    lax.fori_loop(0, half_bins // (2 * SECTOR), both_sides, 0)
    quarters = begun.shape[1]
    if dependent:
        third = half_bins // 2
        for k in range(quarters):
            quarter = (lax.axis_index("comp") + k) % quarters
            sent[k][:third] = kept[quarter]
            sent[k][third : 2 * third] = crossed[quarter]
            sent[k][2 * third :] = begun[0, quarter]
            passed[k] = begun[1, quarter]
    else:
        kept[...] = begun[0]
        passed[...] = begun[1]
    for copy in copies:
        copy.wait()


def stencil(sizes, substeps, courant, trig, *fields, operator=None):
    _, half_bins, rows_local, dependent = sizes
    quarters = 2 * rows_local
    rows = (4 if dependent else 2) * rows_local
    smem = pl.BlockSpec(memory_space=pltpu.SMEM)
    vmem = pl.BlockSpec(memory_space=pltpu.VMEM)
    cells = half_bins // 2 * rows_local * 2 * NLON
    in_specs = [smem] * 2 + [vmem] * (1 + len(fields))
    states = pltpu.VMEM((quarters, half_bins // 2, LANES), jnp.bfloat16)
    field = pltpu.VMEM((2, half_bins // 2, rows_local * NLON), jnp.float32)
    scratch = [
        pltpu.VMEM((rows, 2, 4, TILE, LANES), jnp.float32),
        pltpu.VMEM((2, quarters, half_bins // 2, LANES), jnp.bfloat16),
    ]
    args = list(map(off_chip, (substeps, courant, trig))) + list(map(on_chip, fields))
    out_shape = [states, states, field]
    if dependent:
        in_specs.append(pl.BlockSpec(memory_space=pl.ANY))
        args.append(off_chip(operator))
        out_shape = [states, field, pltpu.VMEM((2 * operator.shape[0], operator.shape[1]), jnp.bfloat16)]
        out_shape += [pltpu.VMEM((half_bins // 2 * 3, LANES), jnp.bfloat16)] * quarters
        scratch.append(pltpu.SemaphoreType.DMA((2,)))
    return pl.pallas_call(
        functools.partial(stencil_kernel, sizes),
        name="stencil_dependent" if dependent else "stencil_free",
        compiler_params=GRANT,
        in_specs=in_specs,
        out_specs=[vmem] * len(out_shape),
        out_shape=out_shape,
        scratch_shapes=scratch,
        cost_estimate=pl.CostEstimate(flops=cells * MAXSTEPS * 100, bytes_accessed=cells * 16, transcendentals=0),
    )(*args)


def integrate_kernel(sizes, whole_w, *refs):
    bins_local, half_bins, comps = sizes
    large, passed, small = refs[:comps], refs[comps], refs[comps + 1 : 2 * comps]
    outs, (state, driver) = refs[2 * comps : 3 * comps], refs[3 * comps :]
    comp, lat, sub = (lax.axis_index(name) for name in ("comp", "lat", "sub"))
    total = comps * bins_local
    sectors = half_bins // (2 * SECTOR)
    groups = bins_local // SECTOR
    third = half_bins // 2
    for k in range(comps):
        source = (comp + comps - k) % comps
        free = (source * groups + lat) % 2
        parts = (
            (large[k], 0, 0, 0),
            (large[k], third, 1, 0),
            (large[k], 2 * third, 0, 1),
            (small[k - 1] if k else passed.at[0], 0, 1, 1),
        )
        for blocks, first, other, dep in parts:
            for sector in range(sectors):
                local = (sub + other) % 2 * half_bins + (2 * sector + (free + dep) % 2) * SECTOR
                row = jnp.where(local < bins_local, source * bins_local + local, total)
                row = pl.ds(pl.multiple_of(row, SECTOR), SECTOR)
                block = blocks[first + sector * SECTOR : first + (sector + 1) * SECTOR, :]
                driver[0, row, :] = block
                state[row, :] = block.astype(jnp.float32)
    stretch = total // 2
    for step in range(SRC_STEPS):
        read = 0 if step == 0 else 1 + step % 2
        write = 1 + (step + 1) % 2
        for first in range(0, total, stretch):
            at = slice(first, first + stretch)
            drive = jnp.dot(whole_w[at, :], driver[read, :total, :], preferred_element_type=jnp.float32)
            value = state[at, :]
            value = value + STEP_SIZE * value * drive
            if step + 1 < SRC_STEPS:
                state[at, :] = value
                driver[write, at, :] = value.astype(jnp.bfloat16)
            else:
                driver[write, at, :] = (value - driver[0, at, :].astype(jnp.float32)).astype(jnp.bfloat16)
    for k in range(comps):
        at = pl.ds(pl.multiple_of((comp + k) % comps * bins_local, SECTOR), bins_local)
        outs[k][...] = driver[write, at, :]


def integrate(sizes, whole_w, large, passed, small):
    bins_local, _, comps = sizes
    total = comps * bins_local
    vmem = pl.BlockSpec(memory_space=pltpu.VMEM)
    return pl.pallas_call(
        functools.partial(integrate_kernel, sizes),
        name="integrate",
        compiler_params=GRANT,
        in_specs=[vmem] * (1 + 2 * comps),
        out_specs=[vmem] * comps,
        out_shape=[pltpu.VMEM((bins_local, LANES), jnp.bfloat16)] * comps,
        scratch_shapes=[
            pltpu.VMEM((total + SECTOR, LANES), jnp.float32),
            pltpu.VMEM((3, total + SECTOR, LANES), jnp.bfloat16),
        ],
        cost_estimate=pl.CostEstimate(
            flops=2 * SRC_STEPS * total * total * LANES, bytes_accessed=2 * total * total, transcendentals=0
        ),
    )(*map(on_chip, (whole_w, *large, passed, *small)))


def finish_kernel(sizes, *refs):
    bins_local, half_bins = sizes
    mine_free, mine_dep, got_free, got_dep, sea_mask = refs[:5]
    out, whole, raised, sem = refs[-4:]
    steps_up = refs[5:-4]
    comp = lax.axis_index("comp")
    for k, increments in enumerate(steps_up):
        raised[(comp + len(steps_up) - k) % len(steps_up)] = increments[...]
    _, sub, parity, _ = device_place(bins_local)
    tiles = whole.shape[1] // LANES
    sea = [
        jnp.broadcast_to(sea_mask[0:1, j * LANES : (j + 1) * LANES].astype(jnp.float32), (SECTOR, LANES))
        for j in range(tiles)
    ]
    sectors = half_bins // (2 * SECTOR)

    def rows_out(group, semaphore):
        at = pl.ds(pl.multiple_of(group, SECTOR), SECTOR)
        return pltpu.make_async_copy(whole.at[at], out.at[at], semaphore)

    for other, pair in enumerate(((mine_free, mine_dep), (got_free, got_dep))):
        base = (sub + other) % 2 * half_bins
        for k in range(sectors):
            for dep, source in enumerate(pair):
                row = base + (2 * k + (parity + dep) % 2) * SECTOR
                rows = pl.ds(pl.multiple_of(row, SECTOR), SECTOR)
                added = pl.ds(pl.multiple_of(jnp.minimum(row, bins_local - SECTOR), SECTOR), SECTOR)
                for j in range(0, tiles, 2):
                    halves = [
                        source[0, k * SECTOR : (k + 1) * SECTOR, i * LANES : (i + 1) * LANES]
                        + raised[i, added, :].astype(jnp.float32)
                        for i in (j, j + 1)
                    ]
                    for i, value in enumerate(join_columns(*halves)):
                        whole[rows, (j + i) * LANES : (j + i + 1) * LANES] = sea[j + i] * value
            for rest in range(2):
                group = base + (2 * k + rest) * SECTOR

                @pl.when(group < bins_local)
                def _():
                    rows_out(group, sem.at[other, k, rest]).start()

    for other in range(2):
        for k in range(sectors):
            for rest in range(2):
                group = (sub + other) % 2 * half_bins + (2 * k + rest) * SECTOR

                @pl.when(group < bins_local)
                def _():
                    rows_out(group, sem.at[other, k, rest]).wait()


def finish(sizes, fields, sea_mask, steps_up):
    bins_local, half_bins = sizes
    points = sea_mask.shape[1]
    vmem = pl.BlockSpec(memory_space=pltpu.VMEM)
    comps = len(steps_up)
    return pl.pallas_call(
        functools.partial(finish_kernel, sizes),
        name="finish",
        compiler_params=GRANT,
        in_specs=[vmem] * (5 + comps),
        out_specs=pl.BlockSpec(memory_space=pl.ANY),
        out_shape=jax.ShapeDtypeStruct((bins_local, points), jnp.float32),
        scratch_shapes=[
            pltpu.VMEM((2 * half_bins, points), jnp.float32),
            pltpu.VMEM((comps, bins_local, LANES), jnp.bfloat16),
            pltpu.SemaphoreType.DMA((2, half_bins // (2 * SECTOR), 2)),
        ],
    )(*map(on_chip, fields), sea_mask, *map(on_chip, steps_up))


def on_chip(values):
    return pltpu.with_memory_space_constraint(values, pltpu.VMEM)


def off_chip(values):
    return pltpu.with_memory_space_constraint(values, pltpu.HBM)


def swap(values, bits):
    count = lax.axis_size("lat") * lax.axis_size("sub")
    return lax.ppermute(values, ("lat", "sub"), [(i, i ^ bits) for i in range(count)])


def two_chip_device(spectrum, sea_mask, neighbours, substeps, courant, source_operator):
    comps = lax.axis_size("comp")
    bins_local, points_local = spectrum.shape
    rows_local = points_local // NLON
    half_bins = (bins_local // SECTOR + 3) // 4 * 2 * SECTOR
    sea_mask = sea_mask[None, :]
    angles = (np.arange(ND, dtype=np.float32) + np.float32(0.5)) * np.float32(2.0 * math.pi / ND)
    trig = np.abs(np.stack([np.cos(angles), np.sin(angles)])).astype(np.float32)
    trig = jnp.asarray(np.repeat(trig[:, :, None], LANES, axis=2))

    other_w = swap(source_operator, 1)
    mine, to_pair, to_near, to_far = pack(
        (bins_local, half_bins, rows_local), spectrum, neighbours, sea_mask
    )
    pair = swap(to_pair, 1)
    near = swap(to_near, 2)
    far = swap(to_far, 3)
    kept, passed, free_field = stencil((bins_local, half_bins, rows_local, False), substeps, courant, trig, mine, pair)
    crossed = swap(passed, 1)
    near, far, other_w, crossed = lax.optimization_barrier((near, far, other_w, crossed))
    passed, dep_field, whole_w, *sent = stencil(
        (bins_local, half_bins, rows_local, True),
        substeps,
        courant,
        trig,
        mine,
        pair,
        near,
        far,
        kept,
        crossed,
        other_w,
        operator=source_operator,
    )
    ring = [[(i, (i + k) % comps) for i in range(comps)] for k in range(comps)]
    passed = swap(passed, 1)
    large = [sent[0]] + [lax.ppermute(sent[k], "comp", ring[k]) for k in range(1, comps)]
    small = [lax.ppermute(passed[k], "comp", ring[k]) for k in range(1, comps)]
    raised = integrate((bins_local, half_bins, comps), whole_w, large, passed, small)
    free_field, dep_field, raised = lax.optimization_barrier((free_field, dep_field, raised))
    home = [raised[0]] + [lax.ppermute(raised[k], "comp", ring[k]) for k in range(1, comps)]
    got_free = swap(free_field[1:], 1)
    got_dep = swap(dep_field[1:], 1)
    return finish((bins_local, half_bins), (free_field, dep_field, got_free, got_dep), sea_mask, home)


def device_step(*arrays):
    bins_local, points_local = arrays[0].shape
    two_chips = (
        lax.axis_size("lat") == 2
        and lax.axis_size("sub") == 2
        and bins_local % SECTOR == 0
        and points_local % NLON == 0
        and points_local == lax.axis_size("comp") * LANES
        and lax.axis_size("comp") * bins_local % LANES == 0
    )
    return (two_chip_device if two_chips else per_device)(*arrays)


def solution(mesh):
    placed = (
        P("comp", ("members", "lat", "sub")),
        P(("members", "lat", "sub")),
        P(None, ("members", "lat", "sub")),
        P(),
        P(),
        P("sub", None),
    )
    return jax.shard_map(
        device_step,
        mesh=mesh,
        in_specs=placed,
        out_specs=P("comp", ("members", "lat", "sub")),
        check_vma=False,
    )
```

```python
import functools
import math

import jax
import jax.numpy as jnp
import numpy as np
from jax import lax
from jax.experimental import pallas as pl
from jax.experimental.pallas import tpu as pltpu
from jax.sharding import PartitionSpec as P


NF = 30
ND = 64
NLON = 256
MAXSTEPS = 6
SRC_STEPS = 4


STEP_SIZE = 0.1


def extended(cells, sides, width):
    for axis, dim in sides:
        count = lax.axis_size(axis)
        ends = count - 1
        head = lax.slice_in_dim(cells, 0, width, axis=dim)
        tail = lax.slice_in_dim(cells, cells.shape[dim] - width, cells.shape[dim], axis=dim)
        cells = jnp.concatenate(
            [
                lax.ppermute(tail, axis, [(i, (i + 1) % count) for i in range(ends)]),
                cells,
                lax.ppermute(head, axis, [((i + 1) % count, i) for i in range(ends)]),
            ],
            axis=dim,
        )
    return cells


def bin_tables(global_bins, substeps, courant):
    frequency = global_bins // ND
    direction = global_bins % ND
    chosen = frequency[:, None] == jnp.arange(NF, dtype=jnp.int32)[None, :]
    bin_steps = jnp.sum(jnp.where(chosen, substeps[None, :], 0), axis=1)
    bin_speed = jnp.sum(jnp.where(chosen, courant[None, :], 0.0), axis=1)
    angles = (direction.astype(jnp.float32) + 0.5) * (2.0 * math.pi / ND)
    cosine = jnp.cos(angles)
    sine_dir = jnp.sin(angles)
    return (
        bin_steps,
        bin_speed * jnp.abs(cosine),
        bin_speed * jnp.abs(sine_dir),
        cosine > 0,
        sine_dir > 0,
    )


def offset_codes(neighbours, sea_float, points_local):
    position = lax.axis_index(("lat", "sub")) * points_local + jnp.arange(
        points_local, dtype=jnp.int32
    )
    column = position % NLON
    west_gap = (column - neighbours[0] % NLON) % NLON
    east_gap = (neighbours[1] % NLON - column) % NLON

    def vertical_code(index_row):
        column_move = (index_row % NLON - column + 1) % NLON - 1
        return jnp.where(index_row == position, 2, column_move)

    stacked = jnp.stack(
        [west_gap, east_gap, vertical_code(neighbours[2]), vertical_code(neighbours[3])]
    ).astype(jnp.float32)
    return jnp.concatenate([stacked, sea_float[None, :]], axis=0).reshape(
        5, points_local // NLON, NLON
    )


def column_roll(values, amount):
    return jnp.roll(values, amount, axis=-1)


def vertical_pick(other_rows, code_row, center):
    moved = jnp.where(
        code_row == -1.0,
        column_roll(other_rows, 1),
        jnp.where(code_row == 1.0, column_roll(other_rows, -1), other_rows),
    )
    return jnp.where(code_row == 2.0, center, moved)


def advance(substep, center, below, above, point_codes, tables):
    bin_steps, weight_x, weight_y, from_west, from_south = tables
    west_vals = jnp.where(
        point_codes[0][None] == 1.0, column_roll(center, 1), column_roll(center, 2)
    )
    east_vals = jnp.where(
        point_codes[1][None] == 1.0, column_roll(center, -1), column_roll(center, -2)
    )
    upwind_lon = jnp.where(from_west[:, None, None], west_vals, east_vals)
    south_vals = vertical_pick(below, point_codes[2][None], center)
    north_vals = vertical_pick(above, point_codes[3][None], center)
    upwind_lat = jnp.where(from_south[:, None, None], south_vals, north_vals)
    advanced = point_codes[4][None] * (
        center
        - weight_x[:, None, None] * (center - upwind_lon)
        - weight_y[:, None, None] * (center - upwind_lat)
    )
    return jnp.where((substep < bin_steps)[:, None, None], advanced, center)


def propagate(spec_part, global_bins, substeps, courant, point_codes):
    tables = bin_tables(global_bins, substeps, courant)
    bin_count = spec_part.shape[0]
    points_local = spec_part.shape[1]
    row_count = points_local // NLON
    field_now = spec_part.reshape(bin_count, row_count, NLON)
    for substep in range(MAXSTEPS):
        padded = extended(field_now, ((("lat", "sub"), 1),), 1)
        field_now = advance(substep, field_now, padded[:, :-2], padded[:, 2:], point_codes, tables)
    return field_now.reshape(bin_count, points_local)


def per_device(spectrum, sea_mask, neighbours, substeps, courant, source_operator):
    comp_index = lax.axis_index("comp")
    bins_local = spectrum.shape[0]
    points_local = spectrum.shape[1]
    sea_float = sea_mask.astype(jnp.float32)
    point_codes = offset_codes(neighbours, sea_float, points_local)
    field_start = sea_float[None, :] * spectrum
    first_bin = comp_index * bins_local
    held_bins = first_bin + jnp.arange(bins_local, dtype=jnp.int32)
    propagated = propagate(field_start, held_bins, substeps, courant, point_codes)
    outgoing = propagated.astype(jnp.bfloat16)
    owned_cols = lax.all_to_all(outgoing, "comp", split_axis=1, concat_axis=0, tiled=True)
    whole_operator = lax.all_gather(source_operator, "sub", axis=0, tiled=True)
    point_rows = owned_cols.T
    start_state = point_rows.astype(jnp.float32)
    state_now = start_state
    full_rows = point_rows
    for source_step in range(SRC_STEPS):
        driving = lax.dot_general(
            full_rows, whole_operator, (((1,), (1,)), ((), ())), preferred_element_type=jnp.float32
        )
        state_now = state_now + STEP_SIZE * state_now * driving
        if source_step + 1 < SRC_STEPS:
            full_rows = state_now.astype(jnp.bfloat16)
    returned = (state_now - start_state).astype(jnp.bfloat16).T
    home_bins = lax.all_to_all(returned, "comp", split_axis=0, concat_axis=1, tiled=True)
    return sea_float[None, :] * (propagated + home_bins.astype(jnp.float32))


LANES = 128
TILE = 8
QUAD = 16
SECTOR = 32
CODE_SCALE = 32767.5
GRANT = pltpu.CompilerParams(vmem_limit_bytes=16 << 20)


def lane_pick(values, index):
    return jnp.take_along_axis(values, index, axis=1, mode="promise_in_bounds")


def split_columns(first, second):
    lane = lax.broadcasted_iota(jnp.int32, first.shape, 1)
    even, low = 2 * lane % LANES, lane < LANES // 2
    return (
        jnp.where(low, lane_pick(first, even), lane_pick(second, even)),
        jnp.where(low, lane_pick(first, even + 1), lane_pick(second, even + 1)),
    )


def join_columns(even, odd):
    lane = lax.broadcasted_iota(jnp.int32, even.shape, 1)
    index, is_even = lane // 2, lane % 2 == 0
    upper = index + LANES // 2
    return (
        jnp.where(is_even, lane_pick(even, index), lane_pick(odd, index)),
        jnp.where(is_even, lane_pick(even, upper), lane_pick(odd, upper)),
    )


def encode(values):
    return ((values * CODE_SCALE + 0.5).astype(jnp.int32) - 32768).astype(jnp.int16)


def device_place(bins_local):
    lat, sub = lax.axis_index("lat"), lax.axis_index("sub")
    first_group = lax.axis_index("comp") * (bins_local // SECTOR)
    return lat, sub, (first_group + lat) % 2, first_group


def pack_kernel(sizes, spectrum, neighbours, sea_mask, mine, to_pair, to_near, to_far, held, sem):
    bins_local, half_bins, rows_local = sizes
    _, sub, parity, _ = device_place(bins_local)
    sectors = half_bins // (2 * SECTOR)
    copies = []
    for other in range(2):
        base = (sub + other) % 2 * half_bins
        for k in range(sectors):
            for rest in range(2):
                group = (2 * k + (parity + rest) % 2) * SECTOR
                source = pl.ds(pl.multiple_of(jnp.minimum(base + group, bins_local - SECTOR), SECTOR), SECTOR)
                index = len(copies)
                copies.append(pltpu.make_async_copy(spectrum.at[source], held.at[index], sem.at[index]))
                copies[index].start()
    for row in range(rows_local):
        halves = [slice(row * NLON + h * LANES, row * NLON + (h + 1) * LANES) for h in range(2)]
        sea = [sea_mask[0:1, at].astype(jnp.float32) for at in halves]
        moves = []
        for h, at in enumerate(halves):
            lane = lax.broadcasted_iota(jnp.int32, (4, LANES), 1) + h * LANES
            move = (neighbours[:, at] - lane + NLON // 2) % NLON - NLON // 2
            moves.append(jnp.concatenate([move.astype(jnp.float32), sea[h], jnp.zeros((3, LANES))], axis=0))
        codes = split_columns(*moves)
        for h, at in enumerate(halves):
            mine[half_bins : half_bins + TILE, at] = codes[h]
            to_pair[half_bins : half_bins + TILE, at] = codes[h]
            coded = codes[h].astype(jnp.int32).astype(jnp.int16)
            to_near[half_bins // 2 : half_bins // 2 + TILE, at] = coded
            to_far[half_bins // 2 : half_bins // 2 + TILE, at] = coded
    sea_rows = [
        jnp.broadcast_to(sea_mask[0:1, j * LANES : (j + 1) * LANES].astype(jnp.float32), (SECTOR, LANES))
        for j in range(2 * rows_local)
    ]

    for index, copy in enumerate(copies):
        other, k, rest = index // (2 * sectors), index // 2 % sectors, index % 2
        whole, sent = (to_pair, to_far) if other else (mine, to_near)
        target = pl.ds(pl.multiple_of((2 * k + (parity + rest) % 2) * SECTOR, SECTOR), SECTOR)
        copy.wait()
        for row in range(rows_local):
            pair = [
                held[index, :, (2 * row + h) * LANES : (2 * row + h + 1) * LANES] * sea_rows[2 * row + h]
                for h in range(2)
            ]
            for h, block in enumerate(split_columns(*pair)):
                at = slice((2 * row + h) * LANES, (2 * row + h + 1) * LANES)
                whole[target, at] = block
                if not rest:
                    sent[k * SECTOR : (k + 1) * SECTOR, at] = encode(block)


def pack(sizes, spectrum, neighbours, sea_mask):
    _, half_bins, rows_local = sizes
    points = rows_local * NLON
    vmem = pl.BlockSpec(memory_space=pltpu.VMEM)
    return pl.pallas_call(
        functools.partial(pack_kernel, sizes),
        name="pack",
        compiler_params=GRANT,
        in_specs=[pl.BlockSpec(memory_space=pl.ANY), vmem, vmem],
        scratch_shapes=[
            pltpu.VMEM((2 * half_bins // SECTOR, SECTOR, points), jnp.float32),
            pltpu.SemaphoreType.DMA((2 * half_bins // SECTOR,)),
        ],
        out_specs=[vmem] * 4,
        out_shape=[pltpu.VMEM((half_bins + TILE, points), jnp.float32)] * 2
        + [pltpu.VMEM((half_bins // 2 + TILE, points), jnp.int16)] * 2,
    )(*map(off_chip, (spectrum, neighbours, sea_mask)))


def stencil_kernel(sizes, *refs):
    bins_local, half_bins, rows_local, dependent = sizes
    if dependent:
        steps_ref, courant_ref, trig, mine, pair, near, far, kept, free_passed, passed, field_out = refs[:11]
        sent, (tab, begun) = refs[11:-2], refs[-2:]
    else:
        steps_ref, courant_ref, trig, mine, pair, kept, passed, field_out, tab, begun = refs
    lat, sub, parity, first_group = device_place(bins_local)
    parity = (parity + int(dependent)) % 2
    first_group = first_group + sub * (half_bins // SECTOR)
    chip_rows = 2 * rows_local
    halo = chip_rows if dependent else 0
    north = lat == (0 if dependent else 1)
    flip = north.astype(jnp.int32)

    def where_is(v):
        core = (v // rows_local + flip) % 2
        local = v % rows_local
        local = local + flip * (rows_local - 1 - 2 * local)
        return core, local, core == sub

    def lanes_of(local, half):
        return pl.ds(pl.multiple_of(local * NLON + half * LANES, LANES), LANES)

    for u in range(halo + chip_rows):
        _, local, here = where_is(u % chip_rows)
        for half in range(2):
            at = lanes_of(local, half)
            if u < halo:
                rows = slice(half_bins // 2, half_bins // 2 + TILE)
                codes = jnp.where(here, near[rows, at].astype(jnp.int32), far[rows, at].astype(jnp.int32))
                codes = codes.astype(jnp.float32)
            else:
                rows = slice(half_bins, half_bins + TILE)
                codes = jnp.where(here, mine[rows, at], pair[rows, at])
            wide = lambda i: jnp.broadcast_to(codes[i : i + 1], (TILE, LANES))
            tab[u, half, 0] = wide(0)
            tab[u, half, 1] = wide(1)
            tab[u, half, 2] = jnp.where(north, wide(3), wide(2))
            tab[u, half, 3] = wide(4)

    def tiles(value):
        return value.reshape(QUAD // TILE, TILE, LANES)

    def turn(value, amount):
        return pltpu.roll(value.reshape(QUAD, LANES), amount % LANES, 1).reshape(QUAD // TILE, TILE, LANES)

    def block(sector, east):
        group = 2 * sector + parity
        band = jnp.minimum((first_group + group) // 2, courant_ref.shape[0] - 1)
        speed, count = courant_ref[band], steps_ref[band]
        side = (flip + east) % 2
        trig_row = pl.ds(pl.multiple_of(SECTOR * flip + QUAD * side, QUAD), QUAD)
        part_row = pl.ds(pl.multiple_of(group * SECTOR + side * QUAD, QUAD), QUAD)
        sent_row = pl.ds(pl.multiple_of(sector * SECTOR + side * QUAD, QUAD), QUAD)
        trig_x, trig_y = tiles(trig[0, trig_row, :]), tiles(trig[1, trig_row, :])
        field = []
        for u in range(halo + chip_rows):
            core, local, here = where_is(u % chip_rows)
            both = []
            for half in range(2):
                at = lanes_of(local, half)
                if u < halo:
                    value = jnp.where(
                        here, near[sent_row, at].astype(jnp.int32), far[sent_row, at].astype(jnp.int32)
                    )
                    value = (value + 32768).astype(jnp.float32) * (1.0 / CODE_SCALE)
                else:
                    value = jnp.where(here, mine[part_row, at], pair[part_row, at])
                both.append(tiles(value))
            field.append(both)
        for t in range(MAXSTEPS):
            now = jnp.where(t < count, speed, 0.0)
            weight_x, weight_y = now * trig_x, now * trig_y
            keep = 1.0 - weight_x - weight_y
            lowest = max(0, halo - (MAXSTEPS - 1 - t))
            for u in reversed(range(lowest, halo + chip_rows)):
                (even, odd), (even_b, odd_b) = field[u], field[max(u - 1, 0)]
                moved = []
                for half in range(2):
                    move_x, move_y = tab[u, half, east], tab[u, half, 2]
                    near_x = (move_x == (1.0 if east else -1.0))[None]
                    back, ahead = (move_y == -1.0)[None], (move_y == 1.0)[None]
                    if half == 0:
                        one = odd if east else turn(odd, 1)
                        two = turn(even, -1 if east else 1)
                        centre, same = even, even_b
                        minus, plus = turn(odd_b, 1), odd_b
                    else:
                        one = turn(even, -1) if east else even
                        two = turn(odd, -1 if east else 1)
                        centre, same = odd, odd_b
                        minus, plus = even_b, turn(even_b, -1)
                    upwind_x = jnp.where(near_x, one, two)
                    upwind_y = jnp.where(back, minus, jnp.where(ahead, plus, same))
                    value = keep * centre + weight_x * upwind_x + weight_y * upwind_y
                    moved.append(tab[u, half, 3][None] * value)
                field[u] = moved
        for v in range(chip_rows):
            core, local, here = where_is(v)
            for half in range(2):
                value = field[halo + v][half].reshape(QUAD, LANES)
                other = 1 - here.astype(jnp.int32)
                begun[other, local * 2 + half, sent_row, :] = value.astype(jnp.bfloat16)
                field_out[other, sent_row, lanes_of(local, half)] = value

    def both_sides(sector, carry):
        block(sector, 0)
        block(sector, 1)
        return carry

    lax.fori_loop(0, half_bins // (2 * SECTOR), both_sides, 0)
    quarters = begun.shape[1]
    if dependent:
        middle = half_bins // 2
        for k in range(quarters):
            quarter = (lax.axis_index("comp") + k) % quarters
            sent[k][:middle] = kept[quarter]
            sent[k][middle:] = begun[0, quarter]
            passed[k, :middle] = free_passed[quarter]
            passed[k, middle:] = begun[1, quarter]
    else:
        kept[...] = begun[0]
        passed[...] = begun[1]


def stencil(sizes, substeps, courant, trig, *fields):
    _, half_bins, rows_local, dependent = sizes
    quarters = 2 * rows_local
    rows = (4 if dependent else 2) * rows_local
    smem = pl.BlockSpec(memory_space=pltpu.SMEM)
    vmem = pl.BlockSpec(memory_space=pltpu.VMEM)
    cells = half_bins // 2 * rows_local * 2 * NLON
    in_specs = [smem] * 2 + [vmem] * (1 + len(fields))
    states = pltpu.VMEM((quarters, half_bins // 2, LANES), jnp.bfloat16)
    field = pltpu.VMEM((2, half_bins // 2, rows_local * NLON), jnp.float32)
    scratch = [
        pltpu.VMEM((rows, 2, 4, TILE, LANES), jnp.float32),
        pltpu.VMEM((2, quarters, half_bins // 2, LANES), jnp.bfloat16),
    ]
    args = list(map(off_chip, (substeps, courant, trig))) + list(map(on_chip, fields))
    out_shape = [states, states, field]
    if dependent:
        out_shape = [pltpu.VMEM((quarters, half_bins, LANES), jnp.bfloat16), field]
        out_shape += [pltpu.VMEM((half_bins, LANES), jnp.bfloat16)] * quarters
    return pl.pallas_call(
        functools.partial(stencil_kernel, sizes),
        name="stencil_dependent" if dependent else "stencil_free",
        compiler_params=GRANT,
        in_specs=in_specs,
        out_specs=[vmem] * len(out_shape),
        out_shape=out_shape,
        scratch_shapes=scratch,
        cost_estimate=pl.CostEstimate(flops=cells * MAXSTEPS * 100, bytes_accessed=cells * 16, transcendentals=0),
    )(*args)


def gather_operator_kernel(own_w, other_w, whole_w, sem):
    sub = lax.axis_index("sub")
    pieces = sem.shape[1]
    rows = own_w.shape[0] // pieces
    copies = []
    for other, source in enumerate((own_w, other_w)):
        for p in range(pieces):
            at = pl.ds(pl.multiple_of((sub + other) % 2 * own_w.shape[0] + p * rows, 64), rows)
            copy = pltpu.make_async_copy(source.at[pl.ds(p * rows, rows)], whole_w.at[at], sem.at[other, p])
            copy.start()
            copies.append(copy)
    for copy in copies:
        copy.wait()


def gather_operator(own_w, other_w):
    rows, columns = own_w.shape
    return pl.pallas_call(
        gather_operator_kernel,
        name="gather_operator",
        compiler_params=GRANT,
        in_specs=[pl.BlockSpec(memory_space=pl.ANY), pl.BlockSpec(memory_space=pltpu.VMEM)],
        out_specs=pl.BlockSpec(memory_space=pltpu.VMEM),
        out_shape=pltpu.VMEM((2 * rows, columns), jnp.bfloat16),
        scratch_shapes=[pltpu.SemaphoreType.DMA((2, 3))],
        cost_estimate=pl.CostEstimate(flops=0, bytes_accessed=4 * rows * columns, transcendentals=0),
    )(off_chip(own_w), on_chip(other_w))


def integrate_kernel(sizes, whole_w, *refs):
    bins_local, half_bins, comps = sizes
    large, passed, small = refs[:comps], refs[comps], refs[comps + 1 : 2 * comps]
    outs, (state, driver) = refs[2 * comps : 3 * comps], refs[3 * comps :]
    comp, lat, sub = (lax.axis_index(name) for name in ("comp", "lat", "sub"))
    total = comps * bins_local
    sectors = half_bins // (2 * SECTOR)
    groups = bins_local // SECTOR
    middle = half_bins // 2
    for k in range(comps):
        source = (comp + comps - k) % comps
        free = (source * groups + lat) % 2
        crossed = small[k - 1] if k else passed.at[0]
        parts = ((large[k], 0, 0, 0), (large[k], middle, 0, 1), (crossed, 0, 1, 0), (crossed, middle, 1, 1))
        for blocks, first, other, dep in parts:
            for sector in range(sectors):
                local = (sub + other) % 2 * half_bins + (2 * sector + (free + dep) % 2) * SECTOR
                row = jnp.where(local < bins_local, source * bins_local + local, total)
                row = pl.ds(pl.multiple_of(row, SECTOR), SECTOR)
                block = blocks[first + sector * SECTOR : first + (sector + 1) * SECTOR, :]
                driver[0, row, :] = block
                state[row, :] = block.astype(jnp.float32)
    stretch = total // 2
    for step in range(SRC_STEPS):
        read = 0 if step == 0 else 1 + step % 2
        write = 1 + (step + 1) % 2
        for first in range(0, total, stretch):
            at = slice(first, first + stretch)
            drive = jnp.dot(whole_w[at, :], driver[read, :total, :], preferred_element_type=jnp.float32)
            value = state[at, :]
            value = value + STEP_SIZE * value * drive
            if step + 1 < SRC_STEPS:
                state[at, :] = value
                driver[write, at, :] = value.astype(jnp.bfloat16)
            else:
                driver[write, at, :] = (value - driver[0, at, :].astype(jnp.float32)).astype(jnp.bfloat16)
    for k in range(comps):
        at = pl.ds(pl.multiple_of((comp + k) % comps * bins_local, SECTOR), bins_local)
        outs[k][...] = driver[write, at, :]


def integrate(sizes, whole_w, large, passed, small):
    bins_local, _, comps = sizes
    total = comps * bins_local
    vmem = pl.BlockSpec(memory_space=pltpu.VMEM)
    return pl.pallas_call(
        functools.partial(integrate_kernel, sizes),
        name="integrate",
        compiler_params=GRANT,
        in_specs=[vmem] * (1 + 2 * comps),
        out_specs=[vmem] * comps,
        out_shape=[pltpu.VMEM((bins_local, LANES), jnp.bfloat16)] * comps,
        scratch_shapes=[
            pltpu.VMEM((total + SECTOR, LANES), jnp.float32),
            pltpu.VMEM((3, total + SECTOR, LANES), jnp.bfloat16),
        ],
        cost_estimate=pl.CostEstimate(
            flops=2 * SRC_STEPS * total * total * LANES, bytes_accessed=2 * total * total, transcendentals=0
        ),
    )(*map(on_chip, (whole_w, *large, passed, *small)))


def finish_kernel(sizes, *refs):
    bins_local, half_bins = sizes
    mine_free, mine_dep, got_free, got_dep, sea_mask = refs[:5]
    out, whole, raised, sem = refs[-4:]
    steps_up = refs[5:-4]
    comp = lax.axis_index("comp")
    for k, increments in enumerate(steps_up):
        raised[(comp + len(steps_up) - k) % len(steps_up)] = increments[...]
    _, sub, parity, _ = device_place(bins_local)
    tiles = whole.shape[1] // LANES
    sea = [
        jnp.broadcast_to(sea_mask[0:1, j * LANES : (j + 1) * LANES].astype(jnp.float32), (SECTOR, LANES))
        for j in range(tiles)
    ]
    sectors = half_bins // (2 * SECTOR)

    def rows_out(group, semaphore):
        at = pl.ds(pl.multiple_of(group, SECTOR), SECTOR)
        return pltpu.make_async_copy(whole.at[at], out.at[at], semaphore)

    for other, pair in enumerate(((mine_free, mine_dep), (got_free, got_dep))):
        base = (sub + other) % 2 * half_bins
        for k in range(sectors):
            for dep, source in enumerate(pair):
                row = base + (2 * k + (parity + dep) % 2) * SECTOR
                rows = pl.ds(pl.multiple_of(row, SECTOR), SECTOR)
                added = pl.ds(pl.multiple_of(jnp.minimum(row, bins_local - SECTOR), SECTOR), SECTOR)
                for j in range(0, tiles, 2):
                    halves = [
                        source[0, k * SECTOR : (k + 1) * SECTOR, i * LANES : (i + 1) * LANES]
                        + raised[i, added, :].astype(jnp.float32)
                        for i in (j, j + 1)
                    ]
                    for i, value in enumerate(join_columns(*halves)):
                        whole[rows, (j + i) * LANES : (j + i + 1) * LANES] = sea[j + i] * value
            for rest in range(2):
                group = base + (2 * k + rest) * SECTOR

                @pl.when(group < bins_local)
                def _():
                    rows_out(group, sem.at[other, k, rest]).start()

    for other in range(2):
        for k in range(sectors):
            for rest in range(2):
                group = (sub + other) % 2 * half_bins + (2 * k + rest) * SECTOR

                @pl.when(group < bins_local)
                def _():
                    rows_out(group, sem.at[other, k, rest]).wait()


def finish(sizes, fields, sea_mask, steps_up):
    bins_local, half_bins = sizes
    points = sea_mask.shape[1]
    vmem = pl.BlockSpec(memory_space=pltpu.VMEM)
    comps = len(steps_up)
    return pl.pallas_call(
        functools.partial(finish_kernel, sizes),
        name="finish",
        compiler_params=GRANT,
        in_specs=[vmem] * (5 + comps),
        out_specs=pl.BlockSpec(memory_space=pl.ANY),
        out_shape=jax.ShapeDtypeStruct((bins_local, points), jnp.float32),
        scratch_shapes=[
            pltpu.VMEM((2 * half_bins, points), jnp.float32),
            pltpu.VMEM((comps, bins_local, LANES), jnp.bfloat16),
            pltpu.SemaphoreType.DMA((2, half_bins // (2 * SECTOR), 2)),
        ],
    )(*map(on_chip, fields), sea_mask, *map(on_chip, steps_up))


def on_chip(values):
    return pltpu.with_memory_space_constraint(values, pltpu.VMEM)


def off_chip(values):
    return pltpu.with_memory_space_constraint(values, pltpu.HBM)


def swap(values, bits):
    count = lax.axis_size("lat") * lax.axis_size("sub")
    return lax.ppermute(values, ("lat", "sub"), [(i, i ^ bits) for i in range(count)])


def two_chip_device(spectrum, sea_mask, neighbours, substeps, courant, source_operator):
    comps = lax.axis_size("comp")
    bins_local, points_local = spectrum.shape
    rows_local = points_local // NLON
    half_bins = (bins_local // SECTOR + 3) // 4 * 2 * SECTOR
    sea_mask = sea_mask[None, :]
    angles = (np.arange(ND, dtype=np.float32) + np.float32(0.5)) * np.float32(2.0 * math.pi / ND)
    trig = np.abs(np.stack([np.cos(angles), np.sin(angles)])).astype(np.float32)
    trig = jnp.asarray(np.repeat(trig[:, :, None], LANES, axis=2))

    mine, to_pair, to_near, to_far = pack(
        (bins_local, half_bins, rows_local), spectrum, neighbours, sea_mask
    )
    pair = swap(to_pair, 1)
    near = swap(to_near, 2)
    far = swap(to_far, 3)
    kept, passed, free_field = stencil((bins_local, half_bins, rows_local, False), substeps, courant, trig, mine, pair)
    source_operator, kept = lax.optimization_barrier((source_operator, kept))
    other_w = swap(source_operator, 1)
    near, far, kept = lax.optimization_barrier((near, far, kept))
    passed, dep_field, *sent = stencil(
        (bins_local, half_bins, rows_local, True), substeps, courant, trig, mine, pair, near, far, kept, passed
    )
    ring = [[(i, (i + k) % comps) for i in range(comps)] for k in range(comps)]
    passed = swap(passed, 1)
    large = [sent[0]] + [lax.ppermute(sent[k], "comp", ring[k]) for k in range(1, comps)]
    small = [lax.ppermute(passed[k], "comp", ring[k]) for k in range(1, comps)]
    whole_w = gather_operator(source_operator, other_w)
    raised = integrate((bins_local, half_bins, comps), whole_w, large, passed, small)
    home = [raised[0]] + [lax.ppermute(raised[k], "comp", ring[k]) for k in range(1, comps)]
    got_free = swap(free_field[1:], 1)
    got_dep = swap(dep_field[1:], 1)
    return finish((bins_local, half_bins), (free_field, dep_field, got_free, got_dep), sea_mask, home)


def device_step(*arrays):
    bins_local, points_local = arrays[0].shape
    two_chips = (
        lax.axis_size("lat") == 2
        and lax.axis_size("sub") == 2
        and bins_local % SECTOR == 0
        and points_local % NLON == 0
        and points_local == lax.axis_size("comp") * LANES
        and lax.axis_size("comp") * bins_local % LANES == 0
    )
    return (two_chip_device if two_chips else per_device)(*arrays)


def solution(mesh):
    placed = (
        P("comp", ("members", "lat", "sub")),
        P(("members", "lat", "sub")),
        P(None, ("members", "lat", "sub")),
        P(),
        P(),
        P("sub", None),
    )
    return jax.shard_map(
        device_step,
        mesh=mesh,
        in_specs=placed,
        out_specs=P("comp", ("members", "lat", "sub")),
        check_vma=False,
    )
```
